512 devices in a mesh: depth: 128 (over z, y, core), rows: 4 (over x).
Axes of the slice: x: 4, y: 8, z: 8, core: 2. Of those that a mesh axis runs over, the one named last changes fastest.
Arguments:
- density: float32 [256, 512, 512], P('depth', 'rows'), may hold values from 0 to 6
- transfer_table: float32 [4, 16], replicated, may hold values from 0.2 to 1
Outputs:
- picture: float32 [4, 512, 512], P(None, ('rows', 'depth'))
The draws below stay inside these ranges and needn't reach their ends.
All inputs are finite; a program needn't handle non-finite values.
Results may differ from the reference program's by a relative error of at most 0.000021.
Values sent between devices are 32-bit elements; how exact they have to be, the bound alone decides.
No kernel may reach another device: no remote copies, remote signals or barrier semaphores. Data moves between devices by JAX's collectives and lax.ppermute only.
A program may use at most 64 MiB of HBM per device.

```python
import jax
import jax.numpy as jnp
from jax import lax

NX = 512
PASSES = 3
KNOTS = 16
NZ = 256
NY = 512


def draw_density(key, part):
    normals = jax.random.normal(key, (NZ, NY, NX), jnp.float32)
    values = jnp.exp(0.5 * normals)
    return jnp.clip(values, 0.05, 5.9)


def setup_inputs(seed: int = 0) -> dict:
    splits = jax.random.split(jax.random.key(seed), 3)
    density = draw_density(jax.random.fold_in(splits[2], 71), 0)
    transfer_table = jnp.clip(jax.random.uniform(splits[1], (4, KNOTS), jnp.float32, 0.2, 1.0), 0.2, 1.0)
    return {"density": density, "transfer_table": transfer_table}


TIME_STEP = 0.15
OPTICAL_DEPTH = 3.0
UPPER_DENSITY = 6.0
AMBIENT = 0.35

def diffusion_flux(center, neighbours):
    summed = jnp.zeros_like(center)
    for other in neighbours:
        change = other - center
        summed = summed + change / (1.0 + change * change)
    return center + TIME_STEP * summed

def appearance(center, neighbours, transfer_table, depth_count):
    deeper, nearer, next_row, prev_row, next_col, prev_col = neighbours
    grad_depth = (deeper - nearer) * 0.5
    grad_row = (next_row - prev_row) * 0.5
    grad_col = (next_col - prev_col) * 0.5
    shading = AMBIENT + (1.0 - AMBIENT) * jnp.abs(0.64 * grad_depth + 0.6 * grad_row + 0.48 * grad_col) / jnp.sqrt(grad_depth * grad_depth + grad_row * grad_row + grad_col * grad_col + 0.25)
    position = center * ((KNOTS - 1) / UPPER_DENSITY)
    mixed = [jnp.zeros_like(center) for channel in range(4)]
    for knot in range(KNOTS):
        hat_weight = jnp.maximum(0.0, 1.0 - jnp.abs(position - knot))
        mixed = [mixed[channel] + transfer_table[channel, knot] * hat_weight for channel in range(4)]
    opacity = 1.0 - jnp.exp(-mixed[3] * (OPTICAL_DEPTH / depth_count))
    colors = jnp.stack([mixed[0] * shading, mixed[1] * shading, mixed[2] * shading])
    return (colors, opacity)

def plane_sides(window):
    center = window[1]
    rows_pad = jnp.pad(center, ((1, 1), (0, 0)), mode='edge')
    cols_pad = jnp.pad(center, ((0, 0), (1, 1)), mode='edge')
    return (window[2], window[0], rows_pad[2:], rows_pad[:-2], cols_pad[:, 2:], cols_pad[:, :-2])

def reference(density, transfer_table):
    field = density
    planes = jnp.arange(NZ, dtype=jnp.int32)
    for sweep in range(PASSES):
        padded = jnp.pad(field, ((1, 1), (0, 0), (0, 0)), mode='edge')

        def one_plane(index):
            window = lax.dynamic_slice_in_dim(padded, index, 3, 0)
            return diffusion_flux(window[1], plane_sides(window))
        field = lax.map(one_plane, planes)
    padded = jnp.pad(field, ((1, 1), (0, 0), (0, 0)), mode='edge')

    def advance(carry, index):
        color_sum, remaining = carry
        window = lax.dynamic_slice_in_dim(padded, index, 3, 0)
        colors, opacity = appearance(window[1], plane_sides(window), transfer_table, NZ)
        color_sum = color_sum + remaining * opacity * colors
        remaining = remaining * (1.0 - opacity)
        return ((color_sum, remaining), None)
    start = (jnp.zeros((3, NY, NX), jnp.float32), jnp.ones((NY, NX), jnp.float32))
    (color_sum, remaining), unused = lax.scan(advance, start, planes)
    return jnp.concatenate([color_sum, (1.0 - remaining)[None]], axis=0)
```

```python
import jax
import jax.numpy as jnp
from jax import lax
from jax.experimental import pallas as pl
from jax.experimental.pallas import tpu as pltpu
from jax.sharding import PartitionSpec as P


PASSES = 3
KNOTS = 16
TIME_STEP = 0.15
OPTICAL_DEPTH = 3.0
UPPER_DENSITY = 6.0
AMBIENT = 0.35

GROUP = 16
BLOCKS = 8
HALO = 4
BAND = 128
COLS = 512
TILE = COLS // GROUP
WIDE = TILE + 2 * HALO
SEGS = 3
SEG_ROWS = 48
PLANES = 2
DEEP = GROUP * PLANES
LANES = 128
VMEM = pltpu.VMEM


def lane_index(shape):
    return lax.broadcasted_iota(jnp.int32, shape, 1)


def pack_kernel(own, above, below, out, ext):
    band = lax.axis_index("rows")
    bands = lax.axis_size("rows")
    for p in range(PLANES):
        ext[p, HALO : HALO + BAND, :] = own[p]
        ext[p, HALO + BAND :, :] = jnp.zeros((SEGS * SEG_ROWS - HALO - BAND, COLS), jnp.float32)

    @pl.when(band > 0)
    def _():
        for p in range(PLANES):
            ext[p, 0:HALO, :] = above[p, 8 - HALO : 8, :]

    @pl.when(band == 0)
    def _():
        for p in range(PLANES):
            for i in range(HALO):
                ext[p, HALO - 1 - i : HALO - i, :] = own[p, i : i + 1, :]

    @pl.when(band < bands - 1)
    def _():
        for p in range(PLANES):
            ext[p, HALO + BAND : 2 * HALO + BAND, :] = below[p, 0:HALO, :]

    @pl.when(band == bands - 1)
    def _():
        for p in range(PLANES):
            for i in range(HALO):
                row = HALO + BAND + i
                ext[p, row : row + 1, :] = own[p, BAND - 1 - i : BAND - i, :]

    lane = lane_index((8, LANES))

    def step(it, carry):
        p = it // 6
        j = it - 6 * p
        tiles = []
        for k in range(SEGS):
            start = pl.multiple_of(SEG_ROWS * k + 8 * j, 8)
            tiles.append([ext[p, pl.ds(start, 8), LANES * q : LANES * (q + 1)] for q in range(4)])
        for t in range(GROUP):
            q, m = divmod(t, 4)
            parts = []
            for k in range(SEGS):
                x = tiles[k][q]
                if m == 0 and q > 0:
                    x = jnp.where(lane >= LANES - HALO, tiles[k][q - 1], x)
                if m == 3 and q < 3:
                    x = jnp.where(lane < HALO, tiles[k][q + 1], x)
                parts.append(pltpu.roll(x, (WIDE * k - TILE * m + HALO) % LANES, 1))
            value = jnp.where(lane < WIDE, parts[0], jnp.where(lane < 2 * WIDE, parts[1], parts[2]))
            out[t, p, pl.ds(pl.multiple_of(8 * j, 8), 8), :] = value
        return carry

    lax.fori_loop(0, PLANES * 6, step, 0)


def next_row(f, lane):
    moved = pltpu.roll(f, SEG_ROWS - 1, 0)
    last = moved[SEG_ROWS - 8 :]
    row = lax.broadcasted_iota(jnp.int32, (8, LANES), 0)
    last = jnp.where(row == 7, pltpu.roll(last, LANES - WIDE, 1), last)
    return jnp.concatenate([moved[: SEG_ROWS - 8], last], axis=0)


def prev_row(f, lane):
    moved = pltpu.roll(f, 1, 0)
    first = moved[:8]
    row = lax.broadcasted_iota(jnp.int32, (8, LANES), 0)
    first = jnp.where(row == 0, pltpu.roll(first, WIDE, 1), first)
    return jnp.concatenate([first, moved[8:]], axis=0)


def flux(change):
    return change / (1.0 + change * change)


def render_kernel(mine, before, after, table, out, fa, fb):
    block = lax.axis_index("depth") // GROUP
    tile = lax.axis_index("depth") % GROUP
    lane = lane_index((SEG_ROWS, LANES))
    column = lane % WIDE
    first_tile = tile == 0
    last_tile = tile == GROUP - 1
    at_first = jnp.logical_and(column == HALO, first_tile)
    at_last = jnp.logical_and(column == HALO + TILE - 1, last_tile)
    open_face = jnp.where(
        jnp.logical_or(at_last, jnp.logical_and(column == HALO - 1, first_tile)), 0.0, 1.0
    )

    for i in range(GROUP):
        for p in range(PLANES):
            fa[HALO + PLANES * i + p] = mine[i, p]

    @pl.when(block > 0)
    def _():
        for i in range(HALO):
            fa[i] = before[i // 2, i % 2]

    @pl.when(block == 0)
    def _():
        for i in range(HALO):
            fa[HALO - 1 - i] = mine[i // 2, i % 2]

    @pl.when(block < BLOCKS - 1)
    def _():
        for i in range(HALO):
            fa[HALO + DEEP + i] = after[i // 2, i % 2]

    @pl.when(block == BLOCKS - 1)
    def _():
        for i in range(HALO):
            d = DEEP - 1 - i
            fa[HALO + DEEP + i] = mine[d // 2, d % 2]

    src, dst = fa, fb
    for sweep in range(PASSES):
        lo, hi = sweep + 1, DEEP + 2 * HALO - 1 - sweep

        def step(p, flux_nearer, src=src, dst=dst):
            f = src[p]
            flux_deeper = flux(src[p + 1] - f)
            row = flux(next_row(f, lane) - f)
            col = flux((pltpu.roll(f, LANES - 1, 1) - f) * open_face)
            total = flux_deeper - flux_nearer
            total = total + (row - prev_row(row, lane))
            total = total + (col - pltpu.roll(col, 1, 1))
            dst[p] = f + TIME_STEP * total
            return flux_deeper

        lax.fori_loop(lo, hi, step, flux(src[lo] - src[lo - 1]))
        src, dst = dst, src

    base = [jnp.broadcast_to(table[c : c + 1, :], (8, LANES)) for c in range(4)]
    slope = [pltpu.roll(base[c], LANES - 1, 1) - base[c] for c in range(4)]

    def lookup(k, part):
        return jnp.concatenate(
            [
                jnp.take_along_axis(part, k[8 * j : 8 * j + 8], axis=1)
                for j in range(SEG_ROWS // 8)
            ],
            axis=0,
        )

    def shade(p, carry):
        red, green, blue, remaining = carry
        f = src[p]
        grad_depth = (src[p + 1] - src[p - 1]) * 0.5
        grad_row = (next_row(f, lane) - prev_row(f, lane)) * 0.5
        right = jnp.where(at_last, f, pltpu.roll(f, LANES - 1, 1))
        left = jnp.where(at_first, f, pltpu.roll(f, 1, 1))
        grad_col = (right - left) * 0.5
        square = grad_depth * grad_depth + grad_row * grad_row + grad_col * grad_col + 0.25
        along = jnp.abs(0.64 * grad_depth + 0.6 * grad_row + 0.48 * grad_col)
        shading = AMBIENT + (1.0 - AMBIENT) * along * lax.rsqrt(square)
        position = f * ((KNOTS - 1) / UPPER_DENSITY) + 1.0
        position = jnp.clip(position, 0.0, KNOTS + 1.0)
        whole = jnp.minimum(jnp.floor(position), float(KNOTS))
        frac = position - whole
        k = whole.astype(jnp.int32)
        mixed = [lookup(k, base[c]) + frac * lookup(k, slope[c]) for c in range(4)]
        kept = jnp.exp(mixed[3] * (-OPTICAL_DEPTH / (DEEP * BLOCKS)))
        weight = remaining * (1.0 - kept) * shading
        return (
            red + weight * mixed[0],
            green + weight * mixed[1],
            blue + weight * mixed[2],
            remaining * kept,
        )

    zero = jnp.zeros((SEG_ROWS, LANES), jnp.float32)
    sums = lax.fori_loop(
        HALO, HALO + DEEP, shade, (zero, zero, zero, jnp.ones_like(zero))
    )
    lanes = lane_index((SEG_ROWS, LANES))
    for k in range(SEGS):
        value = None
        for c in range(4):
            moved = pltpu.roll(sums[c], (TILE * c - WIDE * k - HALO) % LANES, 1)
            value = moved if value is None else jnp.where(lanes >= TILE * c, moved, value)
        first = SEG_ROWS * k - HALO
        lo, hi = max(first, 0), min(first + SEG_ROWS, BAND)
        out[lo:hi, :] = value[lo - first : hi - first]


def gather_kernel(parts, out):
    lane = lane_index((GROUP, LANES))
    total = jnp.zeros((GROUP, LANES), jnp.float32)
    remaining = jnp.ones((GROUP, LANES), jnp.float32)
    for b in range(BLOCKS):
        v = parts[GROUP * b : GROUP * (b + 1)]
        kept = v
        for c in range(3):
            kept = jnp.where(
                jnp.logical_and(lane >= TILE * c, lane < TILE * (c + 1)),
                pltpu.roll(v, TILE * (c + 1), 1),
                kept,
            )
        total = total + remaining * v
        remaining = remaining * kept
    total = jnp.where(lane >= 3 * TILE, 1.0 - remaining, total)
    turned = [total] + [pltpu.roll(total, TILE * s, 1) for s in range(1, 4)]
    for c in range(4):
        for t in range(GROUP):
            m = t % 4
            out[c, :, TILE * t : TILE * (t + 1)] = turned[(m - c) % 4][
                t : t + 1, TILE * m : TILE * (m + 1)
            ]


def call(kernel, shape, scratch, *operands):
    spec = pl.BlockSpec(memory_space=VMEM)
    return pl.pallas_call(
        kernel,
        out_shape=jax.ShapeDtypeStruct(shape, jnp.float32),
        in_specs=[spec] * len(operands),
        out_specs=spec,
        scratch_shapes=scratch,
        name=kernel.__name__,
    )(*operands)


def shifted(value, axis, by):
    size = lax.axis_size(axis)
    pairs = [(i, i + by) for i in range(size) if 0 <= i + by < size]
    return lax.ppermute(value, axis, pairs)


def per_device(density, transfer_table):
    above = shifted(density[:, BAND - 8 :], "rows", 1)
    below = shifted(density[:, :8], "rows", -1)
    rows = SEGS * SEG_ROWS
    sent = call(
        pack_kernel,
        (GROUP, PLANES, SEG_ROWS, LANES),
        [VMEM((PLANES, rows, COLS), jnp.float32)],
        density,
        above,
        below,
    )
    groups = [[GROUP * b + i for i in range(GROUP)] for b in range(BLOCKS)]
    mine = lax.all_to_all(sent, "depth", 0, 0, axis_index_groups=groups, tiled=True)
    near = HALO // PLANES
    before = shifted(mine[GROUP - near :], "depth", GROUP)
    after = shifted(mine[:near], "depth", -GROUP)
    table = jnp.pad(transfer_table, ((0, 4), (1, LANES - KNOTS - 1)))
    field = VMEM((DEEP + 2 * HALO, SEG_ROWS, LANES), jnp.float32)
    partial = call(
        render_kernel, (BAND, LANES), [field, field], mine, before, after, table
    )
    parts = lax.all_to_all(partial, "depth", 0, 0, tiled=True)
    return call(gather_kernel, (4, 1, COLS), [], parts)


def solution(mesh):
    placed = (P("depth", "rows", None), P())
    return jax.shard_map(
        per_device,
        mesh=mesh,
        in_specs=placed,
        out_specs=P(None, ("rows", "depth"), None),
        check_vma=False,
    )
```

```python
import jax
import jax.numpy as jnp
from jax import lax
from jax.experimental import pallas as pl
from jax.experimental.pallas import tpu as pltpu
from jax.sharding import PartitionSpec as P


PASSES = 3
KNOTS = 16
TIME_STEP = 0.15
OPTICAL_DEPTH = 3.0
UPPER_DENSITY = 6.0
AMBIENT = 0.35

GROUP = 16
BLOCKS = 8
HALO = 4
BAND = 128
COLS = 512
TILE = COLS // GROUP
WIDE = TILE + 2 * HALO
SEGS = 3
SEG_ROWS = 48
TILES = SEG_ROWS // 8
PLANES = 2
DEEP = GROUP * PLANES
LANES = 128
TOP = 8
TALL = SEG_ROWS + 2 * TOP
EDGE = 4
VMEM = pltpu.VMEM


def lane_index(rows=8):
    return lax.broadcasted_iota(jnp.int32, (rows, LANES), 1)


def pack_kernel(own, above, below, out, ext):
    band = lax.axis_index("rows")
    bands = lax.axis_size("rows")
    rows = SEGS * SEG_ROWS
    for p in range(PLANES):
        ext[p, HALO : HALO + BAND, :] = own[p]
        ext[p, rows - 8 :, :] = jnp.zeros((8, COLS), jnp.float32)

    @pl.when(band > 0)
    def _():
        for p in range(PLANES):
            ext[p, 0:HALO, :] = above[p, 8 - HALO : 8, :]

    @pl.when(band == 0)
    def _():
        for p in range(PLANES):
            for i in range(HALO):
                ext[p, HALO - 1 - i : HALO - i, :] = own[p, i : i + 1, :]

    @pl.when(band < bands - 1)
    def _():
        for p in range(PLANES):
            ext[p, HALO + BAND : 2 * HALO + BAND, :] = below[p, 0:HALO, :]

    @pl.when(band == bands - 1)
    def _():
        for p in range(PLANES):
            for i in range(HALO):
                row = HALO + BAND + i
                ext[p, row : row + 1, :] = own[p, BAND - 1 - i : BAND - i, :]

    lane = lane_index()
    segment, left, right = [], [], []
    for m in range(4):
        local = (lane - (TILE * m - HALO)) % LANES
        segment.append((local < WIDE, local < 2 * WIDE))
        column = local % WIDE
        left.append(column < HALO)
        right.append(column >= WIDE - HALO)

    def step(it, carry):
        p = it // TILES
        j = it - TILES * p
        rolled = []
        for k in range(SEGS):
            start = pl.multiple_of(SEG_ROWS * k + 8 * j, 8)
            row = [ext[p, pl.ds(start, 8), LANES * q : LANES * (q + 1)] for q in range(4)]
            rolled.append([pltpu.roll(x, WIDE * k, 1) if k else x for x in row])

        def joined(q, m):
            first, second = segment[m]
            return jnp.where(
                first, rolled[0][q], jnp.where(second, rolled[1][q], rolled[2][q])
            )

        for t in range(GROUP):
            q, m = divmod(t, 4)
            value = joined(q, m)
            if m == 0 and q > 0:
                value = jnp.where(left[m], joined(q - 1, m), value)
            if m == 3 and q < 3:
                value = jnp.where(right[m], joined(q + 1, m), value)
            out[t, p, pl.ds(pl.multiple_of(8 * j, 8), 8), :] = value
        return carry

    lax.fori_loop(0, PLANES * TILES, step, 0)


def flux(change):
    return change / (1.0 + change * change)


def rows_at(j, by=0):
    return slice(TOP + 8 * j + by, TOP + 8 * j + by + 8)


def put(ref, p, tiles):
    for j in range(TILES):
        ref[p, rows_at(j), :] = tiles[j]
    ref[p, TOP - 1 : TOP, :] = pltpu.roll(tiles[-1], WIDE, 1)[7:8]
    ref[p, TOP + SEG_ROWS : TOP + SEG_ROWS + 1, :] = pltpu.roll(tiles[0], LANES - WIDE, 1)[0:1]


def take(ref, p, by=0):
    return [ref[p, rows_at(j, by), :] for j in range(TILES)]


class Tile:
    def __init__(self):
        self.block = lax.axis_index("depth") // GROUP
        tile = lax.axis_index("depth") % GROUP
        self.start = TILE * (tile % 4) - HALO
        local = (lane_index() - self.start + LANES) % LANES
        column = local % WIDE
        first, last = tile == 0, tile == GROUP - 1
        self.at_first = jnp.logical_and(column == HALO, first)
        self.at_last = jnp.logical_and(column == HALO + TILE - 1, last)
        self.open_face = jnp.where(
            jnp.logical_or(self.at_last, jnp.logical_and(column == HALO - 1, first)), 0.0, 1.0
        )


def diffuse(src, p, dst, to, fluxes, slot, flux_nearer, tile):
    f = take(src, p)
    below = take(src, p, 1)
    deeper = take(src, p + 1)
    flux_deeper = [flux(deeper[j] - f[j]) for j in range(TILES)]
    row = [flux(below[j] - f[j]) for j in range(TILES)]
    for j in range(TILES):
        fluxes[slot, rows_at(j), :] = row[j]
    fluxes[slot, TOP - 1 : TOP, :] = pltpu.roll(row[-1], WIDE, 1)[7:8]
    row_prev = take(fluxes, slot, -1)
    new = []
    for j in range(TILES):
        col = flux((pltpu.roll(f[j], LANES - 1, 1) - f[j]) * tile.open_face)
        total = flux_deeper[j] - flux_nearer[j]
        total = total + (row[j] - row_prev[j])
        total = total + (col - pltpu.roll(col, 1, 1))
        new.append(f[j] + TIME_STEP * total)
    put(dst, to, new)
    return flux_deeper


def first_flux(src, p):
    here, deeper = take(src, p), take(src, p + 1)
    return [flux(deeper[j] - here[j]) for j in range(TILES)]


def tables(transfer, table):
    table[...] = jnp.zeros((8, LANES), jnp.float32)
    table[0:4, 1 : 1 + KNOTS] = transfer[...]
    base = [jnp.broadcast_to(table[c : c + 1, :], (8, LANES)) for c in range(4)]
    return base, [pltpu.roll(base[c], LANES - 1, 1) - base[c] for c in range(4)]


def shade(src, p, j, carry, lookup, tile):
    red, green, blue, remaining = carry
    base, slope = lookup
    f = src[p, rows_at(j), :]
    depth = src[p + 1, rows_at(j), :] - src[p - 1, rows_at(j), :]
    row = src[p, rows_at(j, 1), :] - src[p, rows_at(j, -1), :]
    right = jnp.where(tile.at_last, f, pltpu.roll(f, LANES - 1, 1))
    left = jnp.where(tile.at_first, f, pltpu.roll(f, 1, 1))
    col = right - left
    square = depth * depth + row * row + col * col + 1.0
    gain = 1.0 - AMBIENT
    along = jnp.abs(0.64 * gain * depth + 0.6 * gain * row + 0.48 * gain * col)
    shading = AMBIENT + along * lax.rsqrt(square)
    position = f * ((KNOTS - 1) / UPPER_DENSITY) + 1.0
    k = position.astype(jnp.int32)
    frac = position - k.astype(jnp.float32)
    mixed = [
        jnp.take_along_axis(base[c], k, axis=1)
        + frac * jnp.take_along_axis(slope[c], k, axis=1)
        for c in range(4)
    ]
    kept = jnp.exp(mixed[3] * (-OPTICAL_DEPTH / (DEEP * BLOCKS)))
    weight = remaining * (1.0 - kept) * shading
    return (
        red + weight * mixed[0],
        green + weight * mixed[1],
        blue + weight * mixed[2],
        remaining * kept,
    )


def inner_kernel(mine, transfer, out, fa, fb, fluxes, table):
    tile = Tile()
    zero = jnp.zeros((8, LANES), jnp.float32)

    def fill(i, carry):
        for p in range(PLANES):
            tiles = [mine[i, p, 8 * j : 8 * j + 8, :] for j in range(TILES)]
            put(fa, PLANES * i + p, tiles)
        return carry

    lax.fori_loop(0, GROUP, fill, 0)
    src, dst = fa, fb
    for sweep in range(PASSES):
        lo, hi = sweep + 1, DEEP - 1 - sweep

        def step(i, carry, src=src, dst=dst, lo=lo):
            for u in range(2):
                p = lo + 2 * i + u
                carry = diffuse(src, p, dst, p, fluxes, u, carry, tile)
            return carry

        lax.fori_loop(0, (hi - lo) // 2, step, first_flux(src, lo - 1))
        kept = (lo, lo + 1, hi - 2, hi - 1)
        for i in range(EDGE):
            for j in range(TILES):
                out[EDGE * sweep + i, 8 * j : 8 * j + 8, :] = dst[kept[i], rows_at(j), :]
        src, dst = dst, src

    lookup = tables(transfer, table)
    for j in range(TILES):

        def planes(i, carry, j=j):
            for u in range(4):
                carry = shade(src, HALO + 4 * i + u, j, carry, lookup, tile)
            return carry

        sums = lax.fori_loop(0, (DEEP - 2 * HALO) // 4, planes, (zero, zero, zero, zero + 1.0))
        for c in range(4):
            out[EDGE * PASSES + c, 8 * j : 8 * j + 8, :] = sums[c]


def outer_kernel(head, tail, before, after, inner, transfer, out, fa, fb, fluxes, table):
    tile = Tile()
    zero = jnp.zeros((8, LANES), jnp.float32)
    lookup = tables(transfer, table)

    def plane_of(ref, i):
        return [ref[i // 2, i % 2, 8 * j : 8 * j + 8, :] for j in range(TILES)]

    def inner_of(i):
        return [inner[i, 8 * j : 8 * j + 8, :] for j in range(TILES)]

    def side(front):
        inside = tile.block > 0 if front else tile.block < BLOCKS - 1
        own = 4 if front else 0
        halo = 0 if front else 2
        for i in range(2):
            put(fa, own + i, plane_of(head if front else tail, i if front else 2 + i))

        @pl.when(inside)
        def _():
            for i in range(HALO):
                put(fa, halo + i, plane_of(before if front else after, i))

        @pl.when(jnp.logical_not(inside))
        def _():
            for i in range(HALO):
                put(fa, halo + i, plane_of(head if front else tail, HALO - 1 - i))

        src, dst = fa, fb
        for sweep in range(PASSES):
            carry = first_flux(src, 0)
            for i in range(4):
                to = i if front else 2 + i
                carry = diffuse(src, i + 1, dst, to, fluxes, i, carry, tile)
            for i in range(2):
                put(dst, own + i, inner_of(EDGE * sweep + (i if front else 2 + i)))
            src, dst = dst, src
        return src

    src = side(True)
    sums = []
    for j in range(TILES):
        carry = (zero, zero, zero, zero + 1.0)
        for i in range(4):
            carry = shade(src, i + 1, j, carry, lookup, tile)
        mid = [inner[EDGE * PASSES + c, 8 * j : 8 * j + 8, :] for c in range(4)]
        remaining = carry[3]
        sums.append([carry[c] + remaining * mid[c] for c in range(3)] + [remaining * mid[3]])
    src = side(False)
    lane = lane_index()
    for j in range(TILES):
        carry = sums[j]
        for i in range(4):
            carry = shade(src, i + 1, j, carry, lookup, tile)
        for k in range(SEGS):
            value = None
            for c in range(4):
                by = TILE * c - WIDE * k - HALO - tile.start + LANES * 2
                moved = pltpu.roll(carry[c], lax.rem(by, LANES), 1)
                value = moved if value is None else jnp.where(lane >= TILE * c, moved, value)
            first = SEG_ROWS * k + 8 * j - HALO
            lo, hi = max(first, 0), min(first + 8, BAND)
            if lo < hi:
                out[lo:hi, :] = value[lo - first : hi - first]


def gather_kernel(parts, out):
    lane = lane_index(GROUP)
    total = jnp.zeros((GROUP, LANES), jnp.float32)
    remaining = jnp.ones((GROUP, LANES), jnp.float32)
    for b in range(BLOCKS):
        v = parts[GROUP * b : GROUP * (b + 1)]
        kept = v
        for c in range(3):
            kept = jnp.where(
                jnp.logical_and(lane >= TILE * c, lane < TILE * (c + 1)),
                pltpu.roll(v, TILE * (c + 1), 1),
                kept,
            )
        total = total + remaining * v
        remaining = remaining * kept
    total = jnp.where(lane >= 3 * TILE, 1.0 - remaining, total)
    turned = [total] + [pltpu.roll(total, TILE * s, 1) for s in range(1, 4)]
    for c in range(4):
        for t in range(GROUP):
            m = t % 4
            out[c, :, TILE * t : TILE * (t + 1)] = turned[(m - c) % 4][
                t : t + 1, TILE * m : TILE * (m + 1)
            ]


def call(kernel, shape, scratch, *operands):
    spec = pl.BlockSpec(memory_space=VMEM)
    return pl.pallas_call(
        kernel,
        out_shape=jax.ShapeDtypeStruct(shape, jnp.float32),
        in_specs=[spec] * len(operands),
        out_specs=spec,
        scratch_shapes=[VMEM(s, jnp.float32) for s in scratch],
        name=kernel.__name__,
    )(*operands)


def shifted(value, axis, by):
    size = lax.axis_size(axis)
    pairs = [(i, i + by) for i in range(size) if 0 <= i + by < size]
    return lax.ppermute(value, axis, pairs)


def per_device(density, transfer_table):
    above = shifted(density[:, BAND - 8 :], "rows", 1)
    below = shifted(density[:, :8], "rows", -1)
    sent = call(
        pack_kernel,
        (GROUP, PLANES, SEG_ROWS, LANES),
        [(PLANES, SEGS * SEG_ROWS, COLS)],
        density,
        above,
        below,
    )
    groups = [[GROUP * b + i for i in range(GROUP)] for b in range(BLOCKS)]
    mine = lax.all_to_all(sent, "depth", 0, 0, axis_index_groups=groups, tiled=True)
    near = HALO // PLANES
    head, tail = mine[:near], mine[GROUP - near :]
    before = shifted(tail, "depth", GROUP)
    after = shifted(head, "depth", -GROUP)
    field = (DEEP, TALL, LANES)
    inner = call(
        inner_kernel,
        (EDGE * PASSES + 4, SEG_ROWS, LANES),
        [field, field, (2, TALL, LANES), (8, LANES)],
        mine,
        transfer_table,
    )
    few = (6, TALL, LANES)
    partial = call(
        outer_kernel,
        (BAND, LANES),
        [few, few, (4, TALL, LANES), (8, LANES)],
        head,
        tail,
        before,
        after,
        inner,
        transfer_table,
    )
    parts = lax.all_to_all(partial, "depth", 0, 0, tiled=True)
    return call(gather_kernel, (4, 1, COLS), [], parts)


def solution(mesh):
    placed = (P("depth", "rows", None), P())
    return jax.shard_map(
        per_device,
        mesh=mesh,
        in_specs=placed,
        out_specs=P(None, ("rows", "depth"), None),
        check_vma=False,
    )
```

```python
import jax
import jax.numpy as jnp
from jax import lax
from jax.experimental import pallas as pl
from jax.experimental.pallas import tpu as pltpu
from jax.sharding import PartitionSpec as P


PASSES = 3
KNOTS = 16
TIME_STEP = 0.15
OPTICAL_DEPTH = 3.0
UPPER_DENSITY = 6.0
AMBIENT = 0.35

GROUP = 16
BLOCKS = 8
HALO = 4
BAND = 128
COLS = 512
TILE = COLS // GROUP
WIDE = TILE + 2 * HALO
SEGS = 3
SEG_ROWS = 48
TILES = SEG_ROWS // 8
PLANES = 2
DEEP = GROUP * PLANES
LANES = 128
TOP = 8
TALL = SEG_ROWS + 2 * TOP
EDGE = 4
UNROLL = 7
SHADED = 8
VMEM = pltpu.VMEM


def lane_index(rows=8):
    return lax.broadcasted_iota(jnp.int32, (rows, LANES), 1)


def pack_kernel(own, above, below, out, ext):
    band = lax.axis_index("rows")
    bands = lax.axis_size("rows")
    rows = SEGS * SEG_ROWS
    for p in range(PLANES):
        ext[p, HALO : HALO + BAND, :] = own[p]
        ext[p, rows - 8 :, :] = jnp.zeros((8, COLS), jnp.float32)

    @pl.when(band > 0)
    def _():
        for p in range(PLANES):
            ext[p, 0:HALO, :] = above[p, 8 - HALO : 8, :]

    @pl.when(band == 0)
    def _():
        for p in range(PLANES):
            for i in range(HALO):
                ext[p, HALO - 1 - i : HALO - i, :] = own[p, i : i + 1, :]

    @pl.when(band < bands - 1)
    def _():
        for p in range(PLANES):
            ext[p, HALO + BAND : 2 * HALO + BAND, :] = below[p, 0:HALO, :]

    @pl.when(band == bands - 1)
    def _():
        for p in range(PLANES):
            for i in range(HALO):
                row = HALO + BAND + i
                ext[p, row : row + 1, :] = own[p, BAND - 1 - i : BAND - i, :]

    lane = lane_index()
    segment, left, right = [], [], []
    for m in range(4):
        local = (lane - (TILE * m - HALO)) % LANES
        segment.append((local < WIDE, local < 2 * WIDE))
        column = local % WIDE
        left.append(column < HALO)
        right.append(column >= WIDE - HALO)

    def step(it, carry):
        p = it // TILES
        j = it - TILES * p
        rolled = []
        for k in range(SEGS):
            start = pl.multiple_of(SEG_ROWS * k + 8 * j, 8)
            row = [ext[p, pl.ds(start, 8), LANES * q : LANES * (q + 1)] for q in range(4)]
            rolled.append([pltpu.roll(x, WIDE * k, 1) if k else x for x in row])

        def joined(q, m):
            first, second = segment[m]
            return jnp.where(
                first, rolled[0][q], jnp.where(second, rolled[1][q], rolled[2][q])
            )

        for t in range(GROUP):
            q, m = divmod(t, 4)
            value = joined(q, m)
            if m == 0 and q > 0:
                value = jnp.where(left[m], joined(q - 1, m), value)
            if m == 3 and q < 3:
                value = jnp.where(right[m], joined(q + 1, m), value)
            out[t, p, pl.ds(pl.multiple_of(8 * j, 8), 8), :] = value
        return carry

    lax.fori_loop(0, PLANES * TILES, step, 0)


def flux(change):
    return change / (1.0 + change * change)


def rows_at(j, by=0):
    if isinstance(j, int):
        return slice(TOP + 8 * j + by, TOP + 8 * j + by + 8)
    return pl.ds(pl.multiple_of(8 * j, 8) + TOP + by, 8)


def put(ref, p, tiles):
    for j in range(TILES):
        ref[p, rows_at(j), :] = tiles[j]
    ref[p, TOP - 1 : TOP, :] = pltpu.roll(tiles[-1], WIDE, 1)[7:8]
    ref[p, TOP + SEG_ROWS : TOP + SEG_ROWS + 1, :] = pltpu.roll(tiles[0], LANES - WIDE, 1)[0:1]


def take(ref, p, by=0):
    return [ref[p, rows_at(j, by), :] for j in range(TILES)]


class Tile:
    def __init__(self):
        self.block = lax.axis_index("depth") // GROUP
        tile = lax.axis_index("depth") % GROUP
        self.start = TILE * (tile % 4) - HALO
        local = (lane_index() - self.start + LANES) % LANES
        column = local % WIDE
        first, last = tile == 0, tile == GROUP - 1
        self.at_first = jnp.logical_and(column == HALO, first)
        self.at_last = jnp.logical_and(column == HALO + TILE - 1, last)
        self.open_face = jnp.where(
            jnp.logical_or(self.at_last, jnp.logical_and(column == HALO - 1, first)), 0.0, 1.0
        )


def diffuse(src, p, dst, to, fluxes, slot, flux_nearer, tile):
    f = take(src, p)
    below = take(src, p, 1)
    deeper = take(src, p + 1)
    flux_deeper = [flux(deeper[j] - f[j]) for j in range(TILES)]
    row = [flux(below[j] - f[j]) for j in range(TILES)]
    for j in range(TILES):
        fluxes[slot, rows_at(j), :] = row[j]
    fluxes[slot, TOP - 1 : TOP, :] = pltpu.roll(row[-1], WIDE, 1)[7:8]
    row_prev = take(fluxes, slot, -1)
    new = []
    for j in range(TILES):
        col = flux((pltpu.roll(f[j], LANES - 1, 1) - f[j]) * tile.open_face)
        total = flux_deeper[j] - flux_nearer[j]
        total = total + (row[j] - row_prev[j])
        total = total + (col - pltpu.roll(col, 1, 1))
        new.append(f[j] + TIME_STEP * total)
    put(dst, to, new)
    return flux_deeper


def first_flux(src, p):
    here, deeper = take(src, p), take(src, p + 1)
    return [flux(deeper[j] - here[j]) for j in range(TILES)]


ALONG_ROWS = lax.GatherDimensionNumbers(
    offset_dims=(),
    collapsed_slice_dims=(0,),
    start_index_map=(0,),
    operand_batching_dims=(1,),
    start_indices_batching_dims=(1,),
)


def along_rows(x, k):
    return lax.gather(
        x, k[..., None], ALONG_ROWS, (1, 1), mode=lax.GatherScatterMode.PROMISE_IN_BOUNDS
    )


def pick(parts, k, high):
    return jnp.where(high, along_rows(parts[1], k), along_rows(parts[0], k))


def tables(transfer):
    base, slope = [], []
    for c in range(4):
        knots = jnp.broadcast_to(transfer[:, c : c + 1], (KNOTS, LANES))
        row = lax.broadcasted_iota(jnp.int32, (KNOTS, LANES), 0)
        after = jnp.where(row == KNOTS - 1, 0.0, pltpu.roll(knots, KNOTS - 1, 0))
        step = after - knots
        base.append((knots[:8], knots[8:]))
        slope.append((step[:8], step[8:]))
    return base, slope


def shade(src, p, j, carry, lookup, tile):
    red, green, blue, remaining = carry
    base, slope = lookup
    f = src[p, rows_at(j), :]
    depth = src[p + 1, rows_at(j), :] - src[p - 1, rows_at(j), :]
    row = src[p, rows_at(j, 1), :] - src[p, rows_at(j, -1), :]
    right = jnp.where(tile.at_last, f, pltpu.roll(f, LANES - 1, 1))
    left = jnp.where(tile.at_first, f, pltpu.roll(f, 1, 1))
    col = right - left
    square = depth * depth + row * row + col * col + 1.0
    gain = 1.0 - AMBIENT
    along = jnp.abs(0.64 * gain * depth + 0.6 * gain * row + 0.48 * gain * col)
    shading = AMBIENT + along * lax.rsqrt(square)
    position = f * ((KNOTS - 1) / UPPER_DENSITY)
    k = position.astype(jnp.int32)
    frac = position - k.astype(jnp.float32)
    high = k >= 8
    k = jnp.bitwise_and(k, 7)
    mixed = [pick(base[c], k, high) + frac * pick(slope[c], k, high) for c in range(4)]
    kept = jnp.exp(mixed[3] * (-OPTICAL_DEPTH / (DEEP * BLOCKS)))
    weight = remaining * (1.0 - kept) * shading
    return (
        red + weight * mixed[0],
        green + weight * mixed[1],
        blue + weight * mixed[2],
        remaining * kept,
    )


def inner_kernel(mine, knots, out, fa, fb, fluxes):
    tile = Tile()
    zero = jnp.zeros((8, LANES), jnp.float32)

    def fill(i, carry):
        for p in range(PLANES):
            put(fa, PLANES * i + p, [mine[i, p, 8 * j : 8 * j + 8, :] for j in range(TILES)])
        return carry

    lax.fori_loop(0, GROUP, fill, 0)
    src, dst = fa, fb
    for sweep in range(PASSES):
        lo, hi = sweep + 1, DEEP - 1 - sweep
        count = hi - lo
        unroll = 6 if count % 6 == 0 else UNROLL

        def step(i, carry, src=src, dst=dst, lo=lo, unroll=unroll):
            for u in range(unroll):
                p = lo + unroll * i + u
                carry = diffuse(src, p, dst, p, fluxes, u, carry, tile)
            return carry

        whole = count // unroll
        carry = lax.fori_loop(0, whole, step, first_flux(src, lo - 1))
        for u in range(count - unroll * whole):
            p = lo + unroll * whole + u
            carry = diffuse(src, p, dst, p, fluxes, u, carry, tile)
        kept = (lo, lo + 1, hi - 2, hi - 1)
        for i in range(EDGE):
            for j in range(TILES):
                out[EDGE * sweep + i, 8 * j : 8 * j + 8, :] = dst[kept[i], rows_at(j), :]
        src, dst = dst, src

    lookup = tables(knots)
    first = (zero, zero, zero, zero + 1.0)

    def shaded(j, unused):
        def planes(i, carry):
            for u in range(SHADED):
                carry = shade(src, HALO + SHADED * i + u, j, carry, lookup, tile)
            return carry

        sums = lax.fori_loop(0, (DEEP - 2 * HALO) // SHADED, planes, first)
        for c in range(4):
            out[EDGE * PASSES + c, pl.ds(pl.multiple_of(8 * j, 8), 8), :] = sums[c]
        return unused

    lax.fori_loop(0, TILES, shaded, 0)


def outer_kernel(head, tail, before, after, inner, knots, out, fa, fb, ga, gb, fluxes):
    tile = Tile()
    zero = jnp.zeros((8, LANES), jnp.float32)
    lookup = tables(knots)

    def fill(ref, to, source, i):
        put(ref, to, [source[i // 2, i % 2, 8 * j : 8 * j + 8, :] for j in range(TILES)])

    for i in range(2):
        fill(fa, 4 + i, head, i)
        fill(ga, i, tail, 2 + i)

    @pl.when(tile.block > 0)
    def _():
        for i in range(HALO):
            fill(fa, i, before, i)

    @pl.when(tile.block == 0)
    def _():
        for i in range(HALO):
            fill(fa, i, head, HALO - 1 - i)

    @pl.when(tile.block < BLOCKS - 1)
    def _():
        for i in range(HALO):
            fill(ga, 2 + i, after, i)

    @pl.when(tile.block == BLOCKS - 1)
    def _():
        for i in range(HALO):
            fill(ga, 2 + i, tail, HALO - 1 - i)

    front, back = (fa, fb), (ga, gb)
    for sweep in range(PASSES):
        for (src, dst), at in ((front, 0), (back, 2)):
            carry = first_flux(src, 0)
            for i in range(4):
                carry = diffuse(src, i + 1, dst, at + i, fluxes, at // 2 * 4 + i, carry, tile)
        for i in range(2):
            for ref, to, k in ((front[1], 4 + i, i), (back[1], i, 2 + i)):
                k += EDGE * sweep
                put(ref, to, [inner[k, 8 * j : 8 * j + 8, :] for j in range(TILES)])
        front, back = front[::-1], back[::-1]

    lane = lane_index()
    for j in range(TILES):
        carry = (zero, zero, zero, zero + 1.0)
        for i in range(4):
            carry = shade(front[0], i + 1, j, carry, lookup, tile)
        mid = [inner[EDGE * PASSES + c, 8 * j : 8 * j + 8, :] for c in range(4)]
        end = (zero, zero, zero, zero + 1.0)
        for i in range(4):
            end = shade(back[0], i + 1, j, end, lookup, tile)
        sums = [carry[c] + carry[3] * (mid[c] + mid[3] * end[c]) for c in range(3)]
        sums.append(carry[3] * mid[3] * end[3])
        for k in range(SEGS):
            value = None
            for c in range(4):
                by = TILE * c - WIDE * k - HALO - tile.start + LANES * 2
                moved = pltpu.roll(sums[c], lax.rem(by, LANES), 1)
                value = moved if value is None else jnp.where(lane >= TILE * c, moved, value)
            first = SEG_ROWS * k + 8 * j - HALO
            lo, hi = max(first, 0), min(first + 8, BAND)
            if lo < hi:
                out[lo:hi, :] = value[lo - first : hi - first]


def gather_kernel(parts, out):
    lane = lane_index(GROUP)
    total = jnp.zeros((GROUP, LANES), jnp.float32)
    remaining = jnp.ones((GROUP, LANES), jnp.float32)
    for b in range(BLOCKS):
        v = parts[GROUP * b : GROUP * (b + 1)]
        kept = v
        for c in range(3):
            kept = jnp.where(
                jnp.logical_and(lane >= TILE * c, lane < TILE * (c + 1)),
                pltpu.roll(v, TILE * (c + 1), 1),
                kept,
            )
        total = total + remaining * v
        remaining = remaining * kept
    total = jnp.where(lane >= 3 * TILE, 1.0 - remaining, total)
    turned = [total] + [pltpu.roll(total, TILE * s, 1) for s in range(1, 4)]
    for c in range(4):
        for t in range(GROUP):
            m = t % 4
            out[c, :, TILE * t : TILE * (t + 1)] = turned[(m - c) % 4][
                t : t + 1, TILE * m : TILE * (m + 1)
            ]


def call(kernel, shape, scratch, *operands):
    spec = pl.BlockSpec(memory_space=VMEM)
    operands = [pltpu.with_memory_space_constraint(x, VMEM) for x in operands]
    return pl.pallas_call(
        kernel,
        out_shape=VMEM(shape, jnp.float32),
        in_specs=[spec] * len(operands),
        out_specs=spec,
        scratch_shapes=[VMEM(s, jnp.float32) for s in scratch],
        name=kernel.__name__,
    )(*operands)


def shifted(value, axis, by):
    size = lax.axis_size(axis)
    pairs = [(i, i + by) for i in range(size) if 0 <= i + by < size]
    return lax.ppermute(value, axis, pairs)


def per_device(density, transfer_table):
    above = shifted(density[:, BAND - 8 :], "rows", 1)
    below = shifted(density[:, :8], "rows", -1)
    sent = call(
        pack_kernel,
        (GROUP, PLANES, SEG_ROWS, LANES),
        [(PLANES, SEGS * SEG_ROWS, COLS)],
        density,
        above,
        below,
    )
    groups = [[GROUP * b + i for i in range(GROUP)] for b in range(BLOCKS)]
    mine = lax.all_to_all(sent, "depth", 0, 0, axis_index_groups=groups, tiled=True)
    near = HALO // PLANES
    head, tail = mine[:near], mine[GROUP - near :]
    before = shifted(tail, "depth", GROUP)
    after = shifted(head, "depth", -GROUP)
    knots = transfer_table.T
    field = (DEEP, TALL, LANES)
    inner = call(
        inner_kernel,
        (EDGE * PASSES + 4, SEG_ROWS, LANES),
        [field, field, (UNROLL, TALL, LANES)],
        mine,
        knots,
    )
    few = (6, TALL, LANES)
    partial = call(
        outer_kernel,
        (BAND, LANES),
        [few, few, few, few, (8, TALL, LANES)],
        head,
        tail,
        before,
        after,
        inner,
        knots,
    )
    parts = lax.all_to_all(partial, "depth", 0, 0, tiled=True)
    return call(gather_kernel, (4, 1, COLS), [], parts)


def solution(mesh):
    placed = (P("depth", "rows", None), P())
    return jax.shard_map(
        per_device,
        mesh=mesh,
        in_specs=placed,
        out_specs=P(None, ("rows", "depth"), None),
        check_vma=False,
    )
```

```python
import jax
import jax.numpy as jnp
from jax import lax
from jax.experimental import pallas as pl
from jax.experimental.pallas import tpu as pltpu
from jax.sharding import PartitionSpec as P


PASSES = 3
KNOTS = 16
TIME_STEP = 0.15
OPTICAL_DEPTH = 3.0
UPPER_DENSITY = 6.0
AMBIENT = 0.35

GROUP = 16
BLOCKS = 8
HALO = 4
BAND = 128
COLS = 512
TILE = COLS // GROUP
WIDE = TILE + 2 * HALO
SEGS = 3
SEG_ROWS = 48
TILES = SEG_ROWS // 8
PLANES = 2
DEEP = GROUP * PLANES
LANES = 128
TOP = 8
TALL = SEG_ROWS + 2 * TOP
FRONT = HALO
UNROLL = 7
SHADED = 8
VMEM = pltpu.VMEM


def lane_index(rows=8):
    return lax.broadcasted_iota(jnp.int32, (rows, LANES), 1)


def window_masks():
    lane = lane_index()
    segment, left, right = [], [], []
    for m in range(4):
        local = (lane - (TILE * m - HALO)) % LANES
        segment.append([(local >= WIDE * k) & (local < WIDE * (k + 1)) for k in range(SEGS)])
        column = local % WIDE
        left.append(column < HALO)
        right.append(column >= WIDE - HALO)
    return segment, left, right


def windows(tiles, joined, left, right):
    for t in range(GROUP):
        q, m = divmod(t, 4)
        value = joined(tiles, q, m)
        if m == 0 and q > 0:
            value = jnp.where(left[m], joined(tiles, q - 1, m), value)
        if m == 3 and q < 3:
            value = jnp.where(right[m], joined(tiles, q + 1, m), value)
        yield t, m, value


def pack_kernel(density, out, own, ext, sem):
    copy = pltpu.make_async_copy(density, own, sem)
    copy.start()
    rows = SEGS * SEG_ROWS
    for p in range(PLANES):
        ext[p, :8, :] = jnp.zeros((8, COLS), jnp.float32)
        ext[p, rows - 16 :, :] = jnp.zeros((16, COLS), jnp.float32)
    segment, left, right = window_masks()
    copy.wait()
    for p in range(PLANES):
        ext[p, HALO : HALO + BAND, :] = own[p]

    def joined(rolled, q, m):
        rest = jnp.where(segment[m][1], rolled[1][q], rolled[2][q])
        return jnp.where(segment[m][0], rolled[0][q], rest)

    def step(it, carry):
        p = it // TILES
        j = it - TILES * p
        row = pl.multiple_of(8 * j, 8)
        rolled = []
        for k in range(SEGS):
            start = pl.multiple_of(row + SEG_ROWS * k, 8)
            tiles = [ext[p, pl.ds(start, 8), LANES * q : LANES * (q + 1)] for q in range(4)]
            rolled.append([pltpu.roll(x, WIDE * k, 1) if k else x for x in tiles])
        for t, m, value in windows(rolled, joined, left, right):
            out[t, p, pl.ds(row, 8), :] = value
        return carry

    lax.fori_loop(0, PLANES * TILES, step, 0)


def halo_kernel(sent, first, last, above, below, out, edge):
    band = lax.axis_index("rows")
    bands = lax.axis_size("rows")

    @pl.when(band > 0)
    def _():
        for p in range(PLANES):
            edge[p, 0:HALO, :] = above[p, 8 - HALO : 8, :]

    @pl.when(band == 0)
    def _():
        for p in range(PLANES):
            for i in range(HALO):
                edge[p, HALO - 1 - i : HALO - i, :] = first[p, i : i + 1, :]

    @pl.when(band < bands - 1)
    def _():
        for p in range(PLANES):
            edge[p, HALO : 2 * HALO, :] = below[p, 0:HALO, :]

    @pl.when(band == bands - 1)
    def _():
        for p in range(PLANES):
            for i in range(HALO):
                edge[p, HALO + i : HALO + i + 1, :] = last[p, 7 - i : 8 - i, :]

    segment, left, right = window_masks()
    row = lax.broadcasted_iota(jnp.int32, (8, LANES), 0)
    places = ((0, 0, row < HALO), (2, SEG_ROWS - 16, row >= HALO))

    def joined(rolled, q, m):
        return rolled[q]

    for p in range(PLANES):
        tiles = [edge[p, :, LANES * q : LANES * (q + 1)] for q in range(4)]
        for k, at, rows in places:
            rolled = [pltpu.roll(x, WIDE * k, 1) for x in tiles] if k else tiles
            for t, m, value in windows(rolled, joined, left, right):
                here = sent[t, p, at : at + 8, :]
                out[t, p, at : at + 8, :] = jnp.where(rows & segment[m][k], value, here)


def flux(change):
    return change / (1.0 + change * change)


def rows_at(j, by=0):
    if isinstance(j, int):
        return slice(TOP + 8 * j + by, TOP + 8 * j + by + 8)
    return pl.ds(pl.multiple_of(8 * j, 8) + TOP + by, 8)


def put(ref, p, tiles):
    for j in range(TILES):
        ref[p, rows_at(j), :] = tiles[j]
    ref[p, TOP - 1 : TOP, :] = pltpu.roll(tiles[-1], WIDE, 1)[7:8]
    ref[p, TOP + SEG_ROWS : TOP + SEG_ROWS + 1, :] = pltpu.roll(tiles[0], LANES - WIDE, 1)[0:1]


def take(ref, p, by=0):
    return [ref[p, rows_at(j, by), :] for j in range(TILES)]


class Tile:
    def __init__(self):
        self.block = lax.axis_index("depth") // GROUP
        tile = lax.axis_index("depth") % GROUP
        self.start = TILE * (tile % 4) - HALO
        local = (lane_index() - self.start + LANES) % LANES
        column = local % WIDE
        first, last = tile == 0, tile == GROUP - 1
        self.at_first = jnp.logical_and(column == HALO, first)
        self.at_last = jnp.logical_and(column == HALO + TILE - 1, last)
        self.open_face = jnp.where(
            jnp.logical_or(self.at_last, jnp.logical_and(column == HALO - 1, first)), 0.0, 1.0
        )


def diffuse(src, p, dst, to, fluxes, slot, flux_nearer, tile):
    f = take(src, p)
    below = take(src, p, 1)
    deeper = take(src, p + 1)
    flux_deeper = [flux(deeper[j] - f[j]) for j in range(TILES)]
    row = [flux(below[j] - f[j]) for j in range(TILES)]
    for j in range(TILES):
        fluxes[slot, rows_at(j), :] = row[j]
    fluxes[slot, TOP - 1 : TOP, :] = pltpu.roll(row[-1], WIDE, 1)[7:8]
    row_prev = take(fluxes, slot, -1)
    new = []
    for j in range(TILES):
        col = flux((pltpu.roll(f[j], LANES - 1, 1) - f[j]) * tile.open_face)
        total = flux_deeper[j] - flux_nearer[j]
        total = total + (row[j] - row_prev[j])
        total = total + (col - pltpu.roll(col, 1, 1))
        new.append(f[j] + TIME_STEP * total)
    put(dst, to, new)
    return flux_deeper


def first_flux(src, p):
    here, deeper = take(src, p), take(src, p + 1)
    return [flux(deeper[j] - here[j]) for j in range(TILES)]


ALONG_ROWS = lax.GatherDimensionNumbers(
    offset_dims=(),
    collapsed_slice_dims=(0,),
    start_index_map=(0,),
    operand_batching_dims=(1,),
    start_indices_batching_dims=(1,),
)


def along_rows(x, k):
    return lax.gather(
        x, k[..., None], ALONG_ROWS, (1, 1), mode=lax.GatherScatterMode.PROMISE_IN_BOUNDS
    )


def pick(parts, k, high):
    return jnp.where(high, along_rows(parts[1], k), along_rows(parts[0], k))


def tables(transfer):
    base, slope = [], []
    for c in range(4):
        knots = jnp.broadcast_to(transfer[:, c : c + 1], (KNOTS, LANES))
        row = lax.broadcasted_iota(jnp.int32, (KNOTS, LANES), 0)
        after = jnp.where(row == KNOTS - 1, 0.0, pltpu.roll(knots, KNOTS - 1, 0))
        step = after - knots
        base.append((knots[:8], knots[8:]))
        slope.append((step[:8], step[8:]))
    return base, slope


def shade(src, p, j, carry, lookup, tile):
    red, green, blue, remaining = carry
    base, slope = lookup
    f = src[p, rows_at(j), :]
    depth = src[p + 1, rows_at(j), :] - src[p - 1, rows_at(j), :]
    row = src[p, rows_at(j, 1), :] - src[p, rows_at(j, -1), :]
    right = jnp.where(tile.at_last, f, pltpu.roll(f, LANES - 1, 1))
    left = jnp.where(tile.at_first, f, pltpu.roll(f, 1, 1))
    col = right - left
    square = depth * depth + row * row + col * col + 1.0
    gain = 1.0 - AMBIENT
    along = jnp.abs(0.64 * gain * depth + 0.6 * gain * row + 0.48 * gain * col)
    shading = AMBIENT + along * lax.rsqrt(square)
    position = f * ((KNOTS - 1) / UPPER_DENSITY)
    k = position.astype(jnp.int32)
    frac = position - k.astype(jnp.float32)
    high = k >= 8
    k = jnp.bitwise_and(k, 7)
    mixed = [pick(base[c], k, high) + frac * pick(slope[c], k, high) for c in range(4)]
    kept = jnp.exp(mixed[3] * (-OPTICAL_DEPTH / (DEEP * BLOCKS)))
    weight = remaining * (1.0 - kept) * shading
    return (
        red + weight * mixed[0],
        green + weight * mixed[1],
        blue + weight * mixed[2],
        remaining * kept,
    )


def inner_kernel(mine, knots, out, fa, fb, fluxes, sums):
    tile = Tile()
    zero = jnp.zeros((8, LANES), jnp.float32)
    is_first = tile.block == 0

    def plane_of(i, p):
        return [mine[i, p, 8 * j : 8 * j + 8, :] for j in range(TILES)]

    def fill(i, carry):
        for p in range(PLANES):
            put(fa, FRONT + PLANES * i + p, plane_of(i, p))
        return carry

    lax.fori_loop(0, GROUP, fill, 0)

    @pl.when(is_first)
    def _():
        for i in range(HALO):
            put(fa, FRONT - 1 - i, plane_of(i // 2, i % 2))

    src, dst = fa, fb
    for sweep in range(PASSES):
        lo, hi = FRONT + sweep + 1, FRONT + DEEP - 1 - sweep

        @pl.when(is_first)
        def _(src=src, dst=dst, lo=lo):
            carry = first_flux(src, lo - 5)
            for u in range(4):
                p = lo - 4 + u
                carry = diffuse(src, p, dst, p, fluxes, u, carry, tile)

        count = hi - lo
        unroll = 6 if count % 6 == 0 else UNROLL

        def step(i, carry, src=src, dst=dst, lo=lo, unroll=unroll):
            for u in range(unroll):
                p = lo + unroll * i + u
                carry = diffuse(src, p, dst, p, fluxes, u, carry, tile)
            return carry

        whole = count // unroll
        carry = lax.fori_loop(0, whole, step, first_flux(src, lo - 1))
        for u in range(count - unroll * whole):
            p = lo + unroll * whole + u
            carry = diffuse(src, p, dst, p, fluxes, u, carry, tile)
        for i in range(2):
            for j in range(TILES):
                out[2 * sweep + i, 8 * j : 8 * j + 8, :] = dst[hi - 2 + i, rows_at(j), :]
        src, dst = dst, src

    lookup = tables(knots)
    start = (zero, zero, zero, zero + 1.0)

    def rows(j):
        return pl.ds(pl.multiple_of(8 * j, 8), 8)

    @pl.when(is_first)
    def _():
        def shaded(j, unused):
            carry = start
            for u in range(HALO):
                carry = shade(src, FRONT + u, j, carry, lookup, tile)
            for c in range(4):
                sums[c, rows(j), :] = carry[c]
            return unused

        lax.fori_loop(0, TILES, shaded, 0)

    @pl.when(jnp.logical_not(is_first))
    def _():
        for c in range(4):
            for j in range(TILES):
                sums[c, 8 * j : 8 * j + 8, :] = start[c]

    def shaded(j, unused):
        def planes(i, carry):
            for u in range(SHADED):
                p = FRONT + HALO + SHADED * i + u
                carry = shade(src, p, j, carry, lookup, tile)
            return carry

        carry = tuple(sums[c, rows(j), :] for c in range(4))
        carry = lax.fori_loop(0, (DEEP - 2 * HALO) // SHADED, planes, carry)
        for c in range(4):
            out[2 * PASSES + c, rows(j), :] = carry[c]
        return unused

    lax.fori_loop(0, TILES, shaded, 0)


def outer_kernel(tail, after, inner, knots, out, fa, fb, fluxes):
    tile = Tile()
    lookup = tables(knots)
    is_last = tile.block == BLOCKS - 1

    def fill(to, source, i):
        put(fa, to, [source[i // 2, i % 2, 8 * j : 8 * j + 8, :] for j in range(TILES)])

    near = HALO // PLANES
    for i in range(2):
        fill(i, tail, 2 * near - 2 + i)

    @pl.when(jnp.logical_not(is_last))
    def _():
        for i in range(2 * HALO):
            fill(2 + i, after, i)

    @pl.when(is_last)
    def _():
        for i in range(2 * HALO):
            fill(2 + i, tail, max(HALO - 1 - i, 0))

    src, dst = fa, fb
    for sweep in range(PASSES):
        carry = first_flux(src, 0)
        for i in range(2 * HALO):
            carry = diffuse(src, i + 1, dst, i + 2, fluxes, i, carry, tile)
        for i in range(2):
            rest = [inner[2 * sweep + i, 8 * j : 8 * j + 8, :] for j in range(TILES)]
            put(dst, i, rest)
        src, dst = dst, src

    lane = lane_index()
    for j in range(TILES):
        sums = tuple(inner[2 * PASSES + c, 8 * j : 8 * j + 8, :] for c in range(4))
        for i in range(2 * HALO):
            if i == HALO:
                own = sums
            sums = shade(src, i + 1, j, sums, lookup, tile)
        sums = [jnp.where(is_last, own[c], sums[c]) for c in range(4)]
        for k in range(SEGS):
            value = None
            for c in range(4):
                by = TILE * c - WIDE * k - HALO - tile.start + LANES * 2
                moved = pltpu.roll(sums[c], lax.rem(by, LANES), 1)
                value = moved if value is None else jnp.where(lane >= TILE * c, moved, value)
            first = SEG_ROWS * k + 8 * j - HALO
            lo, hi = max(first, 0), min(first + 8, BAND)
            if lo < hi:
                out[lo:hi, :] = value[lo - first : hi - first]


def gather_kernel(parts, out):
    lane = lane_index(GROUP)
    total = jnp.zeros((GROUP, LANES), jnp.float32)
    remaining = jnp.ones((GROUP, LANES), jnp.float32)
    for b in range(BLOCKS):
        v = parts[GROUP * b : GROUP * (b + 1)]
        kept = v
        for c in range(3):
            kept = jnp.where(
                jnp.logical_and(lane >= TILE * c, lane < TILE * (c + 1)),
                pltpu.roll(v, TILE * (c + 1), 1),
                kept,
            )
        total = total + remaining * v
        remaining = remaining * kept
    total = jnp.where(lane >= 3 * TILE, 1.0 - remaining, total)
    turned = [total] + [pltpu.roll(total, TILE * s, 1) for s in range(1, 4)]
    for c in range(4):
        for t in range(GROUP):
            m = t % 4
            out[c, :, TILE * t : TILE * (t + 1)] = turned[(m - c) % 4][
                t : t + 1, TILE * m : TILE * (m + 1)
            ]


def call(kernel, shape, scratch, *operands, **options):
    spec = pl.BlockSpec(memory_space=VMEM)
    operands = [pltpu.with_memory_space_constraint(x, VMEM) for x in operands]
    return pl.pallas_call(
        kernel,
        out_shape=VMEM(shape, jnp.float32),
        in_specs=[spec] * len(operands),
        out_specs=spec,
        scratch_shapes=[VMEM(s, jnp.float32) for s in scratch],
        name=kernel.__name__,
        **options,
    )(*operands)


def shifted(value, axis, by):
    size = lax.axis_size(axis)
    pairs = [(i, i + by) for i in range(size) if 0 <= i + by < size]
    return lax.ppermute(value, axis, pairs)


def per_device(density, transfer_table):
    first, last = density[:, :8], density[:, BAND - 8 :]
    above = shifted(last, "rows", 1)
    below = shifted(first, "rows", -1)
    chunks = (GROUP, PLANES, SEG_ROWS, LANES)
    cut = pl.pallas_call(
        pack_kernel,
        out_shape=VMEM(chunks, jnp.float32),
        in_specs=[pl.BlockSpec(memory_space=pl.ANY)],
        out_specs=pl.BlockSpec(memory_space=VMEM),
        scratch_shapes=[
            VMEM((PLANES, BAND, COLS), jnp.float32),
            VMEM((PLANES, SEGS * SEG_ROWS, COLS), jnp.float32),
            pltpu.SemaphoreType.DMA,
        ],
        name="pack_kernel",
    )(density)
    sent = call(
        halo_kernel,
        chunks,
        [(PLANES, 8, COLS)],
        cut,
        first,
        last,
        above,
        below,
        input_output_aliases={0: 0},
    )
    groups = [[GROUP * b + i for i in range(GROUP)] for b in range(BLOCKS)]
    mine = lax.all_to_all(sent, "depth", 0, 0, axis_index_groups=groups, tiled=True)
    near = HALO // PLANES
    tail = mine[GROUP - near :]
    after = shifted(mine[: 2 * near], "depth", -GROUP)
    knots = transfer_table.T
    field = (FRONT + DEEP, TALL, LANES)
    inner = call(
        inner_kernel,
        (2 * PASSES + 4, SEG_ROWS, LANES),
        [field, field, (UNROLL, TALL, LANES), (4, SEG_ROWS, LANES)],
        mine,
        knots,
    )
    few = (2 * HALO + 2, TALL, LANES)
    partial = call(
        outer_kernel,
        (BAND, LANES),
        [few, few, (2 * HALO, TALL, LANES)],
        tail,
        after,
        inner,
        knots,
    )
    parts = lax.all_to_all(partial, "depth", 0, 0, tiled=True)
    return call(gather_kernel, (4, 1, COLS), [], parts)


def solution(mesh):
    placed = (P("depth", "rows", None), P())
    return jax.shard_map(
        per_device,
        mesh=mesh,
        in_specs=placed,
        out_specs=P(None, ("rows", "depth"), None),
        check_vma=False,
    )
```

```python
import jax
import jax.numpy as jnp
from jax import lax
from jax.experimental import pallas as pl
from jax.experimental.pallas import tpu as pltpu
from jax.sharding import PartitionSpec as P


PASSES = 3
KNOTS = 16
TIME_STEP = 0.15
OPTICAL_DEPTH = 3.0
UPPER_DENSITY = 6.0
AMBIENT = 0.35

GROUP = 16
BLOCKS = 8
HALO = 4
BAND = 128
COLS = 512
TILE = COLS // GROUP
WIDE = TILE + 2 * HALO
SEGS = 3
SEG_ROWS = 48
TILES = SEG_ROWS // 8
PLANES = 2
DEEP = GROUP * PLANES
LANES = 128
TOP = 8
TALL = SEG_ROWS + 2 * TOP
FRONT = HALO
UNROLL = 7
SHADED = 8
VMEM = pltpu.VMEM


def lane_index(rows=8):
    return lax.broadcasted_iota(jnp.int32, (rows, LANES), 1)


def window_masks():
    lane = lane_index()
    segment, left, right = [], [], []
    for m in range(4):
        local = (lane - (TILE * m - HALO)) % LANES
        segment.append([(local >= WIDE * k) & (local < WIDE * (k + 1)) for k in range(SEGS)])
        column = local % WIDE
        left.append(column < HALO)
        right.append(column >= WIDE - HALO)
    return segment, left, right


def windows(tiles, joined, left, right):
    for t in range(GROUP):
        q, m = divmod(t, 4)
        value = joined(tiles, q, m)
        if m == 0 and q > 0:
            value = jnp.where(left[m], joined(tiles, q - 1, m), value)
        if m == 3 and q < 3:
            value = jnp.where(right[m], joined(tiles, q + 1, m), value)
        yield t, m, value


def load_kernel(density, own, first, last, sems):
    copies = [
        (density.at[:, pl.ds(0, 8), :], first),
        (density.at[:, pl.ds(BAND - 8, 8), :], last),
    ]
    rows = BAND // 4
    for p in range(PLANES):
        for i in range(4):
            part = pl.ds(rows * i, rows)
            copies.append((density.at[p, part, :], own.at[p, part, :]))
    started = [
        pltpu.make_async_copy(source, to, sems.at[i]) for i, (source, to) in enumerate(copies)
    ]
    for copy in started:
        copy.start()
    for copy in started:
        copy.wait()


def pack_kernel(own, out, ext):
    rows = SEGS * SEG_ROWS
    for p in range(PLANES):
        ext[p, :8, :] = jnp.zeros((8, COLS), jnp.float32)
        ext[p, rows - 16 :, :] = jnp.zeros((16, COLS), jnp.float32)
    segment, left, right = window_masks()
    for p in range(PLANES):
        ext[p, HALO : HALO + BAND, :] = own[p]

    def joined(rolled, q, m):
        rest = jnp.where(segment[m][1], rolled[1][q], rolled[2][q])
        return jnp.where(segment[m][0], rolled[0][q], rest)

    def step(it, carry):
        p = it // TILES
        j = it - TILES * p
        row = pl.multiple_of(8 * j, 8)
        rolled = []
        for k in range(SEGS):
            start = pl.multiple_of(row + SEG_ROWS * k, 8)
            tiles = [ext[p, pl.ds(start, 8), LANES * q : LANES * (q + 1)] for q in range(4)]
            rolled.append([pltpu.roll(x, WIDE * k, 1) if k else x for x in tiles])
        for t, m, value in windows(rolled, joined, left, right):
            out[t, p, pl.ds(row, 8), :] = value
        return carry

    lax.fori_loop(0, PLANES * TILES, step, 0)


def halo_kernel(sent, first, last, above, below, out, edge):
    band = lax.axis_index("rows")
    bands = lax.axis_size("rows")

    @pl.when(band > 0)
    def _():
        for p in range(PLANES):
            edge[p, 0:HALO, :] = above[p, 8 - HALO : 8, :]

    @pl.when(band == 0)
    def _():
        for p in range(PLANES):
            for i in range(HALO):
                edge[p, HALO - 1 - i : HALO - i, :] = first[p, i : i + 1, :]

    @pl.when(band < bands - 1)
    def _():
        for p in range(PLANES):
            edge[p, HALO : 2 * HALO, :] = below[p, 0:HALO, :]

    @pl.when(band == bands - 1)
    def _():
        for p in range(PLANES):
            for i in range(HALO):
                edge[p, HALO + i : HALO + i + 1, :] = last[p, 7 - i : 8 - i, :]

    segment, left, right = window_masks()
    row = lax.broadcasted_iota(jnp.int32, (8, LANES), 0)
    places = ((0, 0, row < HALO), (2, SEG_ROWS - 16, row >= HALO))

    def joined(rolled, q, m):
        return rolled[q]

    for p in range(PLANES):
        tiles = [edge[p, :, LANES * q : LANES * (q + 1)] for q in range(4)]
        for k, at, rows in places:
            rolled = [pltpu.roll(x, WIDE * k, 1) for x in tiles] if k else tiles
            for t, m, value in windows(rolled, joined, left, right):
                here = sent[t, p, at : at + 8, :]
                out[t, p, at : at + 8, :] = jnp.where(rows & segment[m][k], value, here)


def flux(change):
    return change / (1.0 + change * change)


def rows_at(j, by=0):
    if isinstance(j, int):
        return slice(TOP + 8 * j + by, TOP + 8 * j + by + 8)
    return pl.ds(pl.multiple_of(8 * j, 8) + TOP + by, 8)


def put(ref, p, tiles):
    for j in range(TILES):
        ref[p, rows_at(j), :] = tiles[j]
    ref[p, TOP - 1 : TOP, :] = pltpu.roll(tiles[-1], WIDE, 1)[7:8]
    ref[p, TOP + SEG_ROWS : TOP + SEG_ROWS + 1, :] = pltpu.roll(tiles[0], LANES - WIDE, 1)[0:1]


def take(ref, p, by=0):
    return [ref[p, rows_at(j, by), :] for j in range(TILES)]


class Tile:
    def __init__(self):
        self.block = lax.axis_index("depth") // GROUP
        tile = lax.axis_index("depth") % GROUP
        self.start = TILE * (tile % 4) - HALO
        local = (lane_index() - self.start + LANES) % LANES
        column = local % WIDE
        first, last = tile == 0, tile == GROUP - 1
        self.at_first = jnp.logical_and(column == HALO, first)
        self.at_last = jnp.logical_and(column == HALO + TILE - 1, last)
        self.open_face = jnp.where(
            jnp.logical_or(self.at_last, jnp.logical_and(column == HALO - 1, first)), 0.0, 1.0
        )


def diffuse(src, p, dst, to, fluxes, slot, flux_nearer, tile):
    f = take(src, p)
    below = take(src, p, 1)
    deeper = take(src, p + 1)
    flux_deeper = [flux(deeper[j] - f[j]) for j in range(TILES)]
    row = [flux(below[j] - f[j]) for j in range(TILES)]
    for j in range(TILES):
        fluxes[slot, rows_at(j), :] = row[j]
    fluxes[slot, TOP - 1 : TOP, :] = pltpu.roll(row[-1], WIDE, 1)[7:8]
    row_prev = take(fluxes, slot, -1)
    new = []
    for j in range(TILES):
        col = flux((pltpu.roll(f[j], LANES - 1, 1) - f[j]) * tile.open_face)
        total = flux_deeper[j] - flux_nearer[j]
        total = total + (row[j] - row_prev[j])
        total = total + (col - pltpu.roll(col, 1, 1))
        new.append(f[j] + TIME_STEP * total)
    put(dst, to, new)
    return flux_deeper


def first_flux(src, p):
    here, deeper = take(src, p), take(src, p + 1)
    return [flux(deeper[j] - here[j]) for j in range(TILES)]


ALONG_ROWS = lax.GatherDimensionNumbers(
    offset_dims=(),
    collapsed_slice_dims=(0,),
    start_index_map=(0,),
    operand_batching_dims=(1,),
    start_indices_batching_dims=(1,),
)


def along_rows(x, k):
    return lax.gather(
        x, k[..., None], ALONG_ROWS, (1, 1), mode=lax.GatherScatterMode.PROMISE_IN_BOUNDS
    )


def pick(parts, k, high):
    return jnp.where(high, along_rows(parts[1], k), along_rows(parts[0], k))


def tables(transfer):
    base, slope = [], []
    for c in range(4):
        knots = jnp.broadcast_to(transfer[:, c : c + 1], (KNOTS, LANES))
        row = lax.broadcasted_iota(jnp.int32, (KNOTS, LANES), 0)
        after = jnp.where(row == KNOTS - 1, 0.0, pltpu.roll(knots, KNOTS - 1, 0))
        step = after - knots
        base.append((knots[:8], knots[8:]))
        slope.append((step[:8], step[8:]))
    return base, slope


def shade(src, p, j, carry, lookup, tile):
    red, green, blue, remaining = carry
    base, slope = lookup
    f = src[p, rows_at(j), :]
    depth = src[p + 1, rows_at(j), :] - src[p - 1, rows_at(j), :]
    row = src[p, rows_at(j, 1), :] - src[p, rows_at(j, -1), :]
    right = jnp.where(tile.at_last, f, pltpu.roll(f, LANES - 1, 1))
    left = jnp.where(tile.at_first, f, pltpu.roll(f, 1, 1))
    col = right - left
    square = depth * depth + row * row + col * col + 1.0
    gain = 1.0 - AMBIENT
    along = jnp.abs(0.64 * gain * depth + 0.6 * gain * row + 0.48 * gain * col)
    shading = AMBIENT + along * lax.rsqrt(square)
    position = f * ((KNOTS - 1) / UPPER_DENSITY)
    k = position.astype(jnp.int32)
    frac = position - k.astype(jnp.float32)
    high = k >= 8
    k = jnp.bitwise_and(k, 7)
    mixed = [pick(base[c], k, high) + frac * pick(slope[c], k, high) for c in range(4)]
    kept = jnp.exp(mixed[3] * (-OPTICAL_DEPTH / (DEEP * BLOCKS)))
    weight = remaining * (1.0 - kept) * shading
    return (
        red + weight * mixed[0],
        green + weight * mixed[1],
        blue + weight * mixed[2],
        remaining * kept,
    )


def inner_kernel(mine, knots, out, fa, fb, fluxes, sums):
    tile = Tile()
    zero = jnp.zeros((8, LANES), jnp.float32)
    is_first = tile.block == 0

    def plane_of(i, p):
        return [mine[i, p, 8 * j : 8 * j + 8, :] for j in range(TILES)]

    def fill(i, carry):
        for p in range(PLANES):
            put(fa, FRONT + PLANES * i + p, plane_of(i, p))
        return carry

    lax.fori_loop(0, GROUP, fill, 0)

    @pl.when(is_first)
    def _():
        for i in range(HALO):
            put(fa, FRONT - 1 - i, plane_of(i // 2, i % 2))

    src, dst = fa, fb
    for sweep in range(PASSES):
        lo, hi = FRONT + sweep + 1, FRONT + DEEP - 1 - sweep

        @pl.when(is_first)
        def _(src=src, dst=dst, lo=lo):
            carry = first_flux(src, lo - 5)
            for u in range(4):
                p = lo - 4 + u
                carry = diffuse(src, p, dst, p, fluxes, u, carry, tile)

        count = hi - lo
        unroll = 6 if count % 6 == 0 else UNROLL

        def step(i, carry, src=src, dst=dst, lo=lo, unroll=unroll):
            for u in range(unroll):
                p = lo + unroll * i + u
                carry = diffuse(src, p, dst, p, fluxes, u, carry, tile)
            return carry

        whole = count // unroll
        carry = lax.fori_loop(0, whole, step, first_flux(src, lo - 1))
        for u in range(count - unroll * whole):
            p = lo + unroll * whole + u
            carry = diffuse(src, p, dst, p, fluxes, u, carry, tile)
        for i in range(2):
            for j in range(TILES):
                out[2 * sweep + i, 8 * j : 8 * j + 8, :] = dst[hi - 2 + i, rows_at(j), :]
        src, dst = dst, src

    lookup = tables(knots)
    start = (zero, zero, zero, zero + 1.0)

    def rows(j):
        return pl.ds(pl.multiple_of(8 * j, 8), 8)

    @pl.when(is_first)
    def _():
        def shaded(j, unused):
            carry = start
            for u in range(HALO):
                carry = shade(src, FRONT + u, j, carry, lookup, tile)
            for c in range(4):
                sums[c, rows(j), :] = carry[c]
            return unused

        lax.fori_loop(0, TILES, shaded, 0)

    @pl.when(jnp.logical_not(is_first))
    def _():
        for c in range(4):
            for j in range(TILES):
                sums[c, 8 * j : 8 * j + 8, :] = start[c]

    def shaded(j, unused):
        def planes(i, carry):
            for u in range(SHADED):
                p = FRONT + HALO + SHADED * i + u
                carry = shade(src, p, j, carry, lookup, tile)
            return carry

        carry = tuple(sums[c, rows(j), :] for c in range(4))
        carry = lax.fori_loop(0, (DEEP - 2 * HALO) // SHADED, planes, carry)
        for c in range(4):
            out[2 * PASSES + c, rows(j), :] = carry[c]
        return unused

    lax.fori_loop(0, TILES, shaded, 0)


def outer_kernel(tail, after, inner, knots, out, fa, fb, fluxes):
    tile = Tile()
    lookup = tables(knots)
    is_last = tile.block == BLOCKS - 1

    def fill(to, source, i):
        put(fa, to, [source[i // 2, i % 2, 8 * j : 8 * j + 8, :] for j in range(TILES)])

    near = HALO // PLANES
    for i in range(2):
        fill(i, tail, 2 * near - 2 + i)

    @pl.when(jnp.logical_not(is_last))
    def _():
        for i in range(2 * HALO):
            fill(2 + i, after, i)

    @pl.when(is_last)
    def _():
        for i in range(2 * HALO):
            fill(2 + i, tail, max(HALO - 1 - i, 0))

    src, dst = fa, fb
    for sweep in range(PASSES):
        carry = first_flux(src, 0)
        for i in range(2 * HALO):
            carry = diffuse(src, i + 1, dst, i + 2, fluxes, i, carry, tile)
        for i in range(2):
            rest = [inner[2 * sweep + i, 8 * j : 8 * j + 8, :] for j in range(TILES)]
            put(dst, i, rest)
        src, dst = dst, src

    lane = lane_index()
    for j in range(TILES):
        sums = tuple(inner[2 * PASSES + c, 8 * j : 8 * j + 8, :] for c in range(4))
        for i in range(2 * HALO):
            if i == HALO:
                own = sums
            sums = shade(src, i + 1, j, sums, lookup, tile)
        sums = [jnp.where(is_last, own[c], sums[c]) for c in range(4)]
        for k in range(SEGS):
            value = None
            for c in range(4):
                by = TILE * c - WIDE * k - HALO - tile.start + LANES * 2
                moved = pltpu.roll(sums[c], lax.rem(by, LANES), 1)
                value = moved if value is None else jnp.where(lane >= TILE * c, moved, value)
            first = SEG_ROWS * k + 8 * j - HALO
            lo, hi = max(first, 0), min(first + 8, BAND)
            if lo < hi:
                out[lo:hi, :] = value[lo - first : hi - first]


def gather_kernel(parts, out):
    lane = lane_index(GROUP)
    total = jnp.zeros((GROUP, LANES), jnp.float32)
    remaining = jnp.ones((GROUP, LANES), jnp.float32)
    for b in range(BLOCKS):
        v = parts[GROUP * b : GROUP * (b + 1)]
        kept = v
        for c in range(3):
            kept = jnp.where(
                jnp.logical_and(lane >= TILE * c, lane < TILE * (c + 1)),
                pltpu.roll(v, TILE * (c + 1), 1),
                kept,
            )
        total = total + remaining * v
        remaining = remaining * kept
    total = jnp.where(lane >= 3 * TILE, 1.0 - remaining, total)
    turned = [total] + [pltpu.roll(total, TILE * s, 1) for s in range(1, 4)]
    for c in range(4):
        for t in range(GROUP):
            m = t % 4
            out[c, :, TILE * t : TILE * (t + 1)] = turned[(m - c) % 4][
                t : t + 1, TILE * m : TILE * (m + 1)
            ]


def call(kernel, shape, scratch, *operands, **options):
    spec = pl.BlockSpec(memory_space=VMEM)
    operands = [pltpu.with_memory_space_constraint(x, VMEM) for x in operands]
    return pl.pallas_call(
        kernel,
        out_shape=VMEM(shape, jnp.float32),
        in_specs=[spec] * len(operands),
        out_specs=spec,
        scratch_shapes=[VMEM(s, jnp.float32) for s in scratch],
        name=kernel.__name__,
        **options,
    )(*operands)


def shifted(value, axis, by):
    size = lax.axis_size(axis)
    pairs = [(i, i + by) for i in range(size) if 0 <= i + by < size]
    return lax.ppermute(value, axis, pairs)


def per_device(density, transfer_table):
    edge = VMEM((PLANES, 8, COLS), jnp.float32)
    own, first, last = pl.pallas_call(
        load_kernel,
        out_shape=[VMEM(density.shape, jnp.float32), edge, edge],
        in_specs=[pl.BlockSpec(memory_space=pl.ANY)],
        out_specs=[pl.BlockSpec(memory_space=VMEM)] * 3,
        scratch_shapes=[pltpu.SemaphoreType.DMA((2 + 4 * PLANES,))],
        name="load_kernel",
    )(density)
    above = shifted(last, "rows", 1)
    below = shifted(first, "rows", -1)
    chunks = (GROUP, PLANES, SEG_ROWS, LANES)
    cut = call(pack_kernel, chunks, [(PLANES, SEGS * SEG_ROWS, COLS)], own)
    sent = call(
        halo_kernel,
        chunks,
        [(PLANES, 8, COLS)],
        cut,
        first,
        last,
        above,
        below,
        input_output_aliases={0: 0},
    )
    groups = [[GROUP * b + i for i in range(GROUP)] for b in range(BLOCKS)]
    mine = lax.all_to_all(sent, "depth", 0, 0, axis_index_groups=groups, tiled=True)
    near = HALO // PLANES
    tail = mine[GROUP - near :]
    after = shifted(mine[: 2 * near], "depth", -GROUP)
    knots = transfer_table.T
    field = (FRONT + DEEP, TALL, LANES)
    inner = call(
        inner_kernel,
        (2 * PASSES + 4, SEG_ROWS, LANES),
        [field, field, (UNROLL, TALL, LANES), (4, SEG_ROWS, LANES)],
        mine,
        knots,
    )
    few = (2 * HALO + 2, TALL, LANES)
    partial = call(
        outer_kernel,
        (BAND, LANES),
        [few, few, (2 * HALO, TALL, LANES)],
        tail,
        after,
        inner,
        knots,
    )
    parts = lax.all_to_all(partial, "depth", 0, 0, tiled=True)
    return call(gather_kernel, (4, 1, COLS), [], parts)


def solution(mesh):
    placed = (P("depth", "rows", None), P())
    return jax.shard_map(
        per_device,
        mesh=mesh,
        in_specs=placed,
        out_specs=P(None, ("rows", "depth"), None),
        check_vma=False,
    )
```

```python
import jax
import jax.numpy as jnp
from jax import lax
from jax.experimental import pallas as pl
from jax.experimental.pallas import tpu as pltpu
from jax.sharding import PartitionSpec as P


PASSES = 3
KNOTS = 16
TIME_STEP = 0.15
OPTICAL_DEPTH = 3.0
UPPER_DENSITY = 6.0
AMBIENT = 0.35

GROUP = 16
BLOCKS = 8
HALO = 4
BAND = 128
COLS = 512
TILE = COLS // GROUP
WIDE = TILE + 2 * HALO
SEGS = 3
SEG_ROWS = 48
TILES = SEG_ROWS // 8
PLANES = 2
DEEP = GROUP * PLANES
LANES = 128
TOP = 8
TALL = SEG_ROWS + 2 * TOP
FRONT = HALO
PARTS = 4
UNROLL = 7
SHADED = 8
VMEM = pltpu.VMEM


def lane_index(rows=8):
    return lax.broadcasted_iota(jnp.int32, (rows, LANES), 1)


def window_masks():
    lane = lane_index()
    segment, left, right = [], [], []
    for m in range(4):
        local = (lane - (TILE * m - HALO)) % LANES
        segment.append([(local >= WIDE * k) & (local < WIDE * (k + 1)) for k in range(SEGS)])
        column = local % WIDE
        left.append(column < HALO)
        right.append(column >= WIDE - HALO)
    return segment, left, right


def windows(tiles, joined, left, right):
    for t in range(GROUP):
        q, m = divmod(t, 4)
        value = joined(tiles, q, m)
        if m == 0 and q > 0:
            value = jnp.where(left[m], joined(tiles, q - 1, m), value)
        if m == 3 and q < 3:
            value = jnp.where(right[m], joined(tiles, q + 1, m), value)
        yield t, m, value


def slice_kernel(density, first, last, sems):
    copies = [
        pltpu.make_async_copy(density.at[:, pl.ds(row, 8), :], to, sems.at[i])
        for i, (row, to) in enumerate(((0, first), (BAND - 8, last)))
    ]
    for copy in copies:
        copy.start()
    for copy in copies:
        copy.wait()


def pack_kernel(density, out, own, ext, sems):
    rows = SEGS * SEG_ROWS
    part = BAND // PARTS
    copies = []
    for p in range(PLANES):
        for i in range(PARTS):
            at = pl.ds(part * i, part)
            copies.append(
                pltpu.make_async_copy(density.at[p, at, :], own.at[p, at, :], sems.at[p, i])
            )
    for copy in copies:
        copy.start()
    for p in range(PLANES):
        ext[p, :8, :] = jnp.zeros((8, COLS), jnp.float32)
        ext[p, rows - 16 :, :] = jnp.zeros((16, COLS), jnp.float32)
    segment, left, right = window_masks()

    def joined(rolled, q, m):
        rest = jnp.where(segment[m][1], rolled[1][q], rolled[2][q])
        return jnp.where(segment[m][0], rolled[0][q], rest)

    def step(j, p):
        row = pl.multiple_of(8 * j, 8)
        rolled = []
        for k in range(SEGS):
            start = pl.multiple_of(row + SEG_ROWS * k, 8)
            tiles = [ext[p, pl.ds(start, 8), LANES * q : LANES * (q + 1)] for q in range(4)]
            rolled.append([pltpu.roll(x, WIDE * k, 1) if k else x for x in tiles])
        for t, m, value in windows(rolled, joined, left, right):
            out[t, p, pl.ds(row, 8), :] = value
        return p

    for p in range(PLANES):
        for copy in copies[PARTS * p : PARTS * (p + 1)]:
            copy.wait()
        ext[p, HALO : HALO + BAND, :] = own[p]
        for j in range(TILES):
            step(j, p)


def halo_kernel(sent, first, last, above, below, out, edge):
    band = lax.axis_index("rows")
    bands = lax.axis_size("rows")

    @pl.when(band > 0)
    def _():
        for p in range(PLANES):
            edge[p, 0:HALO, :] = above[p, 8 - HALO : 8, :]

    @pl.when(band == 0)
    def _():
        for p in range(PLANES):
            for i in range(HALO):
                edge[p, HALO - 1 - i : HALO - i, :] = first[p, i : i + 1, :]

    @pl.when(band < bands - 1)
    def _():
        for p in range(PLANES):
            edge[p, HALO : 2 * HALO, :] = below[p, 0:HALO, :]

    @pl.when(band == bands - 1)
    def _():
        for p in range(PLANES):
            for i in range(HALO):
                edge[p, HALO + i : HALO + i + 1, :] = last[p, 7 - i : 8 - i, :]

    segment, left, right = window_masks()
    row = lax.broadcasted_iota(jnp.int32, (8, LANES), 0)
    places = ((0, 0, row < HALO), (2, SEG_ROWS - 16, row >= HALO))

    def joined(rolled, q, m):
        return rolled[q]

    for p in range(PLANES):
        tiles = [edge[p, :, LANES * q : LANES * (q + 1)] for q in range(4)]
        for k, at, rows in places:
            rolled = [pltpu.roll(x, WIDE * k, 1) for x in tiles] if k else tiles
            for t, m, value in windows(rolled, joined, left, right):
                here = sent[t, p, at : at + 8, :]
                out[t, p, at : at + 8, :] = jnp.where(rows & segment[m][k], value, here)


def flux(change):
    return change / (1.0 + change * change)


def rows_at(j, by=0):
    if isinstance(j, int):
        return slice(TOP + 8 * j + by, TOP + 8 * j + by + 8)
    return pl.ds(pl.multiple_of(8 * j, 8) + TOP + by, 8)


def put(ref, p, tiles):
    for j in range(TILES):
        ref[p, rows_at(j), :] = tiles[j]
    ref[p, TOP - 1 : TOP, :] = pltpu.roll(tiles[-1], WIDE, 1)[7:8]
    ref[p, TOP + SEG_ROWS : TOP + SEG_ROWS + 1, :] = pltpu.roll(tiles[0], LANES - WIDE, 1)[0:1]


def take(ref, p, by=0):
    return [ref[p, rows_at(j, by), :] for j in range(TILES)]


class Tile:
    def __init__(self):
        self.block = lax.axis_index("depth") // GROUP
        tile = lax.axis_index("depth") % GROUP
        self.start = TILE * (tile % 4) - HALO
        local = (lane_index() - self.start + LANES) % LANES
        column = local % WIDE
        first, last = tile == 0, tile == GROUP - 1
        self.at_first = jnp.logical_and(column == HALO, first)
        self.at_last = jnp.logical_and(column == HALO + TILE - 1, last)
        self.open_face = jnp.where(
            jnp.logical_or(self.at_last, jnp.logical_and(column == HALO - 1, first)), 0.0, 1.0
        )


def diffuse(src, p, dst, to, fluxes, slot, flux_nearer, tile):
    f = take(src, p)
    below = take(src, p, 1)
    deeper = take(src, p + 1)
    flux_deeper = [flux(deeper[j] - f[j]) for j in range(TILES)]
    row = [flux(below[j] - f[j]) for j in range(TILES)]
    for j in range(TILES):
        fluxes[slot, rows_at(j), :] = row[j]
    fluxes[slot, TOP - 1 : TOP, :] = pltpu.roll(row[-1], WIDE, 1)[7:8]
    row_prev = take(fluxes, slot, -1)
    new = []
    for j in range(TILES):
        col = flux((pltpu.roll(f[j], LANES - 1, 1) - f[j]) * tile.open_face)
        total = flux_deeper[j] - flux_nearer[j]
        total = total + (row[j] - row_prev[j])
        total = total + (col - pltpu.roll(col, 1, 1))
        new.append(f[j] + TIME_STEP * total)
    put(dst, to, new)
    return flux_deeper


def first_flux(src, p):
    here, deeper = take(src, p), take(src, p + 1)
    return [flux(deeper[j] - here[j]) for j in range(TILES)]


ALONG_ROWS = lax.GatherDimensionNumbers(
    offset_dims=(),
    collapsed_slice_dims=(0,),
    start_index_map=(0,),
    operand_batching_dims=(1,),
    start_indices_batching_dims=(1,),
)


def along_rows(x, k):
    return lax.gather(
        x, k[..., None], ALONG_ROWS, (1, 1), mode=lax.GatherScatterMode.PROMISE_IN_BOUNDS
    )


def pick(parts, k, high):
    return jnp.where(high, along_rows(parts[1], k), along_rows(parts[0], k))


def tables(transfer):
    base, slope = [], []
    for c in range(4):
        knots = jnp.broadcast_to(transfer[:, c : c + 1], (KNOTS, LANES))
        row = lax.broadcasted_iota(jnp.int32, (KNOTS, LANES), 0)
        after = jnp.where(row == KNOTS - 1, 0.0, pltpu.roll(knots, KNOTS - 1, 0))
        step = after - knots
        base.append((knots[:8], knots[8:]))
        slope.append((step[:8], step[8:]))
    return base, slope


def shade(src, p, j, carry, lookup, tile):
    red, green, blue, remaining = carry
    base, slope = lookup
    f = src[p, rows_at(j), :]
    depth = src[p + 1, rows_at(j), :] - src[p - 1, rows_at(j), :]
    row = src[p, rows_at(j, 1), :] - src[p, rows_at(j, -1), :]
    right = jnp.where(tile.at_last, f, pltpu.roll(f, LANES - 1, 1))
    left = jnp.where(tile.at_first, f, pltpu.roll(f, 1, 1))
    col = right - left
    square = depth * depth + row * row + col * col + 1.0
    gain = 1.0 - AMBIENT
    along = jnp.abs(0.64 * gain * depth + 0.6 * gain * row + 0.48 * gain * col)
    shading = AMBIENT + along * lax.rsqrt(square)
    position = f * ((KNOTS - 1) / UPPER_DENSITY)
    k = position.astype(jnp.int32)
    frac = position - k.astype(jnp.float32)
    high = k >= 8
    k = jnp.bitwise_and(k, 7)
    mixed = [pick(base[c], k, high) + frac * pick(slope[c], k, high) for c in range(4)]
    kept = jnp.exp(mixed[3] * (-OPTICAL_DEPTH / (DEEP * BLOCKS)))
    weight = remaining * (1.0 - kept) * shading
    return (
        red + weight * mixed[0],
        green + weight * mixed[1],
        blue + weight * mixed[2],
        remaining * kept,
    )


def inner_kernel(mine, knots, out, fa, fb, fluxes, sums):
    tile = Tile()
    zero = jnp.zeros((8, LANES), jnp.float32)
    is_first = tile.block == 0

    def plane_of(i, p):
        return [mine[i, p, 8 * j : 8 * j + 8, :] for j in range(TILES)]

    def fill(i, carry):
        for p in range(PLANES):
            put(fa, FRONT + PLANES * i + p, plane_of(i, p))
        return carry

    lax.fori_loop(0, GROUP, fill, 0)

    @pl.when(is_first)
    def _():
        for i in range(HALO):
            put(fa, FRONT - 1 - i, plane_of(i // 2, i % 2))

    src, dst = fa, fb
    for sweep in range(PASSES):
        lo, hi = FRONT + sweep + 1, FRONT + DEEP - 1 - sweep

        @pl.when(is_first)
        def _(src=src, dst=dst, lo=lo):
            carry = first_flux(src, lo - 5)
            for u in range(4):
                p = lo - 4 + u
                carry = diffuse(src, p, dst, p, fluxes, u, carry, tile)

        count = hi - lo
        unroll = 6 if count % 6 == 0 else UNROLL

        def step(i, carry, src=src, dst=dst, lo=lo, unroll=unroll):
            for u in range(unroll):
                p = lo + unroll * i + u
                carry = diffuse(src, p, dst, p, fluxes, u, carry, tile)
            return carry

        whole = count // unroll
        carry = lax.fori_loop(0, whole, step, first_flux(src, lo - 1))
        for u in range(count - unroll * whole):
            p = lo + unroll * whole + u
            carry = diffuse(src, p, dst, p, fluxes, u, carry, tile)
        for i in range(2):
            for j in range(TILES):
                out[2 * sweep + i, 8 * j : 8 * j + 8, :] = dst[hi - 2 + i, rows_at(j), :]
        src, dst = dst, src

    lookup = tables(knots)
    start = (zero, zero, zero, zero + 1.0)

    def rows(j):
        return pl.ds(pl.multiple_of(8 * j, 8), 8)

    @pl.when(is_first)
    def _():
        def shaded(j, unused):
            carry = start
            for u in range(HALO):
                carry = shade(src, FRONT + u, j, carry, lookup, tile)
            for c in range(4):
                sums[c, rows(j), :] = carry[c]
            return unused

        lax.fori_loop(0, TILES, shaded, 0)

    @pl.when(jnp.logical_not(is_first))
    def _():
        for c in range(4):
            for j in range(TILES):
                sums[c, 8 * j : 8 * j + 8, :] = start[c]

    def shaded(j, unused):
        def planes(i, carry):
            for u in range(SHADED):
                p = FRONT + HALO + SHADED * i + u
                carry = shade(src, p, j, carry, lookup, tile)
            return carry

        carry = tuple(sums[c, rows(j), :] for c in range(4))
        carry = lax.fori_loop(0, (DEEP - 2 * HALO) // SHADED, planes, carry)
        for c in range(4):
            out[2 * PASSES + c, rows(j), :] = carry[c]
        return unused

    lax.fori_loop(0, TILES, shaded, 0)


def outer_kernel(tail, after, inner, knots, out, fa, fb, fluxes):
    tile = Tile()
    lookup = tables(knots)
    is_last = tile.block == BLOCKS - 1

    def fill(to, source, i):
        put(fa, to, [source[i // 2, i % 2, 8 * j : 8 * j + 8, :] for j in range(TILES)])

    near = HALO // PLANES
    for i in range(2):
        fill(i, tail, 2 * near - 2 + i)

    @pl.when(jnp.logical_not(is_last))
    def _():
        for i in range(2 * HALO):
            fill(2 + i, after, i)

    @pl.when(is_last)
    def _():
        for i in range(2 * HALO):
            fill(2 + i, tail, max(HALO - 1 - i, 0))

    src, dst = fa, fb
    for sweep in range(PASSES):
        carry = first_flux(src, 0)
        for i in range(2 * HALO):
            carry = diffuse(src, i + 1, dst, i + 2, fluxes, i, carry, tile)
        for i in range(2):
            rest = [inner[2 * sweep + i, 8 * j : 8 * j + 8, :] for j in range(TILES)]
            put(dst, i, rest)
        src, dst = dst, src

    lane = lane_index()
    for j in range(TILES):
        sums = tuple(inner[2 * PASSES + c, 8 * j : 8 * j + 8, :] for c in range(4))
        for i in range(2 * HALO):
            if i == HALO:
                own = sums
            sums = shade(src, i + 1, j, sums, lookup, tile)
        sums = [jnp.where(is_last, own[c], sums[c]) for c in range(4)]
        for k in range(SEGS):
            value = None
            for c in range(4):
                by = TILE * c - WIDE * k - HALO - tile.start + LANES * 2
                moved = pltpu.roll(sums[c], lax.rem(by, LANES), 1)
                value = moved if value is None else jnp.where(lane >= TILE * c, moved, value)
            first = SEG_ROWS * k + 8 * j - HALO
            lo, hi = max(first, 0), min(first + 8, BAND)
            if lo < hi:
                out[lo:hi, :] = value[lo - first : hi - first]


def gather_kernel(parts, out):
    lane = lane_index(GROUP)
    total = jnp.zeros((GROUP, LANES), jnp.float32)
    remaining = jnp.ones((GROUP, LANES), jnp.float32)
    for b in range(BLOCKS):
        v = parts[GROUP * b : GROUP * (b + 1)]
        kept = v
        for c in range(3):
            kept = jnp.where(
                jnp.logical_and(lane >= TILE * c, lane < TILE * (c + 1)),
                pltpu.roll(v, TILE * (c + 1), 1),
                kept,
            )
        total = total + remaining * v
        remaining = remaining * kept
    total = jnp.where(lane >= 3 * TILE, 1.0 - remaining, total)
    turned = [total] + [pltpu.roll(total, TILE * s, 1) for s in range(1, 4)]
    for c in range(4):
        for t in range(GROUP):
            m = t % 4
            out[c, :, TILE * t : TILE * (t + 1)] = turned[(m - c) % 4][
                t : t + 1, TILE * m : TILE * (m + 1)
            ]


def call(kernel, shape, scratch, *operands, **options):
    spec = pl.BlockSpec(memory_space=VMEM)
    operands = [pltpu.with_memory_space_constraint(x, VMEM) for x in operands]
    return pl.pallas_call(
        kernel,
        out_shape=VMEM(shape, jnp.float32),
        in_specs=[spec] * len(operands),
        out_specs=spec,
        scratch_shapes=[VMEM(s, jnp.float32) for s in scratch],
        name=kernel.__name__,
        **options,
    )(*operands)


def shifted(value, axis, by):
    size = lax.axis_size(axis)
    pairs = [(i, i + by) for i in range(size) if 0 <= i + by < size]
    return lax.ppermute(value, axis, pairs)


def per_device(density, transfer_table):
    edge = VMEM((PLANES, 8, COLS), jnp.float32)
    first, last = pl.pallas_call(
        slice_kernel,
        out_shape=[edge, edge],
        in_specs=[pl.BlockSpec(memory_space=pl.ANY)],
        out_specs=[pl.BlockSpec(memory_space=VMEM)] * 2,
        scratch_shapes=[pltpu.SemaphoreType.DMA((2,))],
        name="slice_kernel",
    )(density)
    above = shifted(last, "rows", 1)
    below = shifted(first, "rows", -1)
    chunks = (GROUP, PLANES, SEG_ROWS, LANES)
    cut = pl.pallas_call(
        pack_kernel,
        out_shape=VMEM(chunks, jnp.float32),
        in_specs=[pl.BlockSpec(memory_space=pl.ANY)],
        out_specs=pl.BlockSpec(memory_space=VMEM),
        scratch_shapes=[
            VMEM((PLANES, BAND, COLS), jnp.float32),
            VMEM((PLANES, SEGS * SEG_ROWS, COLS), jnp.float32),
            pltpu.SemaphoreType.DMA((PLANES, PARTS)),
        ],
        name="pack_kernel",
    )(density)
    sent = call(
        halo_kernel,
        chunks,
        [(PLANES, 8, COLS)],
        cut,
        first,
        last,
        above,
        below,
        input_output_aliases={0: 0},
    )
    groups = [[GROUP * b + i for i in range(GROUP)] for b in range(BLOCKS)]
    mine = lax.all_to_all(sent, "depth", 0, 0, axis_index_groups=groups, tiled=True)
    near = HALO // PLANES
    tail = mine[GROUP - near :]
    after = shifted(mine[: 2 * near], "depth", -GROUP)
    knots = transfer_table.T
    field = (FRONT + DEEP, TALL, LANES)
    inner = call(
        inner_kernel,
        (2 * PASSES + 4, SEG_ROWS, LANES),
        [field, field, (UNROLL, TALL, LANES), (4, SEG_ROWS, LANES)],
        mine,
        knots,
    )
    few = (2 * HALO + 2, TALL, LANES)
    partial = call(
        outer_kernel,
        (BAND, LANES),
        [few, few, (2 * HALO, TALL, LANES)],
        tail,
        after,
        inner,
        knots,
    )
    parts = lax.all_to_all(partial, "depth", 0, 0, tiled=True)
    return call(gather_kernel, (4, 1, COLS), [], parts)


def solution(mesh):
    placed = (P("depth", "rows", None), P())
    return jax.shard_map(
        per_device,
        mesh=mesh,
        in_specs=placed,
        out_specs=P(None, ("rows", "depth"), None),
        check_vma=False,
    )
```

```python
import jax
import jax.numpy as jnp
from jax import lax
from jax.experimental import pallas as pl
from jax.experimental.pallas import tpu as pltpu
from jax.sharding import PartitionSpec as P


PASSES = 3
KNOTS = 16
TIME_STEP = 0.15
OPTICAL_DEPTH = 3.0
UPPER_DENSITY = 6.0
AMBIENT = 0.35

GROUP = 16
BLOCKS = 8
HALO = 4
BAND = 128
COLS = 512
TILE = COLS // GROUP
WIDE = TILE + 2 * HALO
SEGS = 3
SEG_ROWS = 48
TILES = SEG_ROWS // 8
PLANES = 2
DEEP = GROUP * PLANES
LANES = 128
TOP = 8
TALL = SEG_ROWS + 2 * TOP
FRONT = HALO
PARTS = 4
UNROLL = 7
SHADED = 8
VMEM = pltpu.VMEM


def lane_index(rows=8):
    return lax.broadcasted_iota(jnp.int32, (rows, LANES), 1)


def window_masks():
    lane = lane_index()
    segment, left, right = [], [], []
    for m in range(4):
        local = (lane - (TILE * m - HALO)) % LANES
        segment.append([(local >= WIDE * k) & (local < WIDE * (k + 1)) for k in range(SEGS)])
        column = local % WIDE
        left.append(column < HALO)
        right.append(column >= WIDE - HALO)
    return segment, left, right


def windows(tiles, joined, left, right):
    for t in range(GROUP):
        q, m = divmod(t, 4)
        value = joined(tiles, q, m)
        if m == 0 and q > 0:
            value = jnp.where(left[m], joined(tiles, q - 1, m), value)
        if m == 3 and q < 3:
            value = jnp.where(right[m], joined(tiles, q + 1, m), value)
        yield t, m, value


def slice_kernel(density, out, sems):
    band = lax.axis_index("rows")
    copies = []
    for to in range(out.shape[0]):
        top = (band > to) | ((band == 0) & (to == 0))
        row = pl.multiple_of(jnp.where(top, 0, BAND - 8), 8)
        source = density.at[:, pl.ds(row, 8), :]
        copies.append(pltpu.make_async_copy(source, out.at[to], sems.at[to]))
    for copy in copies:
        copy.start()
    for copy in copies:
        copy.wait()


def pack_kernel(density, out, own, ext, sems):
    rows = SEGS * SEG_ROWS
    part = BAND // PARTS
    copies = []
    for p in range(PLANES):
        for i in range(PARTS):
            at = pl.ds(part * i, part)
            copies.append(
                pltpu.make_async_copy(density.at[p, at, :], own.at[p, at, :], sems.at[p, i])
            )
    for copy in copies:
        copy.start()
    for p in range(PLANES):
        ext[p, :8, :] = jnp.zeros((8, COLS), jnp.float32)
        ext[p, rows - 16 :, :] = jnp.zeros((16, COLS), jnp.float32)
    segment, left, right = window_masks()

    def joined(rolled, q, m):
        rest = jnp.where(segment[m][1], rolled[1][q], rolled[2][q])
        return jnp.where(segment[m][0], rolled[0][q], rest)

    def step(j, p):
        row = pl.multiple_of(8 * j, 8)
        rolled = []
        for k in range(SEGS):
            start = pl.multiple_of(row + SEG_ROWS * k, 8)
            tiles = [ext[p, pl.ds(start, 8), LANES * q : LANES * (q + 1)] for q in range(4)]
            rolled.append([pltpu.roll(x, WIDE * k, 1) if k else x for x in tiles])
        for t, m, value in windows(rolled, joined, left, right):
            out[t, p, pl.ds(row, 8), :] = value
        return p

    for p in range(PLANES):
        for copy in copies[PARTS * p : PARTS * (p + 1)]:
            copy.wait()
        ext[p, HALO : HALO + BAND, :] = own[p]
        for j in range(TILES):
            step(j, p)


def halo_kernel(sent, strips, out, edge):
    band = lax.axis_index("rows")
    bands = lax.axis_size("rows")

    @pl.when(band > 0)
    def _():
        above = strips.at[jnp.maximum(band - 1, 0)]
        for p in range(PLANES):
            edge[p, 0:HALO, :] = above[p, 8 - HALO : 8, :]

    @pl.when(band == 0)
    def _():
        for p in range(PLANES):
            for i in range(HALO):
                edge[p, HALO - 1 - i : HALO - i, :] = strips[0, p, i : i + 1, :]

    @pl.when(band < bands - 1)
    def _():
        below = strips.at[jnp.minimum(band + 1, bands - 1)]
        for p in range(PLANES):
            edge[p, HALO : 2 * HALO, :] = below[p, 0:HALO, :]

    @pl.when(band == bands - 1)
    def _():
        for p in range(PLANES):
            for i in range(HALO):
                edge[p, HALO + i : HALO + i + 1, :] = strips[strips.shape[0] - 1, p, 7 - i : 8 - i, :]

    segment, left, right = window_masks()
    row = lax.broadcasted_iota(jnp.int32, (8, LANES), 0)
    places = ((0, 0, row < HALO), (2, SEG_ROWS - 16, row >= HALO))

    def joined(rolled, q, m):
        return rolled[q]

    for p in range(PLANES):
        tiles = [edge[p, :, LANES * q : LANES * (q + 1)] for q in range(4)]
        for k, at, rows in places:
            rolled = [pltpu.roll(x, WIDE * k, 1) for x in tiles] if k else tiles
            for t, m, value in windows(rolled, joined, left, right):
                here = sent[t, p, at : at + 8, :]
                out[t, p, at : at + 8, :] = jnp.where(rows & segment[m][k], value, here)


def flux(change):
    return change / (1.0 + change * change)


def rows_at(j, by=0):
    if isinstance(j, int):
        return slice(TOP + 8 * j + by, TOP + 8 * j + by + 8)
    return pl.ds(pl.multiple_of(8 * j, 8) + TOP + by, 8)


def put(ref, p, tiles):
    for j in range(TILES):
        ref[p, rows_at(j), :] = tiles[j]
    ref[p, TOP - 1 : TOP, :] = pltpu.roll(tiles[-1], WIDE, 1)[7:8]
    ref[p, TOP + SEG_ROWS : TOP + SEG_ROWS + 1, :] = pltpu.roll(tiles[0], LANES - WIDE, 1)[0:1]


def take(ref, p, by=0):
    return [ref[p, rows_at(j, by), :] for j in range(TILES)]


class Tile:
    def __init__(self):
        self.block = lax.axis_index("depth") // GROUP
        tile = lax.axis_index("depth") % GROUP
        self.start = TILE * (tile % 4) - HALO
        local = (lane_index() - self.start + LANES) % LANES
        column = local % WIDE
        first, last = tile == 0, tile == GROUP - 1
        self.at_first = jnp.logical_and(column == HALO, first)
        self.at_last = jnp.logical_and(column == HALO + TILE - 1, last)
        self.open_face = jnp.where(
            jnp.logical_or(self.at_last, jnp.logical_and(column == HALO - 1, first)), 0.0, 1.0
        )


def diffuse(src, p, dst, to, fluxes, slot, flux_nearer, tile):
    f = take(src, p)
    below = take(src, p, 1)
    deeper = take(src, p + 1)
    flux_deeper = [flux(deeper[j] - f[j]) for j in range(TILES)]
    row = [flux(below[j] - f[j]) for j in range(TILES)]
    for j in range(TILES):
        fluxes[slot, rows_at(j), :] = row[j]
    fluxes[slot, TOP - 1 : TOP, :] = pltpu.roll(row[-1], WIDE, 1)[7:8]
    row_prev = take(fluxes, slot, -1)
    new = []
    for j in range(TILES):
        col = flux((pltpu.roll(f[j], LANES - 1, 1) - f[j]) * tile.open_face)
        total = flux_deeper[j] - flux_nearer[j]
        total = total + (row[j] - row_prev[j])
        total = total + (col - pltpu.roll(col, 1, 1))
        new.append(f[j] + TIME_STEP * total)
    put(dst, to, new)
    return flux_deeper


def first_flux(src, p):
    here, deeper = take(src, p), take(src, p + 1)
    return [flux(deeper[j] - here[j]) for j in range(TILES)]


ALONG_ROWS = lax.GatherDimensionNumbers(
    offset_dims=(),
    collapsed_slice_dims=(0,),
    start_index_map=(0,),
    operand_batching_dims=(1,),
    start_indices_batching_dims=(1,),
)


def along_rows(x, k):
    return lax.gather(
        x, k[..., None], ALONG_ROWS, (1, 1), mode=lax.GatherScatterMode.PROMISE_IN_BOUNDS
    )


def pick(parts, k, high):
    return jnp.where(high, along_rows(parts[1], k), along_rows(parts[0], k))


def tables(transfer):
    base, slope = [], []
    for c in range(4):
        knots = jnp.broadcast_to(transfer[:, c : c + 1], (KNOTS, LANES))
        row = lax.broadcasted_iota(jnp.int32, (KNOTS, LANES), 0)
        after = jnp.where(row == KNOTS - 1, 0.0, pltpu.roll(knots, KNOTS - 1, 0))
        step = after - knots
        base.append((knots[:8], knots[8:]))
        slope.append((step[:8], step[8:]))
    return base, slope


def shade(src, p, j, carry, lookup, tile):
    red, green, blue, remaining = carry
    base, slope = lookup
    f = src[p, rows_at(j), :]
    depth = src[p + 1, rows_at(j), :] - src[p - 1, rows_at(j), :]
    row = src[p, rows_at(j, 1), :] - src[p, rows_at(j, -1), :]
    right = jnp.where(tile.at_last, f, pltpu.roll(f, LANES - 1, 1))
    left = jnp.where(tile.at_first, f, pltpu.roll(f, 1, 1))
    col = right - left
    square = depth * depth + row * row + col * col + 1.0
    gain = 1.0 - AMBIENT
    along = jnp.abs(0.64 * gain * depth + 0.6 * gain * row + 0.48 * gain * col)
    shading = AMBIENT + along * lax.rsqrt(square)
    position = f * ((KNOTS - 1) / UPPER_DENSITY)
    k = position.astype(jnp.int32)
    frac = position - k.astype(jnp.float32)
    high = k >= 8
    k = jnp.bitwise_and(k, 7)
    mixed = [pick(base[c], k, high) + frac * pick(slope[c], k, high) for c in range(4)]
    kept = jnp.exp(mixed[3] * (-OPTICAL_DEPTH / (DEEP * BLOCKS)))
    weight = remaining * (1.0 - kept) * shading
    return (
        red + weight * mixed[0],
        green + weight * mixed[1],
        blue + weight * mixed[2],
        remaining * kept,
    )


def inner_kernel(mine, knots, out, fa, fb, fluxes, sums):
    tile = Tile()
    zero = jnp.zeros((8, LANES), jnp.float32)
    is_first = tile.block == 0

    def plane_of(i, p):
        return [mine[i, p, 8 * j : 8 * j + 8, :] for j in range(TILES)]

    def fill(i, carry):
        for p in range(PLANES):
            put(fa, FRONT + PLANES * i + p, plane_of(i, p))
        return carry

    lax.fori_loop(0, GROUP, fill, 0)

    @pl.when(is_first)
    def _():
        for i in range(HALO):
            put(fa, FRONT - 1 - i, plane_of(i // 2, i % 2))

    src, dst = fa, fb
    for sweep in range(PASSES):
        lo, hi = FRONT + sweep + 1, FRONT + DEEP - 1 - sweep

        @pl.when(is_first)
        def _(src=src, dst=dst, lo=lo):
            carry = first_flux(src, lo - 5)
            for u in range(4):
                p = lo - 4 + u
                carry = diffuse(src, p, dst, p, fluxes, u, carry, tile)

        count = hi - lo
        unroll = 6 if count % 6 == 0 else UNROLL

        def step(i, carry, src=src, dst=dst, lo=lo, unroll=unroll):
            for u in range(unroll):
                p = lo + unroll * i + u
                carry = diffuse(src, p, dst, p, fluxes, u, carry, tile)
            return carry

        whole = count // unroll
        carry = lax.fori_loop(0, whole, step, first_flux(src, lo - 1))
        for u in range(count - unroll * whole):
            p = lo + unroll * whole + u
            carry = diffuse(src, p, dst, p, fluxes, u, carry, tile)
        for i in range(2):
            for j in range(TILES):
                out[2 * sweep + i, 8 * j : 8 * j + 8, :] = dst[hi - 2 + i, rows_at(j), :]
        src, dst = dst, src

    lookup = tables(knots)
    start = (zero, zero, zero, zero + 1.0)

    def rows(j):
        return pl.ds(pl.multiple_of(8 * j, 8), 8)

    @pl.when(is_first)
    def _():
        def shaded(j, unused):
            carry = start
            for u in range(HALO):
                carry = shade(src, FRONT + u, j, carry, lookup, tile)
            for c in range(4):
                sums[c, rows(j), :] = carry[c]
            return unused

        lax.fori_loop(0, TILES, shaded, 0)

    @pl.when(jnp.logical_not(is_first))
    def _():
        for c in range(4):
            for j in range(TILES):
                sums[c, 8 * j : 8 * j + 8, :] = start[c]

    def shaded(j, unused):
        def planes(i, carry):
            for u in range(SHADED):
                p = FRONT + HALO + SHADED * i + u
                carry = shade(src, p, j, carry, lookup, tile)
            return carry

        carry = tuple(sums[c, rows(j), :] for c in range(4))
        carry = lax.fori_loop(0, (DEEP - 2 * HALO) // SHADED, planes, carry)
        for c in range(4):
            out[2 * PASSES + c, rows(j), :] = carry[c]
        return unused

    lax.fori_loop(0, TILES, shaded, 0)


def outer_kernel(tail, after, inner, knots, out, fa, fb, fluxes):
    tile = Tile()
    lookup = tables(knots)
    is_last = tile.block == BLOCKS - 1

    def fill(to, source, i):
        put(fa, to, [source[i // 2, i % 2, 8 * j : 8 * j + 8, :] for j in range(TILES)])

    near = HALO // PLANES
    for i in range(2):
        fill(i, tail, 2 * near - 2 + i)

    @pl.when(jnp.logical_not(is_last))
    def _():
        for i in range(2 * HALO):
            fill(2 + i, after, i)

    @pl.when(is_last)
    def _():
        for i in range(2 * HALO):
            fill(2 + i, tail, max(HALO - 1 - i, 0))

    src, dst = fa, fb
    for sweep in range(PASSES):
        carry = first_flux(src, 0)
        for i in range(2 * HALO):
            carry = diffuse(src, i + 1, dst, i + 2, fluxes, i, carry, tile)
        for i in range(2):
            rest = [inner[2 * sweep + i, 8 * j : 8 * j + 8, :] for j in range(TILES)]
            put(dst, i, rest)
        src, dst = dst, src

    lane = lane_index()
    for j in range(TILES):
        sums = tuple(inner[2 * PASSES + c, 8 * j : 8 * j + 8, :] for c in range(4))
        for i in range(2 * HALO):
            if i == HALO:
                own = sums
            sums = shade(src, i + 1, j, sums, lookup, tile)
        sums = [jnp.where(is_last, own[c], sums[c]) for c in range(4)]
        for k in range(SEGS):
            value = None
            for c in range(4):
                by = TILE * c - WIDE * k - HALO - tile.start + LANES * 2
                moved = pltpu.roll(sums[c], lax.rem(by, LANES), 1)
                value = moved if value is None else jnp.where(lane >= TILE * c, moved, value)
            first = SEG_ROWS * k + 8 * j - HALO
            lo, hi = max(first, 0), min(first + 8, BAND)
            if lo < hi:
                out[lo:hi, :] = value[lo - first : hi - first]


def gather_kernel(parts, out):
    lane = lane_index(GROUP)
    total = jnp.zeros((GROUP, LANES), jnp.float32)
    remaining = jnp.ones((GROUP, LANES), jnp.float32)
    for b in range(BLOCKS):
        v = parts[GROUP * b : GROUP * (b + 1)]
        kept = v
        for c in range(3):
            kept = jnp.where(
                jnp.logical_and(lane >= TILE * c, lane < TILE * (c + 1)),
                pltpu.roll(v, TILE * (c + 1), 1),
                kept,
            )
        total = total + remaining * v
        remaining = remaining * kept
    total = jnp.where(lane >= 3 * TILE, 1.0 - remaining, total)
    turned = [total] + [pltpu.roll(total, TILE * s, 1) for s in range(1, 4)]
    for c in range(4):
        for t in range(GROUP):
            m = t % 4
            out[c, :, TILE * t : TILE * (t + 1)] = turned[(m - c) % 4][
                t : t + 1, TILE * m : TILE * (m + 1)
            ]


def call(kernel, shape, scratch, *operands, **options):
    spec = pl.BlockSpec(memory_space=VMEM)
    operands = [pltpu.with_memory_space_constraint(x, VMEM) for x in operands]
    return pl.pallas_call(
        kernel,
        out_shape=VMEM(shape, jnp.float32),
        in_specs=[spec] * len(operands),
        out_specs=spec,
        scratch_shapes=[VMEM(s, jnp.float32) for s in scratch],
        name=kernel.__name__,
        **options,
    )(*operands)


def shifted(value, axis, by):
    size = lax.axis_size(axis)
    pairs = [(i, i + by) for i in range(size) if 0 <= i + by < size]
    return lax.ppermute(value, axis, pairs)


def per_device(density, transfer_table):
    bands = lax.axis_size("rows")
    strips = pl.pallas_call(
        slice_kernel,
        out_shape=jax.ShapeDtypeStruct((bands, PLANES, 8, COLS), jnp.float32),
        in_specs=[pl.BlockSpec(memory_space=pl.ANY)],
        out_specs=pl.BlockSpec(memory_space=pl.ANY),
        scratch_shapes=[pltpu.SemaphoreType.DMA((bands,))],
        name="slice_kernel",
    )(density)
    strips = lax.all_to_all(strips, "rows", 0, 0, tiled=True)
    chunks = (GROUP, PLANES, SEG_ROWS, LANES)
    cut = pl.pallas_call(
        pack_kernel,
        out_shape=VMEM(chunks, jnp.float32),
        in_specs=[pl.BlockSpec(memory_space=pl.ANY)],
        out_specs=pl.BlockSpec(memory_space=VMEM),
        scratch_shapes=[
            VMEM((PLANES, BAND, COLS), jnp.float32),
            VMEM((PLANES, SEGS * SEG_ROWS, COLS), jnp.float32),
            pltpu.SemaphoreType.DMA((PLANES, PARTS)),
        ],
        name="pack_kernel",
    )(density)
    sent = call(
        halo_kernel,
        chunks,
        [(PLANES, 8, COLS)],
        cut,
        strips,
        input_output_aliases={0: 0},
    )
    groups = [[GROUP * b + i for i in range(GROUP)] for b in range(BLOCKS)]
    mine = lax.all_to_all(sent, "depth", 0, 0, axis_index_groups=groups, tiled=True)
    near = HALO // PLANES
    tail = mine[GROUP - near :]
    after = shifted(mine[: 2 * near], "depth", -GROUP)
    knots = transfer_table.T
    field = (FRONT + DEEP, TALL, LANES)
    inner = call(
        inner_kernel,
        (2 * PASSES + 4, SEG_ROWS, LANES),
        [field, field, (UNROLL, TALL, LANES), (4, SEG_ROWS, LANES)],
        mine,
        knots,
    )
    few = (2 * HALO + 2, TALL, LANES)
    partial = call(
        outer_kernel,
        (BAND, LANES),
        [few, few, (2 * HALO, TALL, LANES)],
        tail,
        after,
        inner,
        knots,
    )
    parts = lax.all_to_all(partial, "depth", 0, 0, tiled=True)
    return call(gather_kernel, (4, 1, COLS), [], parts)


def solution(mesh):
    placed = (P("depth", "rows", None), P())
    return jax.shard_map(
        per_device,
        mesh=mesh,
        in_specs=placed,
        out_specs=P(None, ("rows", "depth"), None),
        check_vma=False,
    )
```

```python
import jax
import jax.numpy as jnp
from jax import lax
from jax.experimental import pallas as pl
from jax.experimental.pallas import tpu as pltpu
from jax.sharding import PartitionSpec as P


PASSES = 3
KNOTS = 16
TIME_STEP = 0.15
OPTICAL_DEPTH = 3.0
UPPER_DENSITY = 6.0
AMBIENT = 0.35

GROUP = 16
BLOCKS = 8
HALO = 4
BAND = 128
COLS = 512
TILE = COLS // GROUP
WIDE = TILE + 2 * HALO
SEGS = 3
SEG_ROWS = 48
TILES = SEG_ROWS // 8
PLANES = 2
DEEP = GROUP * PLANES
LANES = 128
TOP = 8
TALL = SEG_ROWS + 2 * TOP
FRONT = HALO
PARTS = 4
UNROLL = 7
SHADED = 8
VMEM = pltpu.VMEM


def lane_index(rows=8):
    return lax.broadcasted_iota(jnp.int32, (rows, LANES), 1)


def window_masks():
    lane = lane_index()
    segment, left, right = [], [], []
    for m in range(4):
        local = (lane - (TILE * m - HALO)) % LANES
        segment.append([(local >= WIDE * k) & (local < WIDE * (k + 1)) for k in range(SEGS)])
        column = local % WIDE
        left.append(column < HALO)
        right.append(column >= WIDE - HALO)
    return segment, left, right


def windows(tiles, joined, left, right):
    for t in range(GROUP):
        q, m = divmod(t, 4)
        value = joined(tiles, q, m)
        if m == 0 and q > 0:
            value = jnp.where(left[m], joined(tiles, q - 1, m), value)
        if m == 3 and q < 3:
            value = jnp.where(right[m], joined(tiles, q + 1, m), value)
        yield t, m, value


def slice_kernel(density, one, two, sems):
    even = lax.axis_index("rows") % 2 == 0
    rows = (jnp.where(even, BAND - 8, 0), jnp.where(even, 0, BAND - 8))
    copies = []
    for i, (row, to) in enumerate(zip(rows, (one, two))):
        source = density.at[:, pl.ds(pl.multiple_of(row, 8), 8), :]
        copies.append(pltpu.make_async_copy(source, to, sems.at[i]))
    for copy in copies:
        copy.start()
    for copy in copies:
        copy.wait()


def pack_kernel(density, out, own, ext, sems):
    rows = SEGS * SEG_ROWS
    part = BAND // PARTS
    copies = []
    for p in range(PLANES):
        for i in range(PARTS):
            at = pl.ds(part * i, part)
            copies.append(
                pltpu.make_async_copy(density.at[p, at, :], own.at[p, at, :], sems.at[p, i])
            )
    for copy in copies:
        copy.start()
    for p in range(PLANES):
        ext[p, :8, :] = jnp.zeros((8, COLS), jnp.float32)
        ext[p, rows - 16 :, :] = jnp.zeros((16, COLS), jnp.float32)
    segment, left, right = window_masks()

    def joined(rolled, q, m):
        rest = jnp.where(segment[m][1], rolled[1][q], rolled[2][q])
        return jnp.where(segment[m][0], rolled[0][q], rest)

    def step(j, p):
        row = pl.multiple_of(8 * j, 8)
        rolled = []
        for k in range(SEGS):
            start = pl.multiple_of(row + SEG_ROWS * k, 8)
            tiles = [ext[p, pl.ds(start, 8), LANES * q : LANES * (q + 1)] for q in range(4)]
            rolled.append([pltpu.roll(x, WIDE * k, 1) if k else x for x in tiles])
        for t, m, value in windows(rolled, joined, left, right):
            out[t, p, pl.ds(row, 8), :] = value
        return p

    for p in range(PLANES):
        for copy in copies[PARTS * p : PARTS * (p + 1)]:
            copy.wait()
        ext[p, HALO : HALO + BAND, :] = own[p]
        for j in range(TILES):
            step(j, p)


def halo_kernel(sent, two, from_one, from_two, out, edge):
    band = lax.axis_index("rows")
    bands = lax.axis_size("rows")
    even = band % 2 == 0

    def above(source):
        for p in range(PLANES):
            edge[p, 0:HALO, :] = source[p, 8 - HALO : 8, :]

    def below(source):
        for p in range(PLANES):
            edge[p, HALO : 2 * HALO, :] = source[p, 0:HALO, :]

    @pl.when(even)
    def _():
        below(from_one)

    @pl.when(jnp.logical_not(even))
    def _():
        above(from_one)

    @pl.when(even & (band > 0))
    def _():
        above(from_two)

    @pl.when(jnp.logical_not(even) & (band < bands - 1))
    def _():
        below(from_two)

    @pl.when(band == 0)
    def _():
        for p in range(PLANES):
            for i in range(HALO):
                edge[p, HALO - 1 - i : HALO - i, :] = two[p, i : i + 1, :]

    @pl.when(band == bands - 1)
    def _():
        for p in range(PLANES):
            for i in range(HALO):
                edge[p, HALO + i : HALO + i + 1, :] = two[p, 7 - i : 8 - i, :]

    segment, left, right = window_masks()
    row = lax.broadcasted_iota(jnp.int32, (8, LANES), 0)
    places = ((0, 0, row < HALO), (2, SEG_ROWS - 16, row >= HALO))

    def joined(rolled, q, m):
        return rolled[q]

    for p in range(PLANES):
        tiles = [edge[p, :, LANES * q : LANES * (q + 1)] for q in range(4)]
        for k, at, rows in places:
            rolled = [pltpu.roll(x, WIDE * k, 1) for x in tiles] if k else tiles
            for t, m, value in windows(rolled, joined, left, right):
                here = sent[t, p, at : at + 8, :]
                out[t, p, at : at + 8, :] = jnp.where(rows & segment[m][k], value, here)


def flux(change):
    return change / (1.0 + change * change)


def rows_at(j, by=0):
    if isinstance(j, int):
        return slice(TOP + 8 * j + by, TOP + 8 * j + by + 8)
    return pl.ds(pl.multiple_of(8 * j, 8) + TOP + by, 8)


def put(ref, p, tiles):
    for j in range(TILES):
        ref[p, rows_at(j), :] = tiles[j]
    ref[p, TOP - 1 : TOP, :] = pltpu.roll(tiles[-1], WIDE, 1)[7:8]
    ref[p, TOP + SEG_ROWS : TOP + SEG_ROWS + 1, :] = pltpu.roll(tiles[0], LANES - WIDE, 1)[0:1]


def take(ref, p, by=0):
    return [ref[p, rows_at(j, by), :] for j in range(TILES)]


class Tile:
    def __init__(self):
        self.block = lax.axis_index("depth") // GROUP
        tile = lax.axis_index("depth") % GROUP
        self.start = TILE * (tile % 4) - HALO
        local = (lane_index() - self.start + LANES) % LANES
        column = local % WIDE
        first, last = tile == 0, tile == GROUP - 1
        self.at_first = jnp.logical_and(column == HALO, first)
        self.at_last = jnp.logical_and(column == HALO + TILE - 1, last)
        self.open_face = jnp.where(
            jnp.logical_or(self.at_last, jnp.logical_and(column == HALO - 1, first)), 0.0, 1.0
        )


def diffuse(src, p, dst, to, fluxes, slot, flux_nearer, tile):
    f = take(src, p)
    below = take(src, p, 1)
    deeper = take(src, p + 1)
    flux_deeper = [flux(deeper[j] - f[j]) for j in range(TILES)]
    row = [flux(below[j] - f[j]) for j in range(TILES)]
    for j in range(TILES):
        fluxes[slot, rows_at(j), :] = row[j]
    fluxes[slot, TOP - 1 : TOP, :] = pltpu.roll(row[-1], WIDE, 1)[7:8]
    row_prev = take(fluxes, slot, -1)
    new = []
    for j in range(TILES):
        col = flux((pltpu.roll(f[j], LANES - 1, 1) - f[j]) * tile.open_face)
        total = flux_deeper[j] - flux_nearer[j]
        total = total + (row[j] - row_prev[j])
        total = total + (col - pltpu.roll(col, 1, 1))
        new.append(f[j] + TIME_STEP * total)
    put(dst, to, new)
    return flux_deeper


def first_flux(src, p):
    here, deeper = take(src, p), take(src, p + 1)
    return [flux(deeper[j] - here[j]) for j in range(TILES)]


ALONG_ROWS = lax.GatherDimensionNumbers(
    offset_dims=(),
    collapsed_slice_dims=(0,),
    start_index_map=(0,),
    operand_batching_dims=(1,),
    start_indices_batching_dims=(1,),
)


def along_rows(x, k):
    return lax.gather(
        x, k[..., None], ALONG_ROWS, (1, 1), mode=lax.GatherScatterMode.PROMISE_IN_BOUNDS
    )


def pick(parts, k, high):
    return jnp.where(high, along_rows(parts[1], k), along_rows(parts[0], k))


def tables(transfer):
    base, slope = [], []
    for c in range(4):
        knots = jnp.broadcast_to(transfer[:, c : c + 1], (KNOTS, LANES))
        row = lax.broadcasted_iota(jnp.int32, (KNOTS, LANES), 0)
        after = jnp.where(row == KNOTS - 1, 0.0, pltpu.roll(knots, KNOTS - 1, 0))
        step = after - knots
        base.append((knots[:8], knots[8:]))
        slope.append((step[:8], step[8:]))
    return base, slope


def shade(src, p, j, carry, lookup, tile):
    red, green, blue, remaining = carry
    base, slope = lookup
    f = src[p, rows_at(j), :]
    depth = src[p + 1, rows_at(j), :] - src[p - 1, rows_at(j), :]
    row = src[p, rows_at(j, 1), :] - src[p, rows_at(j, -1), :]
    right = jnp.where(tile.at_last, f, pltpu.roll(f, LANES - 1, 1))
    left = jnp.where(tile.at_first, f, pltpu.roll(f, 1, 1))
    col = right - left
    square = depth * depth + row * row + col * col + 1.0
    gain = 1.0 - AMBIENT
    along = jnp.abs(0.64 * gain * depth + 0.6 * gain * row + 0.48 * gain * col)
    shading = AMBIENT + along * lax.rsqrt(square)
    position = f * ((KNOTS - 1) / UPPER_DENSITY)
    k = position.astype(jnp.int32)
    frac = position - k.astype(jnp.float32)
    high = k >= 8
    k = jnp.bitwise_and(k, 7)
    mixed = [pick(base[c], k, high) + frac * pick(slope[c], k, high) for c in range(4)]
    kept = jnp.exp(mixed[3] * (-OPTICAL_DEPTH / (DEEP * BLOCKS)))
    weight = remaining * (1.0 - kept) * shading
    return (
        red + weight * mixed[0],
        green + weight * mixed[1],
        blue + weight * mixed[2],
        remaining * kept,
    )


def inner_kernel(mine, knots, out, fa, fb, fluxes, sums):
    tile = Tile()
    zero = jnp.zeros((8, LANES), jnp.float32)
    is_first = tile.block == 0

    def plane_of(i, p):
        return [mine[i, p, 8 * j : 8 * j + 8, :] for j in range(TILES)]

    def fill(i, carry):
        for p in range(PLANES):
            put(fa, FRONT + PLANES * i + p, plane_of(i, p))
        return carry

    lax.fori_loop(0, GROUP, fill, 0)

    @pl.when(is_first)
    def _():
        for i in range(HALO):
            put(fa, FRONT - 1 - i, plane_of(i // 2, i % 2))

    src, dst = fa, fb
    for sweep in range(PASSES):
        lo, hi = FRONT + sweep + 1, FRONT + DEEP - 1 - sweep

        @pl.when(is_first)
        def _(src=src, dst=dst, lo=lo):
            carry = first_flux(src, lo - 5)
            for u in range(4):
                p = lo - 4 + u
                carry = diffuse(src, p, dst, p, fluxes, u, carry, tile)

        count = hi - lo
        unroll = 6 if count % 6 == 0 else UNROLL

        def step(i, carry, src=src, dst=dst, lo=lo, unroll=unroll):
            for u in range(unroll):
                p = lo + unroll * i + u
                carry = diffuse(src, p, dst, p, fluxes, u, carry, tile)
            return carry

        whole = count // unroll
        carry = lax.fori_loop(0, whole, step, first_flux(src, lo - 1))
        for u in range(count - unroll * whole):
            p = lo + unroll * whole + u
            carry = diffuse(src, p, dst, p, fluxes, u, carry, tile)
        for i in range(2):
            for j in range(TILES):
                out[2 * sweep + i, 8 * j : 8 * j + 8, :] = dst[hi - 2 + i, rows_at(j), :]
        src, dst = dst, src

    lookup = tables(knots)
    start = (zero, zero, zero, zero + 1.0)

    def rows(j):
        return pl.ds(pl.multiple_of(8 * j, 8), 8)

    @pl.when(is_first)
    def _():
        def shaded(j, unused):
            carry = start
            for u in range(HALO):
                carry = shade(src, FRONT + u, j, carry, lookup, tile)
            for c in range(4):
                sums[c, rows(j), :] = carry[c]
            return unused

        lax.fori_loop(0, TILES, shaded, 0)

    @pl.when(jnp.logical_not(is_first))
    def _():
        for c in range(4):
            for j in range(TILES):
                sums[c, 8 * j : 8 * j + 8, :] = start[c]

    def shaded(j, unused):
        def planes(i, carry):
            for u in range(SHADED):
                p = FRONT + HALO + SHADED * i + u
                carry = shade(src, p, j, carry, lookup, tile)
            return carry

        carry = tuple(sums[c, rows(j), :] for c in range(4))
        carry = lax.fori_loop(0, (DEEP - 2 * HALO) // SHADED, planes, carry)
        for c in range(4):
            out[2 * PASSES + c, rows(j), :] = carry[c]
        return unused

    lax.fori_loop(0, TILES, shaded, 0)


def outer_kernel(tail, after, inner, knots, out, fa, fb, fluxes):
    tile = Tile()
    lookup = tables(knots)
    is_last = tile.block == BLOCKS - 1

    def fill(to, source, i):
        put(fa, to, [source[i // 2, i % 2, 8 * j : 8 * j + 8, :] for j in range(TILES)])

    near = HALO // PLANES
    for i in range(2):
        fill(i, tail, 2 * near - 2 + i)

    @pl.when(jnp.logical_not(is_last))
    def _():
        for i in range(2 * HALO):
            fill(2 + i, after, i)

    @pl.when(is_last)
    def _():
        for i in range(2 * HALO):
            fill(2 + i, tail, max(HALO - 1 - i, 0))

    src, dst = fa, fb
    for sweep in range(PASSES):
        carry = first_flux(src, 0)
        for i in range(2 * HALO):
            carry = diffuse(src, i + 1, dst, i + 2, fluxes, i, carry, tile)
        for i in range(2):
            rest = [inner[2 * sweep + i, 8 * j : 8 * j + 8, :] for j in range(TILES)]
            put(dst, i, rest)
        src, dst = dst, src

    lane = lane_index()
    for j in range(TILES):
        sums = tuple(inner[2 * PASSES + c, 8 * j : 8 * j + 8, :] for c in range(4))
        for i in range(2 * HALO):
            if i == HALO:
                own = sums
            sums = shade(src, i + 1, j, sums, lookup, tile)
        sums = [jnp.where(is_last, own[c], sums[c]) for c in range(4)]
        for k in range(SEGS):
            value = None
            for c in range(4):
                by = TILE * c - WIDE * k - HALO - tile.start + LANES * 2
                moved = pltpu.roll(sums[c], lax.rem(by, LANES), 1)
                value = moved if value is None else jnp.where(lane >= TILE * c, moved, value)
            first = SEG_ROWS * k + 8 * j - HALO
            lo, hi = max(first, 0), min(first + 8, BAND)
            if lo < hi:
                out[lo:hi, :] = value[lo - first : hi - first]


def gather_kernel(parts, out):
    lane = lane_index(GROUP)
    total = jnp.zeros((GROUP, LANES), jnp.float32)
    remaining = jnp.ones((GROUP, LANES), jnp.float32)
    for b in range(BLOCKS):
        v = parts[GROUP * b : GROUP * (b + 1)]
        kept = v
        for c in range(3):
            kept = jnp.where(
                jnp.logical_and(lane >= TILE * c, lane < TILE * (c + 1)),
                pltpu.roll(v, TILE * (c + 1), 1),
                kept,
            )
        total = total + remaining * v
        remaining = remaining * kept
    total = jnp.where(lane >= 3 * TILE, 1.0 - remaining, total)
    turned = [total] + [pltpu.roll(total, TILE * s, 1) for s in range(1, 4)]
    for c in range(4):
        for t in range(GROUP):
            m = t % 4
            out[c, :, TILE * t : TILE * (t + 1)] = turned[(m - c) % 4][
                t : t + 1, TILE * m : TILE * (m + 1)
            ]


def call(kernel, shape, scratch, *operands, **options):
    spec = pl.BlockSpec(memory_space=VMEM)
    operands = [pltpu.with_memory_space_constraint(x, VMEM) for x in operands]
    return pl.pallas_call(
        kernel,
        out_shape=VMEM(shape, jnp.float32),
        in_specs=[spec] * len(operands),
        out_specs=spec,
        scratch_shapes=[VMEM(s, jnp.float32) for s in scratch],
        **options,
    )(*operands)


def shifted(value, axis, by):
    size = lax.axis_size(axis)
    pairs = [(i, i + by) for i in range(size) if 0 <= i + by < size]
    return lax.ppermute(value, axis, pairs)


def rendered(density, transfer_table):
    bands = lax.axis_size("rows")
    edge = VMEM((PLANES, 8, COLS), jnp.float32)
    one, two = pl.pallas_call(
        slice_kernel,
        out_shape=[edge, edge],
        in_specs=[pl.BlockSpec(memory_space=pl.ANY)],
        out_specs=[pl.BlockSpec(memory_space=VMEM)] * 2,
        scratch_shapes=[pltpu.SemaphoreType.DMA((2,))],
        name="slice_kernel",
    )(density)
    pairs = [(i, i + 1) for i in range(0, bands, 2)]
    from_one = lax.ppermute(one, "rows", pairs + [(b, a) for a, b in pairs])
    pairs = [(i, i + 1) for i in range(1, bands - 1, 2)]
    from_two = lax.ppermute(two, "rows", pairs + [(b, a) for a, b in pairs])
    chunks = (GROUP, PLANES, SEG_ROWS, LANES)
    cut = pl.pallas_call(
        pack_kernel,
        out_shape=VMEM(chunks, jnp.float32),
        in_specs=[pl.BlockSpec(memory_space=pl.ANY)],
        out_specs=pl.BlockSpec(memory_space=VMEM),
        scratch_shapes=[
            VMEM((PLANES, BAND, COLS), jnp.float32),
            VMEM((PLANES, SEGS * SEG_ROWS, COLS), jnp.float32),
            pltpu.SemaphoreType.DMA((PLANES, PARTS)),
        ],
        name="pack_kernel",
    )(density)
    sent = call(
        halo_kernel,
        chunks,
        [(PLANES, 8, COLS)],
        cut,
        two,
        from_one,
        from_two,
        input_output_aliases={0: 0},
    )
    groups = [[GROUP * b + i for i in range(GROUP)] for b in range(BLOCKS)]
    mine = lax.all_to_all(sent, "depth", 0, 0, axis_index_groups=groups, tiled=True)
    near = HALO // PLANES
    tail = mine[GROUP - near :]
    after = shifted(mine[: 2 * near], "depth", -GROUP)
    knots = transfer_table.T
    field = (FRONT + DEEP, TALL, LANES)
    inner = call(
        inner_kernel,
        (2 * PASSES + 4, SEG_ROWS, LANES),
        [field, field, (UNROLL, TALL, LANES), (4, SEG_ROWS, LANES)],
        mine,
        knots,
    )
    few = (2 * HALO + 2, TALL, LANES)
    partial = call(
        outer_kernel,
        (BAND, LANES),
        [few, few, (2 * HALO, TALL, LANES)],
        tail,
        after,
        inner,
        knots,
    )
    parts = lax.all_to_all(partial, "depth", 0, 0, tiled=True)
    return call(gather_kernel, (4, 1, COLS), [], parts)


def solution(mesh):
    placed = (P("depth", "rows", None), P())
    return jax.shard_map(
        rendered,
        mesh=mesh,
        in_specs=placed,
        out_specs=P(None, ("rows", "depth"), None),
        check_vma=False,
    )
```

```python
import jax
import jax.numpy as jnp
from jax import lax
from jax.experimental import pallas as pl
from jax.experimental.pallas import tpu as pltpu
from jax.sharding import PartitionSpec as P


PASSES = 3
KNOTS = 16
TIME_STEP = 0.15
OPTICAL_DEPTH = 3.0
UPPER_DENSITY = 6.0
AMBIENT = 0.35

GROUP = 16
BLOCKS = 8
HALO = 4
BAND = 128
COLS = 512
TILE = COLS // GROUP
WIDE = TILE + 2 * HALO
SEGS = 3
SEG_ROWS = 48
TILES = SEG_ROWS // 8
PLANES = 2
DEEP = GROUP * PLANES
LANES = 128
TOP = 8
TALL = SEG_ROWS + 2 * TOP
FRONT = HALO
PARTS = 4
UNROLL = 7
SHADED = 8
VMEM = pltpu.VMEM


def lane_index(rows=8):
    return lax.broadcasted_iota(jnp.int32, (rows, LANES), 1)


def window_masks():
    lane = lane_index()
    segment, left, right = [], [], []
    for m in range(4):
        local = (lane - (TILE * m - HALO)) % LANES
        segment.append([(local >= WIDE * k) & (local < WIDE * (k + 1)) for k in range(SEGS)])
        column = local % WIDE
        left.append(column < HALO)
        right.append(column >= WIDE - HALO)
    return segment, left, right


def windows(tiles, joined, left, right):
    for t in range(GROUP):
        q, m = divmod(t, 4)
        value = joined(tiles, q, m)
        if m == 0 and q > 0:
            value = jnp.where(left[m], joined(tiles, q - 1, m), value)
        if m == 3 and q < 3:
            value = jnp.where(right[m], joined(tiles, q + 1, m), value)
        yield t, m, value


def slice_kernel(density, one, two, ends, sems):
    even = lax.axis_index("rows") % 2 == 0
    copies = []
    for i, row in enumerate((0, BAND - 8)):
        source = density.at[:, pl.ds(row, 8), :]
        copies.append(pltpu.make_async_copy(source, ends.at[i], sems.at[i]))
    for copy in copies:
        copy.start()
    for copy in copies:
        copy.wait()
    for p in range(PLANES):
        first = ends[0, p, 0:HALO, :]
        last = ends[1, p, 8 - HALO : 8, :]
        one[p] = jnp.where(even, last, first)
        two[p] = jnp.where(even, first, last)


def pack_kernel(density, out, own, ext, sems):
    rows = SEGS * SEG_ROWS
    part = BAND // PARTS
    copies = []
    for p in range(PLANES):
        for i in range(PARTS):
            at = pl.ds(part * i, part)
            copies.append(
                pltpu.make_async_copy(density.at[p, at, :], own.at[p, at, :], sems.at[p, i])
            )
    for copy in copies:
        copy.start()
    for p in range(PLANES):
        ext[p, :8, :] = jnp.zeros((8, COLS), jnp.float32)
        ext[p, rows - 16 :, :] = jnp.zeros((16, COLS), jnp.float32)
    segment, left, right = window_masks()

    def joined(rolled, q, m):
        rest = jnp.where(segment[m][1], rolled[1][q], rolled[2][q])
        return jnp.where(segment[m][0], rolled[0][q], rest)

    def step(j, p):
        row = pl.multiple_of(8 * j, 8)
        rolled = []
        for k in range(SEGS):
            start = pl.multiple_of(row + SEG_ROWS * k, 8)
            tiles = [ext[p, pl.ds(start, 8), LANES * q : LANES * (q + 1)] for q in range(4)]
            rolled.append([pltpu.roll(x, WIDE * k, 1) if k else x for x in tiles])
        for t, m, value in windows(rolled, joined, left, right):
            out[t, p, pl.ds(row, 8), :] = value
        return p

    for p in range(PLANES):
        for copy in copies[PARTS * p : PARTS * (p + 1)]:
            copy.wait()
        ext[p, HALO : HALO + BAND, :] = own[p]
        for j in range(TILES):
            step(j, p)


def halo_kernel(sent, two, from_one, from_two, out, edge):
    band = lax.axis_index("rows")
    bands = lax.axis_size("rows")
    even = band % 2 == 0

    def above(source):
        for p in range(PLANES):
            edge[p, 0:HALO, :] = source[p]

    def below(source):
        for p in range(PLANES):
            edge[p, HALO : 2 * HALO, :] = source[p]

    @pl.when(even)
    def _():
        below(from_one)

    @pl.when(jnp.logical_not(even))
    def _():
        above(from_one)

    @pl.when(even & (band > 0))
    def _():
        above(from_two)

    @pl.when(jnp.logical_not(even) & (band < bands - 1))
    def _():
        below(from_two)

    @pl.when(band == 0)
    def _():
        for p in range(PLANES):
            for i in range(HALO):
                edge[p, HALO - 1 - i : HALO - i, :] = two[p, i : i + 1, :]

    @pl.when(band == bands - 1)
    def _():
        for p in range(PLANES):
            for i in range(HALO):
                edge[p, HALO + i : HALO + i + 1, :] = two[p, HALO - 1 - i : HALO - i, :]

    segment, left, right = window_masks()
    row = lax.broadcasted_iota(jnp.int32, (8, LANES), 0)
    places = ((0, 0, row < HALO), (2, SEG_ROWS - 16, row >= HALO))

    def joined(rolled, q, m):
        return rolled[q]

    for p in range(PLANES):
        tiles = [edge[p, :, LANES * q : LANES * (q + 1)] for q in range(4)]
        for k, at, rows in places:
            rolled = [pltpu.roll(x, WIDE * k, 1) for x in tiles] if k else tiles
            for t, m, value in windows(rolled, joined, left, right):
                here = sent[t, p, at : at + 8, :]
                out[t, p, at : at + 8, :] = jnp.where(rows & segment[m][k], value, here)


def flux(change):
    return change / (1.0 + change * change)


def rows_at(j, by=0):
    if isinstance(j, int):
        return slice(TOP + 8 * j + by, TOP + 8 * j + by + 8)
    return pl.ds(pl.multiple_of(8 * j, 8) + TOP + by, 8)


def put(ref, p, tiles):
    for j in range(TILES):
        ref[p, rows_at(j), :] = tiles[j]
    ref[p, TOP - 1 : TOP, :] = pltpu.roll(tiles[-1], WIDE, 1)[7:8]
    ref[p, TOP + SEG_ROWS : TOP + SEG_ROWS + 1, :] = pltpu.roll(tiles[0], LANES - WIDE, 1)[0:1]


def take(ref, p, by=0):
    return [ref[p, rows_at(j, by), :] for j in range(TILES)]


class Tile:
    def __init__(self):
        self.block = lax.axis_index("depth") // GROUP
        tile = lax.axis_index("depth") % GROUP
        self.start = TILE * (tile % 4) - HALO
        local = (lane_index() - self.start + LANES) % LANES
        column = local % WIDE
        first, last = tile == 0, tile == GROUP - 1
        self.at_first = jnp.logical_and(column == HALO, first)
        self.at_last = jnp.logical_and(column == HALO + TILE - 1, last)
        self.open_face = jnp.where(
            jnp.logical_or(self.at_last, jnp.logical_and(column == HALO - 1, first)), 0.0, 1.0
        )


def diffuse(src, p, dst, to, fluxes, slot, flux_nearer, tile):
    f = take(src, p)
    below = take(src, p, 1)
    deeper = take(src, p + 1)
    flux_deeper = [flux(deeper[j] - f[j]) for j in range(TILES)]
    row = [flux(below[j] - f[j]) for j in range(TILES)]
    for j in range(TILES):
        fluxes[slot, rows_at(j), :] = row[j]
    fluxes[slot, TOP - 1 : TOP, :] = pltpu.roll(row[-1], WIDE, 1)[7:8]
    row_prev = take(fluxes, slot, -1)
    new = []
    for j in range(TILES):
        col = flux((pltpu.roll(f[j], LANES - 1, 1) - f[j]) * tile.open_face)
        total = flux_deeper[j] - flux_nearer[j]
        total = total + (row[j] - row_prev[j])
        total = total + (col - pltpu.roll(col, 1, 1))
        new.append(f[j] + TIME_STEP * total)
    put(dst, to, new)
    return flux_deeper


def first_flux(src, p):
    here, deeper = take(src, p), take(src, p + 1)
    return [flux(deeper[j] - here[j]) for j in range(TILES)]


ALONG_ROWS = lax.GatherDimensionNumbers(
    offset_dims=(),
    collapsed_slice_dims=(0,),
    start_index_map=(0,),
    operand_batching_dims=(1,),
    start_indices_batching_dims=(1,),
)


def along_rows(x, k):
    return lax.gather(
        x, k[..., None], ALONG_ROWS, (1, 1), mode=lax.GatherScatterMode.PROMISE_IN_BOUNDS
    )


def pick(parts, k, high):
    return jnp.where(high, along_rows(parts[1], k), along_rows(parts[0], k))


def tables(transfer):
    base, slope = [], []
    for c in range(4):
        knots = jnp.broadcast_to(transfer[:, c : c + 1], (KNOTS, LANES))
        row = lax.broadcasted_iota(jnp.int32, (KNOTS, LANES), 0)
        after = jnp.where(row == KNOTS - 1, 0.0, pltpu.roll(knots, KNOTS - 1, 0))
        step = after - knots
        base.append((knots[:8], knots[8:]))
        slope.append((step[:8], step[8:]))
    return base, slope


def shade(src, p, j, carry, lookup, tile):
    red, green, blue, remaining = carry
    base, slope = lookup
    f = src[p, rows_at(j), :]
    depth = src[p + 1, rows_at(j), :] - src[p - 1, rows_at(j), :]
    row = src[p, rows_at(j, 1), :] - src[p, rows_at(j, -1), :]
    right = jnp.where(tile.at_last, f, pltpu.roll(f, LANES - 1, 1))
    left = jnp.where(tile.at_first, f, pltpu.roll(f, 1, 1))
    col = right - left
    square = depth * depth + row * row + col * col + 1.0
    gain = 1.0 - AMBIENT
    along = jnp.abs(0.64 * gain * depth + 0.6 * gain * row + 0.48 * gain * col)
    shading = AMBIENT + along * lax.rsqrt(square)
    position = f * ((KNOTS - 1) / UPPER_DENSITY)
    k = position.astype(jnp.int32)
    frac = position - k.astype(jnp.float32)
    high = k >= 8
    k = jnp.bitwise_and(k, 7)
    mixed = [pick(base[c], k, high) + frac * pick(slope[c], k, high) for c in range(4)]
    kept = jnp.exp(mixed[3] * (-OPTICAL_DEPTH / (DEEP * BLOCKS)))
    weight = remaining * (1.0 - kept) * shading
    return (
        red + weight * mixed[0],
        green + weight * mixed[1],
        blue + weight * mixed[2],
        remaining * kept,
    )


def inner_kernel(mine, knots, out, fa, fb, fluxes, sums):
    tile = Tile()
    zero = jnp.zeros((8, LANES), jnp.float32)
    is_first = tile.block == 0

    def plane_of(i, p):
        return [mine[i, p, 8 * j : 8 * j + 8, :] for j in range(TILES)]

    def fill(i, carry):
        for u in range(4):
            for p in range(PLANES):
                k = 4 * i + u
                put(fa, FRONT + PLANES * k + p, plane_of(k, p))
        return carry

    lax.fori_loop(0, GROUP // 4, fill, 0)

    @pl.when(is_first)
    def _():
        for i in range(HALO):
            put(fa, FRONT - 1 - i, plane_of(i // 2, i % 2))

    src, dst = fa, fb
    for sweep in range(PASSES):
        lo, hi = FRONT + sweep + 1, FRONT + DEEP - 1 - sweep

        @pl.when(is_first)
        def _(src=src, dst=dst, lo=lo):
            carry = first_flux(src, lo - 5)
            for u in range(4):
                p = lo - 4 + u
                carry = diffuse(src, p, dst, p, fluxes, u, carry, tile)

        count = hi - lo
        unroll = 6 if count % 6 == 0 else UNROLL

        def step(i, carry, src=src, dst=dst, lo=lo, unroll=unroll):
            for u in range(unroll):
                p = lo + unroll * i + u
                carry = diffuse(src, p, dst, p, fluxes, u, carry, tile)
            return carry

        whole = count // unroll
        carry = lax.fori_loop(0, whole, step, first_flux(src, lo - 1))
        for u in range(count - unroll * whole):
            p = lo + unroll * whole + u
            carry = diffuse(src, p, dst, p, fluxes, u, carry, tile)
        for i in range(2):
            for j in range(TILES):
                out[2 * sweep + i, 8 * j : 8 * j + 8, :] = dst[hi - 2 + i, rows_at(j), :]
        src, dst = dst, src

    lookup = tables(knots)
    start = (zero, zero, zero, zero + 1.0)

    def rows(j):
        return pl.ds(pl.multiple_of(8 * j, 8), 8)

    @pl.when(is_first)
    def _():
        def shaded(j, unused):
            carry = start
            for u in range(HALO):
                carry = shade(src, FRONT + u, j, carry, lookup, tile)
            for c in range(4):
                sums[c, rows(j), :] = carry[c]
            return unused

        lax.fori_loop(0, TILES, shaded, 0)

    @pl.when(jnp.logical_not(is_first))
    def _():
        for c in range(4):
            for j in range(TILES):
                sums[c, 8 * j : 8 * j + 8, :] = start[c]

    def shaded(j, unused):
        def planes(i, carry):
            for u in range(SHADED):
                p = FRONT + HALO + SHADED * i + u
                carry = shade(src, p, j, carry, lookup, tile)
            return carry

        carry = tuple(sums[c, rows(j), :] for c in range(4))
        carry = lax.fori_loop(0, (DEEP - 2 * HALO) // SHADED, planes, carry)
        for c in range(4):
            out[2 * PASSES + c, rows(j), :] = carry[c]
        return unused

    lax.fori_loop(0, TILES, shaded, 0)


def outer_kernel(tail, after, inner, knots, out, fa, fb, fluxes):
    tile = Tile()
    lookup = tables(knots)
    is_last = tile.block == BLOCKS - 1

    def fill(to, source, i):
        put(fa, to, [source[i // 2, i % 2, 8 * j : 8 * j + 8, :] for j in range(TILES)])

    near = HALO // PLANES
    for i in range(2):
        fill(i, tail, 2 * near - 2 + i)

    @pl.when(jnp.logical_not(is_last))
    def _():
        for i in range(2 * HALO):
            fill(2 + i, after, i)

    @pl.when(is_last)
    def _():
        for i in range(2 * HALO):
            fill(2 + i, tail, max(HALO - 1 - i, 0))

    src, dst = fa, fb
    for sweep in range(PASSES):
        carry = first_flux(src, 0)
        for i in range(2 * HALO):
            carry = diffuse(src, i + 1, dst, i + 2, fluxes, i, carry, tile)
        for i in range(2):
            rest = [inner[2 * sweep + i, 8 * j : 8 * j + 8, :] for j in range(TILES)]
            put(dst, i, rest)
        src, dst = dst, src

    lane = lane_index()
    for j in range(TILES):
        sums = tuple(inner[2 * PASSES + c, 8 * j : 8 * j + 8, :] for c in range(4))
        for i in range(2 * HALO):
            if i == HALO:
                own = sums
            sums = shade(src, i + 1, j, sums, lookup, tile)
        sums = [jnp.where(is_last, own[c], sums[c]) for c in range(4)]
        for k in range(SEGS):
            value = None
            for c in range(4):
                by = TILE * c - WIDE * k - HALO - tile.start + LANES * 2
                moved = pltpu.roll(sums[c], lax.rem(by, LANES), 1)
                value = moved if value is None else jnp.where(lane >= TILE * c, moved, value)
            first = SEG_ROWS * k + 8 * j - HALO
            lo, hi = max(first, 0), min(first + 8, BAND)
            if lo < hi:
                out[lo:hi, :] = value[lo - first : hi - first]


def gather_kernel(parts, out):
    lane = lane_index(GROUP)
    total = jnp.zeros((GROUP, LANES), jnp.float32)
    remaining = jnp.ones((GROUP, LANES), jnp.float32)
    for b in range(BLOCKS):
        v = parts[GROUP * b : GROUP * (b + 1)]
        kept = v
        for c in range(3):
            kept = jnp.where(
                jnp.logical_and(lane >= TILE * c, lane < TILE * (c + 1)),
                pltpu.roll(v, TILE * (c + 1), 1),
                kept,
            )
        total = total + remaining * v
        remaining = remaining * kept
    total = jnp.where(lane >= 3 * TILE, 1.0 - remaining, total)
    turned = [total] + [pltpu.roll(total, TILE * s, 1) for s in range(1, 4)]
    for c in range(4):
        for t in range(GROUP):
            m = t % 4
            out[c, :, TILE * t : TILE * (t + 1)] = turned[(m - c) % 4][
                t : t + 1, TILE * m : TILE * (m + 1)
            ]


def call(kernel, shape, scratch, *operands, **options):
    spec = pl.BlockSpec(memory_space=VMEM)
    operands = [pltpu.with_memory_space_constraint(x, VMEM) for x in operands]
    return pl.pallas_call(
        kernel,
        out_shape=VMEM(shape, jnp.float32),
        in_specs=[spec] * len(operands),
        out_specs=spec,
        scratch_shapes=[VMEM(s, jnp.float32) for s in scratch],
        **options,
    )(*operands)


def shifted(value, axis, by):
    size = lax.axis_size(axis)
    pairs = [(i, i + by) for i in range(size) if 0 <= i + by < size]
    return lax.ppermute(value, axis, pairs)


def rendered(density, transfer_table):
    bands = lax.axis_size("rows")
    edge = VMEM((PLANES, HALO, COLS), jnp.float32)
    one, two = pl.pallas_call(
        slice_kernel,
        out_shape=[edge, edge],
        in_specs=[pl.BlockSpec(memory_space=pl.ANY)],
        out_specs=[pl.BlockSpec(memory_space=VMEM)] * 2,
        scratch_shapes=[
            VMEM((2, PLANES, 8, COLS), jnp.float32),
            pltpu.SemaphoreType.DMA((2,)),
        ],
        name="slice_kernel",
    )(density)
    pairs = [(i, i + 1) for i in range(0, bands, 2)]
    from_one = lax.ppermute(one, "rows", pairs + [(b, a) for a, b in pairs])
    pairs = [(i, i + 1) for i in range(1, bands - 1, 2)]
    from_two = lax.ppermute(two, "rows", pairs + [(b, a) for a, b in pairs])
    chunks = (GROUP, PLANES, SEG_ROWS, LANES)
    cut = pl.pallas_call(
        pack_kernel,
        out_shape=VMEM(chunks, jnp.float32),
        in_specs=[pl.BlockSpec(memory_space=pl.ANY)],
        out_specs=pl.BlockSpec(memory_space=VMEM),
        scratch_shapes=[
            VMEM((PLANES, BAND, COLS), jnp.float32),
            VMEM((PLANES, SEGS * SEG_ROWS, COLS), jnp.float32),
            pltpu.SemaphoreType.DMA((PLANES, PARTS)),
        ],
        name="pack_kernel",
    )(density)
    sent = call(
        halo_kernel,
        chunks,
        [(PLANES, 8, COLS)],
        cut,
        two,
        from_one,
        from_two,
        input_output_aliases={0: 0},
    )
    groups = [[GROUP * b + i for i in range(GROUP)] for b in range(BLOCKS)]
    mine = lax.all_to_all(sent, "depth", 0, 0, axis_index_groups=groups, tiled=True)
    near = HALO // PLANES
    tail = mine[GROUP - near :]
    after = shifted(mine[: 2 * near], "depth", -GROUP)
    knots = transfer_table.T
    field = (FRONT + DEEP, TALL, LANES)
    inner = call(
        inner_kernel,
        (2 * PASSES + 4, SEG_ROWS, LANES),
        [field, field, (UNROLL, TALL, LANES), (4, SEG_ROWS, LANES)],
        mine,
        knots,
    )
    few = (2 * HALO + 2, TALL, LANES)
    partial = call(
        outer_kernel,
        (BAND, LANES),
        [few, few, (2 * HALO, TALL, LANES)],
        tail,
        after,
        inner,
        knots,
    )
    parts = lax.all_to_all(partial, "depth", 0, 0, tiled=True)
    spec = pl.BlockSpec(memory_space=VMEM)
    return pl.pallas_call(
        gather_kernel,
        out_shape=jax.ShapeDtypeStruct((4, 1, COLS), jnp.float32),
        in_specs=[spec],
        out_specs=spec,
        name="gather_kernel",
    )(pltpu.with_memory_space_constraint(parts, VMEM))


def solution(mesh):
    placed = (P("depth", "rows", None), P())
    return jax.shard_map(
        rendered,
        mesh=mesh,
        in_specs=placed,
        out_specs=P(None, ("rows", "depth"), None),
        check_vma=False,
    )
```

```python
import jax
import jax.numpy as jnp
from jax import lax
from jax.experimental import pallas as pl
from jax.experimental.pallas import tpu as pltpu
from jax.sharding import PartitionSpec as P


PASSES = 3
KNOTS = 16
TIME_STEP = 0.15
OPTICAL_DEPTH = 3.0
UPPER_DENSITY = 6.0
AMBIENT = 0.35

GROUP = 16
BLOCKS = 8
HALO = 4
BAND = 128
COLS = 512
TILE = COLS // GROUP
WIDE = TILE + 2 * HALO
SEGS = 3
SEG_ROWS = 46
RAW_ROWS = 43
TILES = 6
LINES = 8 * TILES
PLANES = 2
DEEP = GROUP * PLANES
LANES = 128
TOP = 8
TALL = 64
FRONT = HALO
CHUNK = 2 * RAW_ROWS
SPARE = SEGS * WIDE
TAIL = 2 * PASSES + 4
PARTS = 4
UNROLL = 7
SHADED = 8
VMEM = pltpu.VMEM


def lane_index(rows=8):
    return lax.broadcasted_iota(jnp.int32, (rows, LANES), 1)


def window_masks():
    lane = lane_index()
    segment, left, right, spare = [], [], [], []
    for m in range(4):
        local = (lane - (TILE * m - HALO)) % LANES
        segment.append([(local >= WIDE * k) & (local < WIDE * (k + 1)) for k in range(SEGS)])
        column = local % WIDE
        left.append(column < HALO)
        right.append(column >= WIDE - HALO)
        spare.append(local >= SPARE)
    return segment, left, right, spare


def windows(tiles, joined, left, right):
    for t in range(GROUP):
        q, m = divmod(t, 4)
        value = joined(tiles, q, m)
        if m == 0 and q > 0:
            value = jnp.where(left[m], joined(tiles, q - 1, m), value)
        if m == 3 and q < 3:
            value = jnp.where(right[m], joined(tiles, q + 1, m), value)
        yield t, m, value


def slice_kernel(density, one, two, ends, sems):
    even = lax.axis_index("rows") % 2 == 0
    copies = []
    for i, row in enumerate((0, BAND - 8)):
        source = density.at[:, pl.ds(row, 8), :]
        copies.append(pltpu.make_async_copy(source, ends.at[i], sems.at[i]))
    for copy in copies:
        copy.start()
    for copy in copies:
        copy.wait()
    for p in range(PLANES):
        first = ends[0, p, 0:HALO, :]
        last = ends[1, p, 8 - HALO : 8, :]
        one[p] = jnp.where(even, last, first)
        two[p] = jnp.where(even, first, last)


def pack_kernel(density, out, own, sems):
    part = BAND // PARTS
    copies = []
    for p in range(PLANES):
        for i in range(PARTS):
            at = pl.ds(part * i, part)
            copies.append(
                pltpu.make_async_copy(density.at[p, at, :], own.at[p, at, :], sems.at[p, i])
            )
    for copy in copies:
        copy.start()
    for p in range(PLANES):
        own[p, BAND:, :] = jnp.zeros((8, COLS), jnp.float32)
    segment, left, right, _ = window_masks()

    def joined(rolled, q, m):
        rest = jnp.where(segment[m][1], rolled[1][q], rolled[2][q])
        return jnp.where(segment[m][0], rolled[0][q], rest)

    for p in range(PLANES):
        for copy in copies[PARTS * p : PARTS * (p + 1)]:
            copy.wait()
        for j in range(TILES):
            count = min(8, RAW_ROWS - 8 * j)
            rolled = []
            for k in range(SEGS):
                start = RAW_ROWS * k + 8 * j
                rows = own[p, start : start + 8, :]
                tiles = [rows[:, LANES * q : LANES * (q + 1)] for q in range(4)]
                rolled.append([pltpu.roll(x, WIDE * k, 1) if k else x for x in tiles])
            for t, m, value in windows(rolled, joined, left, right):
                start = CHUNK * t + RAW_ROWS * p + 8 * j
                out[start : start + count, :] = value[:count]


def halo_kernel(sent, two, from_one, from_two, out, edge):
    band = lax.axis_index("rows")
    bands = lax.axis_size("rows")
    even = band % 2 == 0

    def above(source):
        for p in range(PLANES):
            edge[p, 0:HALO, :] = source[p]

    def below(source):
        for p in range(PLANES):
            edge[p, HALO : 2 * HALO, :] = source[p]

    @pl.when(even)
    def _():
        below(from_one)

    @pl.when(jnp.logical_not(even))
    def _():
        above(from_one)

    @pl.when(even & (band > 0))
    def _():
        above(from_two)

    @pl.when(jnp.logical_not(even) & (band < bands - 1))
    def _():
        below(from_two)

    @pl.when(band == 0)
    def _():
        for p in range(PLANES):
            for i in range(HALO):
                edge[p, HALO - 1 - i : HALO - i, :] = two[p, i : i + 1, :]

    @pl.when(band == bands - 1)
    def _():
        for p in range(PLANES):
            for i in range(HALO):
                edge[p, HALO + i : HALO + i + 1, :] = two[p, HALO - 1 - i : HALO - i, :]

    _, left, right, spare = window_masks()

    def joined(tiles, q, m):
        return tiles[q]

    for p in range(PLANES):
        tiles = [edge[p, :, LANES * q : LANES * (q + 1)] for q in range(4)]
        for t, m, value in windows(tiles, joined, left, right):
            for g in range(WIDE // 8):
                start = CHUNK * t + RAW_ROWS * p + 8 * g
                moved = pltpu.roll(value, SPARE - 8 * g, 1)
                here = sent[start : start + 8, :]
                out[start : start + 8, :] = jnp.where(spare[m], moved, here)


def flux(change):
    return change / (1.0 + change * change)


def rows_at(j, by=0):
    if isinstance(j, int):
        return slice(TOP + 8 * j + by, TOP + 8 * j + by + 8)
    return pl.ds(pl.multiple_of(8 * j, 8) + TOP + by, 8)


def put(ref, p, tiles):
    for j in range(TILES):
        ref[p, rows_at(j), :] = tiles[j]
    last = SEG_ROWS - 8 * (TILES - 1) - 1
    ref[p, TOP - 1 : TOP, :] = pltpu.roll(tiles[-1], WIDE, 1)[last : last + 1]
    ref[p, TOP + SEG_ROWS : TOP + SEG_ROWS + 1, :] = pltpu.roll(tiles[0], LANES - WIDE, 1)[0:1]


def take(ref, p, by=0):
    return [ref[p, rows_at(j, by), :] for j in range(TILES)]


class Tile:
    def __init__(self):
        self.block = lax.axis_index("depth") // GROUP
        tile = lax.axis_index("depth") % GROUP
        self.start = TILE * (tile % 4) - HALO
        local = (lane_index() - self.start + LANES) % LANES
        column = local % WIDE
        first, last = tile == 0, tile == GROUP - 1
        self.at_first = jnp.logical_and(column == HALO, first)
        self.at_last = jnp.logical_and(column == HALO + TILE - 1, last)
        self.open_face = jnp.where(
            jnp.logical_or(self.at_last, jnp.logical_and(column == HALO - 1, first)), 0.0, 1.0
        )
        row = lax.broadcasted_iota(jnp.int32, (8, LANES), 0)
        self.local = local
        self.segment = [(local >= WIDE * k) & (local < WIDE * (k + 1)) for k in range(SEGS)]
        self.top = self.segment[0] & (row < HALO)
        self.bottom = self.segment[2] & (row < HALO)
        self.head = self.segment[1] & (row == 0)
        self.foot = self.segment[1] & (row >= 4) & (row < 6)

    def unpack(self, raw, start):
        def load(by):
            return raw[pl.ds(start + by, 8), :]

        zeroth, end = load(0), load(RAW_ROWS - 8)
        tiles = []
        for j in range(TILES):
            if j == 0:
                parts = (pltpu.roll(zeroth, 4, 0), pltpu.roll(zeroth, 1, 0), load(2))
            elif j < TILES - 1:
                parts = (load(8 * j - 4), load(8 * j - 1), load(8 * j + 2))
            else:
                parts = (pltpu.roll(end, 7, 0), pltpu.roll(end, 4, 0), end)
            rest = jnp.where(self.segment[1], parts[1], parts[2])
            tiles.append(jnp.where(self.segment[0], parts[0], rest))
        halo = None
        for g in range(WIDE // 8):
            rows = load(8 * g) if g else zeroth
            moved = pltpu.roll(rows, LANES - SPARE + 8 * g, 1)
            halo = moved if halo is None else jnp.where(self.local >= 8 * g, moved, halo)
        head = pltpu.roll(pltpu.roll(end, WIDE, 1), 1, 0)
        foot = pltpu.roll(pltpu.roll(zeroth, LANES - WIDE, 1), 4, 0)
        below = pltpu.roll(pltpu.roll(halo, 2 * WIDE, 1), 4, 0)
        tiles[0] = jnp.where(self.top, halo, jnp.where(self.head, head, tiles[0]))
        tiles[-1] = jnp.where(self.bottom, below, jnp.where(self.foot, foot, tiles[-1]))
        return tiles


def diffuse(src, p, dst, to, fluxes, slot, flux_nearer, tile):
    f = take(src, p)
    below = take(src, p, 1)
    deeper = take(src, p + 1)
    flux_deeper = [flux(deeper[j] - f[j]) for j in range(TILES)]
    row = [flux(below[j] - f[j]) for j in range(TILES)]
    for j in range(TILES):
        fluxes[slot, rows_at(j), :] = row[j]
    last = SEG_ROWS - 8 * (TILES - 1) - 1
    fluxes[slot, TOP - 1 : TOP, :] = pltpu.roll(row[-1], WIDE, 1)[last : last + 1]
    row_prev = take(fluxes, slot, -1)
    new = []
    for j in range(TILES):
        col = flux((pltpu.roll(f[j], LANES - 1, 1) - f[j]) * tile.open_face)
        total = flux_deeper[j] - flux_nearer[j]
        total = total + (row[j] - row_prev[j])
        total = total + (col - pltpu.roll(col, 1, 1))
        new.append(f[j] + TIME_STEP * total)
    put(dst, to, new)
    return flux_deeper


def first_flux(src, p):
    here, deeper = take(src, p), take(src, p + 1)
    return [flux(deeper[j] - here[j]) for j in range(TILES)]


ALONG_ROWS = lax.GatherDimensionNumbers(
    offset_dims=(),
    collapsed_slice_dims=(0,),
    start_index_map=(0,),
    operand_batching_dims=(1,),
    start_indices_batching_dims=(1,),
)


def along_rows(x, k):
    return lax.gather(
        x, k[..., None], ALONG_ROWS, (1, 1), mode=lax.GatherScatterMode.PROMISE_IN_BOUNDS
    )


def pick(parts, k, high):
    return jnp.where(high, along_rows(parts[1], k), along_rows(parts[0], k))


def tables(transfer):
    base, slope = [], []
    for c in range(4):
        knots = jnp.broadcast_to(transfer[:, c : c + 1], (KNOTS, LANES))
        row = lax.broadcasted_iota(jnp.int32, (KNOTS, LANES), 0)
        after = jnp.where(row == KNOTS - 1, 0.0, pltpu.roll(knots, KNOTS - 1, 0))
        step = after - knots
        base.append((knots[:8], knots[8:]))
        slope.append((step[:8], step[8:]))
    return base, slope


def shade(src, p, j, carry, lookup, tile):
    red, green, blue, remaining = carry
    base, slope = lookup
    f = src[p, rows_at(j), :]
    depth = src[p + 1, rows_at(j), :] - src[p - 1, rows_at(j), :]
    row = src[p, rows_at(j, 1), :] - src[p, rows_at(j, -1), :]
    right = jnp.where(tile.at_last, f, pltpu.roll(f, LANES - 1, 1))
    left = jnp.where(tile.at_first, f, pltpu.roll(f, 1, 1))
    col = right - left
    square = depth * depth + row * row + col * col + 1.0
    gain = 1.0 - AMBIENT
    along = jnp.abs(0.64 * gain * depth + 0.6 * gain * row + 0.48 * gain * col)
    shading = AMBIENT + along * lax.rsqrt(square)
    position = f * ((KNOTS - 1) / UPPER_DENSITY)
    k = position.astype(jnp.int32)
    frac = position - k.astype(jnp.float32)
    high = k >= 8
    k = jnp.bitwise_and(k, 7)
    mixed = [pick(base[c], k, high) + frac * pick(slope[c], k, high) for c in range(4)]
    kept = jnp.exp(mixed[3] * (-OPTICAL_DEPTH / (DEEP * BLOCKS)))
    weight = remaining * (1.0 - kept) * shading
    return (
        red + weight * mixed[0],
        green + weight * mixed[1],
        blue + weight * mixed[2],
        remaining * kept,
    )


def inner_kernel(mine, knots, out, fa, fb, fluxes, sums):
    tile = Tile()
    zero = jnp.zeros((8, LANES), jnp.float32)
    is_first = tile.block == 0

    def fill(i, carry):
        for u in range(4):
            for p in range(PLANES):
                k = 4 * i + u
                put(fa, FRONT + PLANES * k + p, tile.unpack(mine, CHUNK * k + RAW_ROWS * p))
        return carry

    lax.fori_loop(0, GROUP // 4, fill, 0)
    for i in range(HALO):
        for j in range(TILES):
            plane = fa[FRONT + DEEP - HALO + i, rows_at(j), :]
            out[TAIL + i, 8 * j : 8 * j + 8, :] = plane

    @pl.when(is_first)
    def _():
        for i in range(HALO):
            fa[FRONT - 1 - i] = fa[FRONT + i]

    src, dst = fa, fb
    for sweep in range(PASSES):
        lo, hi = FRONT + sweep + 1, FRONT + DEEP - 1 - sweep

        @pl.when(is_first)
        def _(src=src, dst=dst, lo=lo):
            carry = first_flux(src, lo - 5)
            for u in range(4):
                p = lo - 4 + u
                carry = diffuse(src, p, dst, p, fluxes, u, carry, tile)

        count = hi - lo
        unroll = 6 if count % 6 == 0 else UNROLL

        def step(i, carry, src=src, dst=dst, lo=lo, unroll=unroll):
            for u in range(unroll):
                p = lo + unroll * i + u
                carry = diffuse(src, p, dst, p, fluxes, u, carry, tile)
            return carry

        whole = count // unroll
        carry = lax.fori_loop(0, whole, step, first_flux(src, lo - 1))
        for u in range(count - unroll * whole):
            p = lo + unroll * whole + u
            carry = diffuse(src, p, dst, p, fluxes, u, carry, tile)
        for i in range(2):
            for j in range(TILES):
                out[2 * sweep + i, 8 * j : 8 * j + 8, :] = dst[hi - 2 + i, rows_at(j), :]
        src, dst = dst, src

    lookup = tables(knots)
    start = (zero, zero, zero, zero + 1.0)

    def rows(j):
        return pl.ds(pl.multiple_of(8 * j, 8), 8)

    @pl.when(is_first)
    def _():
        def shaded(j, unused):
            carry = start
            for u in range(HALO):
                carry = shade(src, FRONT + u, j, carry, lookup, tile)
            for c in range(4):
                sums[c, rows(j), :] = carry[c]
            return unused

        lax.fori_loop(0, TILES, shaded, 0)

    @pl.when(jnp.logical_not(is_first))
    def _():
        for c in range(4):
            for j in range(TILES):
                sums[c, 8 * j : 8 * j + 8, :] = start[c]

    def shaded(j, unused):
        def planes(i, carry):
            for u in range(SHADED):
                p = FRONT + HALO + SHADED * i + u
                carry = shade(src, p, j, carry, lookup, tile)
            return carry

        carry = tuple(sums[c, rows(j), :] for c in range(4))
        carry = lax.fori_loop(0, (DEEP - 2 * HALO) // SHADED, planes, carry)
        for c in range(4):
            out[2 * PASSES + c, rows(j), :] = carry[c]
        return unused

    lax.fori_loop(0, TILES, shaded, 0)


def outer_kernel(after, inner, knots, out, fa, fb, fluxes):
    tile = Tile()
    lookup = tables(knots)
    is_last = tile.block == BLOCKS - 1

    def tail(to, i):
        put(fa, to, [inner[TAIL + i, 8 * j : 8 * j + 8, :] for j in range(TILES)])

    for i in range(2):
        tail(i, HALO - 2 + i)

    @pl.when(jnp.logical_not(is_last))
    def _():
        for i in range(2 * HALO):
            k, p = divmod(i, PLANES)
            put(fa, 2 + i, tile.unpack(after, CHUNK * k + RAW_ROWS * p))

    @pl.when(is_last)
    def _():
        for i in range(2 * HALO):
            tail(2 + i, max(HALO - 1 - i, 0))

    src, dst = fa, fb
    for sweep in range(PASSES):
        carry = first_flux(src, 0)
        for i in range(2 * HALO):
            carry = diffuse(src, i + 1, dst, i + 2, fluxes, i, carry, tile)
        for i in range(2):
            rest = [inner[2 * sweep + i, 8 * j : 8 * j + 8, :] for j in range(TILES)]
            put(dst, i, rest)
        src, dst = dst, src

    lane = lane_index()
    for j in range(TILES):
        sums = tuple(inner[2 * PASSES + c, 8 * j : 8 * j + 8, :] for c in range(4))
        for i in range(2 * HALO):
            if i == HALO:
                own = sums
            sums = shade(src, i + 1, j, sums, lookup, tile)
        sums = [jnp.where(is_last, own[c], sums[c]) for c in range(4)]
        for k in range(SEGS):
            value = None
            for c in range(4):
                by = TILE * c - WIDE * k - HALO - tile.start + LANES * 2
                moved = pltpu.roll(sums[c], lax.rem(by, LANES), 1)
                value = moved if value is None else jnp.where(lane >= TILE * c, moved, value)
            first = SEG_ROWS * k + 8 * j - HALO
            lo, hi = max(first, 0), min(first + min(8, SEG_ROWS - 8 * j), BAND)
            if lo < hi:
                out[lo:hi, :] = value[lo - first : hi - first]


def gather_kernel(parts, out):
    lane = lane_index(GROUP)
    total = jnp.zeros((GROUP, LANES), jnp.float32)
    remaining = jnp.ones((GROUP, LANES), jnp.float32)
    for b in range(BLOCKS):
        v = parts[GROUP * b : GROUP * (b + 1)]
        kept = v
        for c in range(3):
            kept = jnp.where(
                jnp.logical_and(lane >= TILE * c, lane < TILE * (c + 1)),
                pltpu.roll(v, TILE * (c + 1), 1),
                kept,
            )
        total = total + remaining * v
        remaining = remaining * kept
    total = jnp.where(lane >= 3 * TILE, 1.0 - remaining, total)
    turned = [total] + [pltpu.roll(total, TILE * s, 1) for s in range(1, 4)]
    for c in range(4):
        for t in range(GROUP):
            m = t % 4
            out[c, :, TILE * t : TILE * (t + 1)] = turned[(m - c) % 4][
                t : t + 1, TILE * m : TILE * (m + 1)
            ]


def call(kernel, shape, scratch, *operands, **options):
    spec = pl.BlockSpec(memory_space=VMEM)
    operands = [pltpu.with_memory_space_constraint(x, VMEM) for x in operands]
    return pl.pallas_call(
        kernel,
        out_shape=VMEM(shape, jnp.float32),
        in_specs=[spec] * len(operands),
        out_specs=spec,
        scratch_shapes=[VMEM(s, jnp.float32) for s in scratch],
        **options,
    )(*operands)


def shifted(value, axis, by):
    size = lax.axis_size(axis)
    pairs = [(i, i + by) for i in range(size) if 0 <= i + by < size]
    return lax.ppermute(value, axis, pairs)


def rendered(density, transfer_table):
    bands = lax.axis_size("rows")
    edge = VMEM((PLANES, HALO, COLS), jnp.float32)
    one, two = pl.pallas_call(
        slice_kernel,
        out_shape=[edge, edge],
        in_specs=[pl.BlockSpec(memory_space=pl.ANY)],
        out_specs=[pl.BlockSpec(memory_space=VMEM)] * 2,
        scratch_shapes=[
            VMEM((2, PLANES, 8, COLS), jnp.float32),
            pltpu.SemaphoreType.DMA((2,)),
        ],
        name="slice_kernel",
    )(density)
    pairs = [(i, i + 1) for i in range(0, bands, 2)]
    from_one = lax.ppermute(one, "rows", pairs + [(b, a) for a, b in pairs])
    pairs = [(i, i + 1) for i in range(1, bands - 1, 2)]
    from_two = lax.ppermute(two, "rows", pairs + [(b, a) for a, b in pairs])
    chunks = (GROUP * CHUNK, LANES)
    cut = pl.pallas_call(
        pack_kernel,
        out_shape=VMEM(chunks, jnp.float32),
        in_specs=[pl.BlockSpec(memory_space=pl.ANY)],
        out_specs=pl.BlockSpec(memory_space=VMEM),
        scratch_shapes=[
            VMEM((PLANES, BAND + 8, COLS), jnp.float32),
            pltpu.SemaphoreType.DMA((PLANES, PARTS)),
        ],
        name="pack_kernel",
    )(density)
    sent = call(
        halo_kernel,
        chunks,
        [(PLANES, 8, COLS)],
        cut,
        two,
        from_one,
        from_two,
        input_output_aliases={0: 0},
    )
    groups = [[GROUP * b + i for i in range(GROUP)] for b in range(BLOCKS)]
    sent = sent.reshape(GROUP, CHUNK, 1, LANES)
    mine = lax.all_to_all(sent, "depth", 0, 0, axis_index_groups=groups, tiled=True)
    mine = mine.reshape(GROUP * CHUNK, LANES)
    after = shifted(mine[: 2 * HALO // PLANES * CHUNK], "depth", -GROUP)
    knots = transfer_table.T
    field = (FRONT + DEEP, TALL, LANES)
    inner = call(
        inner_kernel,
        (TAIL + HALO, LINES, LANES),
        [field, field, (UNROLL, TALL, LANES), (4, LINES, LANES)],
        mine,
        knots,
    )
    few = (2 * HALO + 2, TALL, LANES)
    partial = call(
        outer_kernel,
        (BAND, LANES),
        [few, few, (2 * HALO, TALL, LANES)],
        after,
        inner,
        knots,
    )
    parts = lax.all_to_all(partial, "depth", 0, 0, tiled=True)
    spec = pl.BlockSpec(memory_space=VMEM)
    return pl.pallas_call(
        gather_kernel,
        out_shape=jax.ShapeDtypeStruct((4, 1, COLS), jnp.float32),
        in_specs=[spec],
        out_specs=spec,
        name="gather_kernel",
    )(pltpu.with_memory_space_constraint(parts, VMEM))


def solution(mesh):
    placed = (P("depth", "rows", None), P())
    return jax.shard_map(
        rendered,
        mesh=mesh,
        in_specs=placed,
        out_specs=P(None, ("rows", "depth"), None),
        check_vma=False,
    )
```

```python
import jax
import jax.numpy as jnp
from jax import lax
from jax.experimental import pallas as pl
from jax.experimental.pallas import tpu as pltpu
from jax.sharding import PartitionSpec as P


PASSES = 3
KNOTS = 16
TIME_STEP = 0.15
OPTICAL_DEPTH = 3.0
UPPER_DENSITY = 6.0
AMBIENT = 0.35
SCALE = TIME_STEP**-0.5

GROUP = 16
BLOCKS = 8
HALO = 4
BAND = 128
COLS = 512
TILE = COLS // GROUP
WIDE = TILE + 2 * HALO
SEGS = 3
SEG_ROWS = 46
RAW_ROWS = 43
TILES = 6
LINES = 8 * TILES
PLANES = 2
DEEP = GROUP * PLANES
LANES = 128
TOP = 8
TALL = 64
FRONT = HALO
CHUNK = 2 * RAW_ROWS
SPARE = SEGS * WIDE
TAIL = 2 * PASSES + 4
PARTS = 4
UNROLL = 7
SHADED = 8
VMEM = pltpu.VMEM


def lane_index(rows=8):
    return lax.broadcasted_iota(jnp.int32, (rows, LANES), 1)


def window_masks():
    lane = lane_index()
    segment, left, right, spare = [], [], [], []
    for m in range(4):
        local = (lane - (TILE * m - HALO)) % LANES
        segment.append([(local >= WIDE * k) & (local < WIDE * (k + 1)) for k in range(SEGS)])
        column = local % WIDE
        left.append(column < HALO)
        right.append(column >= WIDE - HALO)
        spare.append(local >= SPARE)
    return segment, left, right, spare


def windows(tiles, joined, left, right):
    for t in range(GROUP):
        q, m = divmod(t, 4)
        value = joined(tiles, q, m)
        if m == 0 and q > 0:
            value = jnp.where(left[m], joined(tiles, q - 1, m), value)
        if m == 3 and q < 3:
            value = jnp.where(right[m], joined(tiles, q + 1, m), value)
        yield t, m, value


def slice_kernel(density, one, two, ends, sems):
    even = lax.axis_index("rows") % 2 == 0
    copies = []
    for i, row in enumerate((0, BAND - 8)):
        source = density.at[:, pl.ds(row, 8), :]
        copies.append(pltpu.make_async_copy(source, ends.at[i], sems.at[i]))
    for copy in copies:
        copy.start()
    for copy in copies:
        copy.wait()
    for p in range(PLANES):
        first = ends[0, p, 0:HALO, :]
        last = ends[1, p, 8 - HALO : 8, :]
        one[p] = jnp.where(even, last, first)
        two[p] = jnp.where(even, first, last)


def pack_kernel(density, out, own, sems):
    part = BAND // PARTS
    copies = []
    for p in range(PLANES):
        for i in range(PARTS):
            at = pl.ds(part * i, part)
            copies.append(
                pltpu.make_async_copy(density.at[p, at, :], own.at[p, at, :], sems.at[p, i])
            )
    for copy in copies:
        copy.start()
    for p in range(PLANES):
        own[p, BAND:, :] = jnp.zeros((8, COLS), jnp.float32)
    segment, left, right, _ = window_masks()

    def joined(rolled, q, m):
        rest = jnp.where(segment[m][1], rolled[1][q], rolled[2][q])
        return jnp.where(segment[m][0], rolled[0][q], rest)

    for p in range(PLANES):
        for copy in copies[PARTS * p : PARTS * (p + 1)]:
            copy.wait()
        for j in range(TILES):
            count = min(8, RAW_ROWS - 8 * j)
            rolled = []
            for k in range(SEGS):
                start = RAW_ROWS * k + 8 * j
                rows = own[p, start : start + 8, :]
                tiles = [rows[:, LANES * q : LANES * (q + 1)] for q in range(4)]
                rolled.append([pltpu.roll(x, WIDE * k, 1) if k else x for x in tiles])
            for t, m, value in windows(rolled, joined, left, right):
                start = CHUNK * t + RAW_ROWS * p + 8 * j
                out[start : start + count, :] = (value * SCALE)[:count]


def halo_kernel(sent, two, from_one, from_two, out, edge):
    band = lax.axis_index("rows")
    bands = lax.axis_size("rows")
    even = band % 2 == 0

    def above(source):
        for p in range(PLANES):
            edge[p, 0:HALO, :] = source[p]

    def below(source):
        for p in range(PLANES):
            edge[p, HALO : 2 * HALO, :] = source[p]

    @pl.when(even)
    def _():
        below(from_one)

    @pl.when(jnp.logical_not(even))
    def _():
        above(from_one)

    @pl.when(even & (band > 0))
    def _():
        above(from_two)

    @pl.when(jnp.logical_not(even) & (band < bands - 1))
    def _():
        below(from_two)

    @pl.when(band == 0)
    def _():
        for p in range(PLANES):
            for i in range(HALO):
                edge[p, HALO - 1 - i : HALO - i, :] = two[p, i : i + 1, :]

    @pl.when(band == bands - 1)
    def _():
        for p in range(PLANES):
            for i in range(HALO):
                edge[p, HALO + i : HALO + i + 1, :] = two[p, HALO - 1 - i : HALO - i, :]

    _, left, right, spare = window_masks()

    def joined(tiles, q, m):
        return tiles[q]

    for p in range(PLANES):
        tiles = [edge[p, :, LANES * q : LANES * (q + 1)] for q in range(4)]
        for t, m, value in windows(tiles, joined, left, right):
            for g in range(WIDE // 8):
                start = CHUNK * t + RAW_ROWS * p + 8 * g
                moved = pltpu.roll(value, SPARE - 8 * g, 1)
                here = sent[start : start + 8, :]
                out[start : start + 8, :] = jnp.where(spare[m], moved * SCALE, here)


def flux(change):
    return change / (SCALE * SCALE + change * change)


def rows_at(j, by=0):
    if isinstance(j, int):
        return slice(TOP + 8 * j + by, TOP + 8 * j + by + 8)
    return pl.ds(pl.multiple_of(8 * j, 8) + TOP + by, 8)


def put(ref, p, tiles):
    for j in range(TILES):
        ref[p, rows_at(j), :] = tiles[j]
    last = SEG_ROWS - 8 * (TILES - 1) - 1
    ref[p, TOP - 1 : TOP, :] = pltpu.roll(tiles[-1], WIDE, 1)[last : last + 1]
    ref[p, TOP + SEG_ROWS : TOP + SEG_ROWS + 1, :] = pltpu.roll(tiles[0], LANES - WIDE, 1)[0:1]


def take(ref, p, by=0):
    return [ref[p, rows_at(j, by), :] for j in range(TILES)]


class Tile:
    def __init__(self):
        self.block = lax.axis_index("depth") // GROUP
        tile = lax.axis_index("depth") % GROUP
        self.start = TILE * (tile % 4) - HALO
        local = (lane_index() - self.start + LANES) % LANES
        column = local % WIDE
        first, last = tile == 0, tile == GROUP - 1
        self.at_first = jnp.logical_and(column == HALO, first)
        self.at_last = jnp.logical_and(column == HALO + TILE - 1, last)
        self.open_face = jnp.where(
            jnp.logical_or(self.at_last, jnp.logical_and(column == HALO - 1, first)), 0.0, 1.0
        )
        row = lax.broadcasted_iota(jnp.int32, (8, LANES), 0)
        self.local = local
        self.segment = [(local >= WIDE * k) & (local < WIDE * (k + 1)) for k in range(SEGS)]
        self.top = self.segment[0] & (row < HALO)
        self.bottom = self.segment[2] & (row < HALO)
        self.head = self.segment[1] & (row == 0)
        self.foot = self.segment[1] & (row >= 4) & (row < 6)

    def unpack(self, raw, start):
        def load(by):
            return raw[pl.ds(start + by, 8), :]

        zeroth, end = load(0), load(RAW_ROWS - 8)
        tiles = []
        for j in range(TILES):
            if j == 0:
                parts = (pltpu.roll(zeroth, 4, 0), pltpu.roll(zeroth, 1, 0), load(2))
            elif j < TILES - 1:
                parts = (load(8 * j - 4), load(8 * j - 1), load(8 * j + 2))
            else:
                parts = (pltpu.roll(end, 7, 0), pltpu.roll(end, 4, 0), end)
            rest = jnp.where(self.segment[1], parts[1], parts[2])
            tiles.append(jnp.where(self.segment[0], parts[0], rest))
        halo = None
        for g in range(WIDE // 8):
            rows = load(8 * g) if g else zeroth
            moved = pltpu.roll(rows, LANES - SPARE + 8 * g, 1)
            halo = moved if halo is None else jnp.where(self.local >= 8 * g, moved, halo)
        head = pltpu.roll(pltpu.roll(end, WIDE, 1), 1, 0)
        foot = pltpu.roll(pltpu.roll(zeroth, LANES - WIDE, 1), 4, 0)
        below = pltpu.roll(pltpu.roll(halo, 2 * WIDE, 1), 4, 0)
        tiles[0] = jnp.where(self.top, halo, jnp.where(self.head, head, tiles[0]))
        tiles[-1] = jnp.where(self.bottom, below, jnp.where(self.foot, foot, tiles[-1]))
        return tiles


def diffuse(src, p, dst, to, fluxes, slot, flux_nearer, tile):
    f = take(src, p)
    below = take(src, p, 1)
    deeper = take(src, p + 1)
    flux_deeper = [flux(deeper[j] - f[j]) for j in range(TILES)]
    row = [flux(below[j] - f[j]) for j in range(TILES)]
    for j in range(TILES):
        fluxes[slot, rows_at(j), :] = row[j]
    last = SEG_ROWS - 8 * (TILES - 1) - 1
    fluxes[slot, TOP - 1 : TOP, :] = pltpu.roll(row[-1], WIDE, 1)[last : last + 1]
    row_prev = take(fluxes, slot, -1)
    new = []
    for j in range(TILES):
        col = flux((pltpu.roll(f[j], LANES - 1, 1) - f[j]) * tile.open_face)
        total = flux_deeper[j] - flux_nearer[j]
        total = total + (row[j] - row_prev[j])
        total = total + (col - pltpu.roll(col, 1, 1))
        new.append(f[j] + total)
    put(dst, to, new)
    return flux_deeper


def first_flux(src, p):
    here, deeper = take(src, p), take(src, p + 1)
    return [flux(deeper[j] - here[j]) for j in range(TILES)]


ALONG_ROWS = lax.GatherDimensionNumbers(
    offset_dims=(),
    collapsed_slice_dims=(0,),
    start_index_map=(0,),
    operand_batching_dims=(1,),
    start_indices_batching_dims=(1,),
)


def along_rows(x, k):
    return lax.gather(
        x, k[..., None], ALONG_ROWS, (1, 1), mode=lax.GatherScatterMode.PROMISE_IN_BOUNDS
    )


def tables(transfer):
    even, odd = [], []
    for c in range(4):
        for half, first in ((even, 0), (odd, 1)):
            knots = transfer[pl.ds(first, 8, stride=2), :]
            half.append(jnp.broadcast_to(knots[:, c : c + 1], (8, LANES)))
    return even, odd


def shade(src, p, j, carry, lookup, tile):
    red, green, blue, remaining = carry
    even, odd = lookup
    f = src[p, rows_at(j), :]
    depth = src[p + 1, rows_at(j), :] - src[p - 1, rows_at(j), :]
    row = src[p, rows_at(j, 1), :] - src[p, rows_at(j, -1), :]
    right = jnp.where(tile.at_last, f, pltpu.roll(f, LANES - 1, 1))
    left = jnp.where(tile.at_first, f, pltpu.roll(f, 1, 1))
    col = right - left
    square = depth * depth + row * row + col * col + SCALE * SCALE
    gain = 1.0 - AMBIENT
    along = jnp.abs(0.64 * gain * depth + 0.6 * gain * row + 0.48 * gain * col)
    shading = AMBIENT + along * lax.rsqrt(square)
    position = f * ((KNOTS - 1) / UPPER_DENSITY / SCALE)
    k = position.astype(jnp.int32)
    frac = position - k.astype(jnp.float32)
    near_odd = lax.shift_right_logical(k, 1)
    near_even = jnp.bitwise_and(lax.shift_right_logical(k + 1, 1), 7)
    weight_odd = jnp.where(jnp.bitwise_and(k, 1) == 0, frac, 1.0 - frac)
    mixed = []
    for c in range(4):
        low = along_rows(even[c], near_even)
        mixed.append(low + weight_odd * (along_rows(odd[c], near_odd) - low))
    kept = jnp.exp(mixed[3] * (-OPTICAL_DEPTH / (DEEP * BLOCKS)))
    weight = remaining * (1.0 - kept) * shading
    return (
        red + weight * mixed[0],
        green + weight * mixed[1],
        blue + weight * mixed[2],
        remaining * kept,
    )


def inner_kernel(mine, knots, out, fa, fb, fluxes, sums):
    tile = Tile()
    zero = jnp.zeros((8, LANES), jnp.float32)
    is_first = tile.block == 0

    def fill(i, carry):
        for u in range(4):
            for p in range(PLANES):
                k = 4 * i + u
                put(fa, FRONT + PLANES * k + p, tile.unpack(mine, CHUNK * k + RAW_ROWS * p))
        return carry

    lax.fori_loop(0, GROUP // 4, fill, 0)
    for i in range(HALO):
        for j in range(TILES):
            plane = fa[FRONT + DEEP - HALO + i, rows_at(j), :]
            out[TAIL + i, 8 * j : 8 * j + 8, :] = plane

    @pl.when(is_first)
    def _():
        for i in range(HALO):
            fa[FRONT - 1 - i] = fa[FRONT + i]

    src, dst = fa, fb
    for sweep in range(PASSES):
        lo, hi = FRONT + sweep + 1, FRONT + DEEP - 1 - sweep

        @pl.when(is_first)
        def _(src=src, dst=dst, lo=lo):
            carry = first_flux(src, lo - 5)
            for u in range(4):
                p = lo - 4 + u
                carry = diffuse(src, p, dst, p, fluxes, u, carry, tile)

        count = hi - lo
        unroll = 6 if count % 6 == 0 else UNROLL

        def step(i, carry, src=src, dst=dst, lo=lo, unroll=unroll):
            for u in range(unroll):
                p = lo + unroll * i + u
                carry = diffuse(src, p, dst, p, fluxes, u, carry, tile)
            return carry

        whole = count // unroll
        carry = lax.fori_loop(0, whole, step, first_flux(src, lo - 1))
        for u in range(count - unroll * whole):
            p = lo + unroll * whole + u
            carry = diffuse(src, p, dst, p, fluxes, u, carry, tile)
        for i in range(2):
            for j in range(TILES):
                out[2 * sweep + i, 8 * j : 8 * j + 8, :] = dst[hi - 2 + i, rows_at(j), :]
        src, dst = dst, src

    lookup = tables(knots)
    start = (zero, zero, zero, zero + 1.0)

    def rows(j):
        return pl.ds(pl.multiple_of(8 * j, 8), 8)

    @pl.when(is_first)
    def _():
        def shaded(j, unused):
            carry = start
            for u in range(HALO):
                carry = shade(src, FRONT + u, j, carry, lookup, tile)
            for c in range(4):
                sums[c, rows(j), :] = carry[c]
            return unused

        lax.fori_loop(0, TILES, shaded, 0)

    @pl.when(jnp.logical_not(is_first))
    def _():
        for c in range(4):
            for j in range(TILES):
                sums[c, 8 * j : 8 * j + 8, :] = start[c]

    def shaded(j, unused):
        def planes(i, carry):
            for u in range(SHADED):
                p = FRONT + HALO + SHADED * i + u
                carry = shade(src, p, j, carry, lookup, tile)
            return carry

        carry = tuple(sums[c, rows(j), :] for c in range(4))
        carry = lax.fori_loop(0, (DEEP - 2 * HALO) // SHADED, planes, carry)
        for c in range(4):
            out[2 * PASSES + c, rows(j), :] = carry[c]
        return unused

    lax.fori_loop(0, TILES, shaded, 0)


def outer_kernel(after, inner, knots, out, fa, fb, fluxes):
    tile = Tile()
    lookup = tables(knots)
    is_last = tile.block == BLOCKS - 1

    def tail(to, i):
        put(fa, to, [inner[TAIL + i, 8 * j : 8 * j + 8, :] for j in range(TILES)])

    for i in range(2):
        tail(i, HALO - 2 + i)

    @pl.when(jnp.logical_not(is_last))
    def _():
        for i in range(2 * HALO):
            k, p = divmod(i, PLANES)
            put(fa, 2 + i, tile.unpack(after, CHUNK * k + RAW_ROWS * p))

    @pl.when(is_last)
    def _():
        for i in range(2 * HALO):
            tail(2 + i, max(HALO - 1 - i, 0))

    src, dst = fa, fb
    for sweep in range(PASSES):
        carry = first_flux(src, 0)
        for i in range(2 * HALO):
            carry = diffuse(src, i + 1, dst, i + 2, fluxes, i, carry, tile)
        for i in range(2):
            rest = [inner[2 * sweep + i, 8 * j : 8 * j + 8, :] for j in range(TILES)]
            put(dst, i, rest)
        src, dst = dst, src

    lane = lane_index()
    for j in range(TILES):
        sums = tuple(inner[2 * PASSES + c, 8 * j : 8 * j + 8, :] for c in range(4))
        for i in range(2 * HALO):
            if i == HALO:
                own = sums
            sums = shade(src, i + 1, j, sums, lookup, tile)
        sums = [jnp.where(is_last, own[c], sums[c]) for c in range(4)]
        for k in range(SEGS):
            value = None
            for c in range(4):
                by = TILE * c - WIDE * k - HALO - tile.start + LANES * 2
                moved = pltpu.roll(sums[c], lax.rem(by, LANES), 1)
                value = moved if value is None else jnp.where(lane >= TILE * c, moved, value)
            first = SEG_ROWS * k + 8 * j - HALO
            lo, hi = max(first, 0), min(first + min(8, SEG_ROWS - 8 * j), BAND)
            if lo < hi:
                out[lo:hi, :] = value[lo - first : hi - first]


def gather_kernel(parts, out):
    lane = lane_index(GROUP)
    total = jnp.zeros((GROUP, LANES), jnp.float32)
    remaining = jnp.ones((GROUP, LANES), jnp.float32)
    for b in range(BLOCKS):
        v = parts[GROUP * b : GROUP * (b + 1)]
        kept = v
        for c in range(3):
            kept = jnp.where(
                jnp.logical_and(lane >= TILE * c, lane < TILE * (c + 1)),
                pltpu.roll(v, TILE * (c + 1), 1),
                kept,
            )
        total = total + remaining * v
        remaining = remaining * kept
    total = jnp.where(lane >= 3 * TILE, 1.0 - remaining, total)
    turned = [total] + [pltpu.roll(total, TILE * s, 1) for s in range(1, 4)]
    for c in range(4):
        for t in range(GROUP):
            m = t % 4
            out[c, :, TILE * t : TILE * (t + 1)] = turned[(m - c) % 4][
                t : t + 1, TILE * m : TILE * (m + 1)
            ]


def call(kernel, shape, scratch, *operands, **options):
    spec = pl.BlockSpec(memory_space=VMEM)
    operands = [pltpu.with_memory_space_constraint(x, VMEM) for x in operands]
    return pl.pallas_call(
        kernel,
        out_shape=VMEM(shape, jnp.float32),
        in_specs=[spec] * len(operands),
        out_specs=spec,
        scratch_shapes=[VMEM(s, jnp.float32) for s in scratch],
        **options,
    )(*operands)


def shifted(value, axis, by):
    size = lax.axis_size(axis)
    pairs = [(i, i + by) for i in range(size) if 0 <= i + by < size]
    return lax.ppermute(value, axis, pairs)


def rendered(density, transfer_table):
    bands = lax.axis_size("rows")
    edge = VMEM((PLANES, HALO, COLS), jnp.float32)
    one, two = pl.pallas_call(
        slice_kernel,
        out_shape=[edge, edge],
        in_specs=[pl.BlockSpec(memory_space=pl.ANY)],
        out_specs=[pl.BlockSpec(memory_space=VMEM)] * 2,
        scratch_shapes=[
            VMEM((2, PLANES, 8, COLS), jnp.float32),
            pltpu.SemaphoreType.DMA((2,)),
        ],
        name="slice_kernel",
    )(density)
    pairs = [(i, i + 1) for i in range(0, bands, 2)]
    from_one = lax.ppermute(one, "rows", pairs + [(b, a) for a, b in pairs])
    pairs = [(i, i + 1) for i in range(1, bands - 1, 2)]
    from_two = lax.ppermute(two, "rows", pairs + [(b, a) for a, b in pairs])
    chunks = (GROUP * CHUNK, LANES)
    cut = pl.pallas_call(
        pack_kernel,
        out_shape=VMEM(chunks, jnp.float32),
        in_specs=[pl.BlockSpec(memory_space=pl.ANY)],
        out_specs=pl.BlockSpec(memory_space=VMEM),
        scratch_shapes=[
            VMEM((PLANES, BAND + 8, COLS), jnp.float32),
            pltpu.SemaphoreType.DMA((PLANES, PARTS)),
        ],
        name="pack_kernel",
    )(density)
    sent = call(
        halo_kernel,
        chunks,
        [(PLANES, 8, COLS)],
        cut,
        two,
        from_one,
        from_two,
        input_output_aliases={0: 0},
    )
    groups = [[GROUP * b + i for i in range(GROUP)] for b in range(BLOCKS)]
    sent = sent.reshape(GROUP, CHUNK, 1, LANES)
    mine = lax.all_to_all(sent, "depth", 0, 0, axis_index_groups=groups, tiled=True)
    mine = mine.reshape(GROUP * CHUNK, LANES)
    after = shifted(mine[: 2 * HALO // PLANES * CHUNK], "depth", -GROUP)
    knots = transfer_table.T
    field = (FRONT + DEEP, TALL, LANES)
    inner = call(
        inner_kernel,
        (TAIL + HALO, LINES, LANES),
        [field, field, (UNROLL, TALL, LANES), (4, LINES, LANES)],
        mine,
        knots,
    )
    few = (2 * HALO + 2, TALL, LANES)
    partial = call(
        outer_kernel,
        (BAND, LANES),
        [few, few, (2 * HALO, TALL, LANES)],
        after,
        inner,
        knots,
    )
    parts = lax.all_to_all(partial, "depth", 0, 0, tiled=True)
    spec = pl.BlockSpec(memory_space=VMEM)
    return pl.pallas_call(
        gather_kernel,
        out_shape=jax.ShapeDtypeStruct((4, 1, COLS), jnp.float32),
        in_specs=[spec],
        out_specs=spec,
        name="gather_kernel",
    )(pltpu.with_memory_space_constraint(parts, VMEM))


def solution(mesh):
    placed = (P("depth", "rows", None), P())
    return jax.shard_map(
        rendered,
        mesh=mesh,
        in_specs=placed,
        out_specs=P(None, ("rows", "depth"), None),
        check_vma=False,
    )
```

```python
import jax
import jax.numpy as jnp
from jax import lax
from jax.experimental import pallas as pl
from jax.experimental.pallas import tpu as pltpu
from jax.sharding import PartitionSpec as P


PASSES = 3
KNOTS = 16
TIME_STEP = 0.15
OPTICAL_DEPTH = 3.0
UPPER_DENSITY = 6.0
AMBIENT = 0.35
SCALE = TIME_STEP**-0.5

GROUP = 16
BLOCKS = 8
HALO = 4
BAND = 128
COLS = 512
TILE = COLS // GROUP
WIDE = TILE + 2 * HALO
SEGS = 3
SEG_ROWS = 46
RAW_ROWS = 43
STARTS = (0, 42, 88)
TILES = 6
LINES = 8 * TILES
PLANES = 2
DEEP = GROUP * PLANES
LANES = 128
TOP = 8
TALL = 64
FRONT = HALO
CHUNK = 2 * RAW_ROWS
SPARE = SEGS * WIDE
TAIL = 2 * PASSES + 4
PARTS = 4
UNROLL = 7
SHADED = 8
VMEM = pltpu.VMEM


def lane_index(rows=8):
    return lax.broadcasted_iota(jnp.int32, (rows, LANES), 1)


def window_masks():
    lane = lane_index()
    segment, left, right, spare = [], [], [], []
    for m in range(4):
        local = (lane - (TILE * m - HALO)) % LANES
        segment.append([(local >= WIDE * k) & (local < WIDE * (k + 1)) for k in range(SEGS)])
        column = local % WIDE
        left.append(column < HALO)
        right.append(column >= WIDE - HALO)
        spare.append(local >= SPARE)
    return segment, left, right, spare


def windows(tiles, joined, left, right):
    for t in range(GROUP):
        q, m = divmod(t, 4)
        value = joined(tiles, q, m)
        if m == 0 and q > 0:
            value = jnp.where(left[m], joined(tiles, q - 1, m), value)
        if m == 3 and q < 3:
            value = jnp.where(right[m], joined(tiles, q + 1, m), value)
        yield t, m, value


def slice_kernel(density, one, two, ends, sems):
    even = lax.axis_index("rows") % 2 == 0
    copies = []
    for i, row in enumerate((0, BAND - 8)):
        source = density.at[:, pl.ds(row, 8), :]
        copies.append(pltpu.make_async_copy(source, ends.at[i], sems.at[i]))
    for copy in copies:
        copy.start()
    for copy in copies:
        copy.wait()
    for p in range(PLANES):
        first = ends[0, p, 0:HALO, :]
        last = ends[1, p, 8 - HALO : 8, :]
        one[p] = jnp.where(even, last, first)
        two[p] = jnp.where(even, first, last)


def pack_kernel(density, out, own, sems):
    part = BAND // PARTS
    copies = []
    for p in range(PLANES):
        for i in range(PARTS):
            at = pl.ds(part * i, part)
            copies.append(
                pltpu.make_async_copy(density.at[p, at, :], own.at[p, at, :], sems.at[p, i])
            )
    for copy in copies:
        copy.start()
    for p in range(PLANES):
        own[p, BAND:, :] = jnp.zeros((8, COLS), jnp.float32)
    segment, left, right, _ = window_masks()

    def joined(rolled, q, m):
        rest = jnp.where(segment[m][1], rolled[1][q], rolled[2][q])
        return jnp.where(segment[m][0], rolled[0][q], rest)

    for p in range(PLANES):
        for copy in copies[PARTS * p : PARTS * (p + 1)]:
            copy.wait()
        for j in range(TILES):
            count = min(8, RAW_ROWS - 8 * j)
            rolled = []
            for k in range(SEGS):
                start = STARTS[k] + 8 * j if (k, j) != (2, TILES - 1) else STARTS[2] - 3
                rows = own[p, start : start + 8, :]
                tiles = [rows[:, LANES * q : LANES * (q + 1)] for q in range(4)]
                rolled.append([pltpu.roll(x, WIDE * k, 1) if k else x for x in tiles])
            for t, m, value in windows(rolled, joined, left, right):
                start = CHUNK * t + RAW_ROWS * p + 8 * j
                out[start : start + count, :] = (value * SCALE)[:count]


def halo_kernel(sent, two, from_one, from_two, out, edge):
    band = lax.axis_index("rows")
    bands = lax.axis_size("rows")
    even = band % 2 == 0

    def above(source):
        for p in range(PLANES):
            edge[p, 0:HALO, :] = source[p]

    def below(source):
        for p in range(PLANES):
            edge[p, HALO : 2 * HALO, :] = source[p]

    @pl.when(even)
    def _():
        below(from_one)

    @pl.when(jnp.logical_not(even))
    def _():
        above(from_one)

    @pl.when(even & (band > 0))
    def _():
        above(from_two)

    @pl.when(jnp.logical_not(even) & (band < bands - 1))
    def _():
        below(from_two)

    @pl.when(band == 0)
    def _():
        for p in range(PLANES):
            for i in range(HALO):
                edge[p, HALO - 1 - i : HALO - i, :] = two[p, i : i + 1, :]

    @pl.when(band == bands - 1)
    def _():
        for p in range(PLANES):
            for i in range(HALO):
                edge[p, HALO + i : HALO + i + 1, :] = two[p, HALO - 1 - i : HALO - i, :]

    _, left, right, spare = window_masks()

    def joined(tiles, q, m):
        return tiles[q]

    for p in range(PLANES):
        tiles = [edge[p, :, LANES * q : LANES * (q + 1)] for q in range(4)]
        for t, m, value in windows(tiles, joined, left, right):
            for g in range(WIDE // 8):
                start = CHUNK * t + RAW_ROWS * p + 8 * g
                moved = pltpu.roll(value, SPARE - 8 * g, 1)
                here = sent[start : start + 8, :]
                out[start : start + 8, :] = jnp.where(spare[m], moved * SCALE, here)


def flux(change):
    return change / (SCALE * SCALE + change * change)


def rows_at(j, by=0):
    if isinstance(j, int):
        return slice(TOP + 8 * j + by, TOP + 8 * j + by + 8)
    return pl.ds(pl.multiple_of(8 * j, 8) + TOP + by, 8)


def put(ref, p, tiles):
    for j in range(TILES):
        ref[p, rows_at(j), :] = tiles[j]
    last = SEG_ROWS - 8 * (TILES - 1) - 1
    ref[p, TOP - 1 : TOP, :] = pltpu.roll(tiles[-1], WIDE, 1)[last : last + 1]
    ref[p, TOP + SEG_ROWS : TOP + SEG_ROWS + 1, :] = pltpu.roll(tiles[0], LANES - WIDE, 1)[0:1]


def take(ref, p, by=0):
    return [ref[p, rows_at(j, by), :] for j in range(TILES)]


class Tile:
    def __init__(self):
        self.block = lax.axis_index("depth") // GROUP
        tile = lax.axis_index("depth") % GROUP
        self.start = TILE * (tile % 4) - HALO
        local = (lane_index() - self.start + LANES) % LANES
        column = local % WIDE
        first, last = tile == 0, tile == GROUP - 1
        self.at_first = jnp.logical_and(column == HALO, first)
        self.at_last = jnp.logical_and(column == HALO + TILE - 1, last)
        self.open_face = jnp.where(
            jnp.logical_or(self.at_last, jnp.logical_and(column == HALO - 1, first)), 0.0, 1.0
        )
        row = lax.broadcasted_iota(jnp.int32, (8, LANES), 0)
        self.local = local
        self.segment = [(local >= WIDE * k) & (local < WIDE * (k + 1)) for k in range(SEGS)]
        self.top = self.segment[0] & (row < HALO)
        self.bottom = self.segment[2] & (row < HALO)
        self.foot = self.segment[1] & (row >= 3)

    def unpack(self, raw, start):
        def load(by):
            return raw[pl.ds(start + by, 8), :]

        lines = [load(8 * j) for j in range(TILES - 1)]
        zeroth, end = lines[0], load(RAW_ROWS - 8)
        tiles = []
        for j in range(TILES - 1):
            first = load(8 * j - HALO) if j else pltpu.roll(zeroth, HALO, 0)
            tiles.append(jnp.where(self.segment[0], first, lines[j]))
        foot = pltpu.roll(pltpu.roll(end, LANES - WIDE, 1), 6, 0)
        rest = jnp.where(self.foot, foot, pltpu.roll(end, 3, 0))
        tiles.append(jnp.where(self.segment[0], pltpu.roll(end, 7, 0), rest))
        halo = None
        for g in range(WIDE // 8):
            moved = pltpu.roll(lines[g], LANES - SPARE + 8 * g, 1)
            halo = moved if halo is None else jnp.where(self.local >= 8 * g, moved, halo)
        below = pltpu.roll(pltpu.roll(halo, 2 * WIDE, 1), HALO, 0)
        tiles[0] = jnp.where(self.top, halo, tiles[0])
        tiles[-1] = jnp.where(self.bottom, below, tiles[-1])
        return tiles


def diffuse(src, p, dst, to, fluxes, slot, flux_nearer, tile):
    f = take(src, p)
    below = take(src, p, 1)
    deeper = take(src, p + 1)
    flux_deeper = [flux(deeper[j] - f[j]) for j in range(TILES)]
    row = [flux(below[j] - f[j]) for j in range(TILES)]
    for j in range(TILES):
        fluxes[slot, rows_at(j), :] = row[j]
    last = SEG_ROWS - 8 * (TILES - 1) - 1
    fluxes[slot, TOP - 1 : TOP, :] = pltpu.roll(row[-1], WIDE, 1)[last : last + 1]
    row_prev = take(fluxes, slot, -1)
    new = []
    for j in range(TILES):
        col = flux((pltpu.roll(f[j], LANES - 1, 1) - f[j]) * tile.open_face)
        total = flux_deeper[j] - flux_nearer[j]
        total = total + (row[j] - row_prev[j])
        total = total + (col - pltpu.roll(col, 1, 1))
        new.append(f[j] + total)
    put(dst, to, new)
    return flux_deeper


def first_flux(src, p):
    here, deeper = take(src, p), take(src, p + 1)
    return [flux(deeper[j] - here[j]) for j in range(TILES)]


ALONG_ROWS = lax.GatherDimensionNumbers(
    offset_dims=(),
    collapsed_slice_dims=(0,),
    start_index_map=(0,),
    operand_batching_dims=(1,),
    start_indices_batching_dims=(1,),
)


def along_rows(x, k):
    return lax.gather(
        x, k[..., None], ALONG_ROWS, (1, 1), mode=lax.GatherScatterMode.PROMISE_IN_BOUNDS
    )


def tables(transfer):
    even, odd = [], []
    for c in range(4):
        for half, first in ((even, 0), (odd, 1)):
            knots = transfer[pl.ds(first, 8, stride=2), :]
            half.append(jnp.broadcast_to(knots[:, c : c + 1], (8, LANES)))
    return even, odd


def shade(src, p, j, carry, lookup, tile):
    red, green, blue, remaining = carry
    even, odd = lookup
    f = src[p, rows_at(j), :]
    depth = src[p + 1, rows_at(j), :] - src[p - 1, rows_at(j), :]
    row = src[p, rows_at(j, 1), :] - src[p, rows_at(j, -1), :]
    right = jnp.where(tile.at_last, f, pltpu.roll(f, LANES - 1, 1))
    left = jnp.where(tile.at_first, f, pltpu.roll(f, 1, 1))
    col = right - left
    square = depth * depth + row * row + col * col + SCALE * SCALE
    gain = 1.0 - AMBIENT
    along = jnp.abs(0.64 * gain * depth + 0.6 * gain * row + 0.48 * gain * col)
    shading = AMBIENT + along * lax.rsqrt(square)
    position = f * ((KNOTS - 1) / UPPER_DENSITY / SCALE)
    k = position.astype(jnp.int32)
    frac = position - k.astype(jnp.float32)
    near_odd = jnp.bitwise_and(lax.shift_right_logical(k, 1), 7)
    near_even = jnp.bitwise_and(lax.shift_right_logical(k + 1, 1), 7)
    weight_odd = jnp.where(jnp.bitwise_and(k, 1) == 0, frac, 1.0 - frac)
    mixed = []
    for c in range(4):
        low = along_rows(even[c], near_even)
        mixed.append(low + weight_odd * (along_rows(odd[c], near_odd) - low))
    kept = jnp.exp(mixed[3] * (-OPTICAL_DEPTH / (DEEP * BLOCKS)))
    weight = remaining * (1.0 - kept) * shading
    return (
        red + weight * mixed[0],
        green + weight * mixed[1],
        blue + weight * mixed[2],
        remaining * kept,
    )


def inner_kernel(mine, knots, out, fa, fb, fluxes, sums):
    tile = Tile()
    zero = jnp.zeros((8, LANES), jnp.float32)
    is_first = tile.block == 0

    def fill(i, carry):
        for u in range(2):
            for p in range(PLANES):
                k = 2 * i + u
                put(fa, FRONT + PLANES * k + p, tile.unpack(mine, CHUNK * k + RAW_ROWS * p))
        return carry

    lax.fori_loop(0, GROUP // 2, fill, 0)
    for i in range(HALO):
        for j in range(TILES):
            plane = fa[FRONT + DEEP - HALO + i, rows_at(j), :]
            out[TAIL + i, 8 * j : 8 * j + 8, :] = plane

    @pl.when(is_first)
    def _():
        for i in range(HALO):
            fa[FRONT - 1 - i] = fa[FRONT + i]

    src, dst = fa, fb
    for sweep in range(PASSES):
        lo, hi = FRONT + sweep + 1, FRONT + DEEP - 1 - sweep

        @pl.when(is_first)
        def _(src=src, dst=dst, lo=lo):
            carry = first_flux(src, lo - 5)
            for u in range(4):
                p = lo - 4 + u
                carry = diffuse(src, p, dst, p, fluxes, u, carry, tile)

        count = hi - lo
        unroll = 6 if count % 6 == 0 else UNROLL

        def step(i, carry, src=src, dst=dst, lo=lo, unroll=unroll):
            for u in range(unroll):
                p = lo + unroll * i + u
                carry = diffuse(src, p, dst, p, fluxes, u, carry, tile)
            return carry

        whole = count // unroll
        carry = lax.fori_loop(0, whole, step, first_flux(src, lo - 1))
        for u in range(count - unroll * whole):
            p = lo + unroll * whole + u
            carry = diffuse(src, p, dst, p, fluxes, u, carry, tile)
        for i in range(2):
            for j in range(TILES):
                out[2 * sweep + i, 8 * j : 8 * j + 8, :] = dst[hi - 2 + i, rows_at(j), :]
        src, dst = dst, src

    lookup = tables(knots)
    start = (zero, zero, zero, zero + 1.0)

    def rows(j):
        return pl.ds(pl.multiple_of(8 * j, 8), 8)

    @pl.when(is_first)
    def _():
        def shaded(j, unused):
            carry = start
            for u in range(HALO):
                carry = shade(src, FRONT + u, j, carry, lookup, tile)
            for c in range(4):
                sums[c, rows(j), :] = carry[c]
            return unused

        lax.fori_loop(0, TILES, shaded, 0)

    @pl.when(jnp.logical_not(is_first))
    def _():
        for c in range(4):
            for j in range(TILES):
                sums[c, 8 * j : 8 * j + 8, :] = start[c]

    def shaded(j, unused):
        def planes(i, carry):
            for u in range(SHADED):
                p = FRONT + HALO + SHADED * i + u
                carry = shade(src, p, j, carry, lookup, tile)
            return carry

        carry = tuple(sums[c, rows(j), :] for c in range(4))
        carry = lax.fori_loop(0, (DEEP - 2 * HALO) // SHADED, planes, carry)
        for c in range(4):
            out[2 * PASSES + c, rows(j), :] = carry[c]
        return unused

    lax.fori_loop(0, TILES, shaded, 0)


def outer_kernel(after, inner, knots, out, fa, fb, fluxes):
    tile = Tile()
    lookup = tables(knots)
    is_last = tile.block == BLOCKS - 1

    def tail(i):
        return [inner[TAIL + i, 8 * j : 8 * j + 8, :] for j in range(TILES)]

    for i in range(2):
        put(fa, i, tail(HALO - 2 + i))
    for i in range(2 * HALO):
        k, p = divmod(i, PLANES)
        plane = tile.unpack(after, CHUNK * k + RAW_ROWS * p)
        if i < HALO:
            mirror = tail(HALO - 1 - i)
            plane = [jnp.where(is_last, mirror[j], plane[j]) for j in range(TILES)]
        put(fa, 2 + i, plane)

    src, dst = fa, fb
    for sweep in range(PASSES):
        carry = first_flux(src, 0)
        for i in range(2 * HALO):
            carry = diffuse(src, i + 1, dst, i + 2, fluxes, i, carry, tile)
        for i in range(2):
            rest = [inner[2 * sweep + i, 8 * j : 8 * j + 8, :] for j in range(TILES)]
            put(dst, i, rest)
        src, dst = dst, src

    lane = lane_index()
    for j in range(TILES):
        sums = tuple(inner[2 * PASSES + c, 8 * j : 8 * j + 8, :] for c in range(4))
        for i in range(2 * HALO):
            if i == HALO:
                own = sums
            sums = shade(src, i + 1, j, sums, lookup, tile)
        sums = [jnp.where(is_last, own[c], sums[c]) for c in range(4)]
        for k in range(SEGS):
            value = None
            for c in range(4):
                by = TILE * c - WIDE * k - HALO - tile.start + LANES * 2
                moved = pltpu.roll(sums[c], lax.rem(by, LANES), 1)
                value = moved if value is None else jnp.where(lane >= TILE * c, moved, value)
            first = SEG_ROWS * k + 8 * j - HALO
            lo, hi = max(first, 0), min(first + min(8, SEG_ROWS - 8 * j), BAND)
            if lo < hi:
                out[lo:hi, :] = value[lo - first : hi - first]


def gather_kernel(parts, out):
    lane = lane_index(GROUP)
    total = jnp.zeros((GROUP, LANES), jnp.float32)
    remaining = jnp.ones((GROUP, LANES), jnp.float32)
    for b in range(BLOCKS):
        v = parts[GROUP * b : GROUP * (b + 1)]
        kept = v
        for c in range(3):
            kept = jnp.where(
                jnp.logical_and(lane >= TILE * c, lane < TILE * (c + 1)),
                pltpu.roll(v, TILE * (c + 1), 1),
                kept,
            )
        total = total + remaining * v
        remaining = remaining * kept
    total = jnp.where(lane >= 3 * TILE, 1.0 - remaining, total)
    turned = [total] + [pltpu.roll(total, TILE * s, 1) for s in range(1, 4)]
    for c in range(4):
        for t in range(GROUP):
            m = t % 4
            out[c, :, TILE * t : TILE * (t + 1)] = turned[(m - c) % 4][
                t : t + 1, TILE * m : TILE * (m + 1)
            ]


def call(kernel, shape, scratch, *operands, **options):
    spec = pl.BlockSpec(memory_space=VMEM)
    operands = [pltpu.with_memory_space_constraint(x, VMEM) for x in operands]
    return pl.pallas_call(
        kernel,
        out_shape=VMEM(shape, jnp.float32),
        in_specs=[spec] * len(operands),
        out_specs=spec,
        scratch_shapes=[VMEM(s, jnp.float32) for s in scratch],
        **options,
    )(*operands)


def shifted(value, axis, by):
    size = lax.axis_size(axis)
    pairs = [(i, i + by) for i in range(size) if 0 <= i + by < size]
    return lax.ppermute(value, axis, pairs)


def rendered(density, transfer_table):
    bands = lax.axis_size("rows")
    edge = VMEM((PLANES, HALO, COLS), jnp.float32)
    one, two = pl.pallas_call(
        slice_kernel,
        out_shape=[edge, edge],
        in_specs=[pl.BlockSpec(memory_space=pl.ANY)],
        out_specs=[pl.BlockSpec(memory_space=VMEM)] * 2,
        scratch_shapes=[
            VMEM((2, PLANES, 8, COLS), jnp.float32),
            pltpu.SemaphoreType.DMA((2,)),
        ],
        name="slice_kernel",
    )(density)
    pairs = [(i, i + 1) for i in range(0, bands, 2)]
    from_one = lax.ppermute(one, "rows", pairs + [(b, a) for a, b in pairs])
    pairs = [(i, i + 1) for i in range(1, bands - 1, 2)]
    from_two = lax.ppermute(two, "rows", pairs + [(b, a) for a, b in pairs])
    chunks = (GROUP * CHUNK, LANES)
    cut = pl.pallas_call(
        pack_kernel,
        out_shape=VMEM(chunks, jnp.float32),
        in_specs=[pl.BlockSpec(memory_space=pl.ANY)],
        out_specs=pl.BlockSpec(memory_space=VMEM),
        scratch_shapes=[
            VMEM((PLANES, BAND + 8, COLS), jnp.float32),
            pltpu.SemaphoreType.DMA((PLANES, PARTS)),
        ],
        name="pack_kernel",
    )(density)
    sent = call(
        halo_kernel,
        chunks,
        [(PLANES, 8, COLS)],
        cut,
        two,
        from_one,
        from_two,
        input_output_aliases={0: 0},
    )
    groups = [[GROUP * b + i for i in range(GROUP)] for b in range(BLOCKS)]
    sent = sent.reshape(GROUP, CHUNK, 1, LANES)
    mine = lax.all_to_all(sent, "depth", 0, 0, axis_index_groups=groups, tiled=True)
    mine = mine.reshape(GROUP * CHUNK, LANES)
    after = shifted(mine[: 2 * HALO // PLANES * CHUNK], "depth", -GROUP)
    knots = transfer_table.T
    field = (FRONT + DEEP, TALL, LANES)
    inner = call(
        inner_kernel,
        (TAIL + HALO, LINES, LANES),
        [field, field, (UNROLL, TALL, LANES), (4, LINES, LANES)],
        mine,
        knots,
    )
    few = (2 * HALO + 2, TALL, LANES)
    partial = call(
        outer_kernel,
        (BAND, LANES),
        [few, few, (2 * HALO, TALL, LANES)],
        after,
        inner,
        knots,
    )
    parts = lax.all_to_all(partial, "depth", 0, 0, tiled=True)
    spec = pl.BlockSpec(memory_space=VMEM)
    return pl.pallas_call(
        gather_kernel,
        out_shape=jax.ShapeDtypeStruct((4, 1, COLS), jnp.float32),
        in_specs=[spec],
        out_specs=spec,
        name="gather_kernel",
    )(pltpu.with_memory_space_constraint(parts, VMEM))


def solution(mesh):
    placed = (P("depth", "rows", None), P())
    return jax.shard_map(
        rendered,
        mesh=mesh,
        in_specs=placed,
        out_specs=P(None, ("rows", "depth"), None),
        check_vma=False,
    )
```

```python
import jax
import jax.numpy as jnp
from jax import lax
from jax.experimental import pallas as pl
from jax.experimental.pallas import tpu as pltpu
from jax.sharding import PartitionSpec as P


PASSES = 3
KNOTS = 16
TIME_STEP = 0.15
OPTICAL_DEPTH = 3.0
UPPER_DENSITY = 6.0
AMBIENT = 0.35
SCALE = TIME_STEP**-0.5

GROUP = 16
BLOCKS = 8
HALO = 4
BAND = 128
COLS = 512
TILE = COLS // GROUP
WIDE = TILE + 2 * HALO
SEGS = 3
SEG_ROWS = 46
RAW_ROWS = 43
TILES = 6
LINES = 8 * TILES
PLANES = 2
DEEP = GROUP * PLANES
LANES = 128
TOP = 8
TALL = 64
FRONT = HALO
CHUNK = 2 * RAW_ROWS
SPARE = SEGS * WIDE
TAIL = 2 * PASSES + 4
PARTS = 4
UNROLL = 7
SHADED = 8
VMEM = pltpu.VMEM


def lane_index(rows=8):
    return lax.broadcasted_iota(jnp.int32, (rows, LANES), 1)


def window_masks():
    lane = lane_index()
    segment, left, right, spare = [], [], [], []
    for m in range(4):
        local = (lane - (TILE * m - HALO)) % LANES
        segment.append([(local >= WIDE * k) & (local < WIDE * (k + 1)) for k in range(SEGS)])
        column = local % WIDE
        left.append(column < HALO)
        right.append(column >= WIDE - HALO)
        spare.append(local >= SPARE)
    return segment, left, right, spare


def windows(tiles, joined, left, right):
    for t in range(GROUP):
        q, m = divmod(t, 4)
        value = joined(tiles, q, m)
        if m == 0 and q > 0:
            value = jnp.where(left[m], joined(tiles, q - 1, m), value)
        if m == 3 and q < 3:
            value = jnp.where(right[m], joined(tiles, q + 1, m), value)
        yield t, m, value


def slice_kernel(density, one, two, ends, sems):
    even = lax.axis_index("rows") % 2 == 0
    copies = []
    for i, row in enumerate((0, BAND - 8)):
        source = density.at[:, pl.ds(row, 8), :]
        copies.append(pltpu.make_async_copy(source, ends.at[i], sems.at[i]))
    for copy in copies:
        copy.start()
    for copy in copies:
        copy.wait()
    for p in range(PLANES):
        first = ends[0, p, 0:HALO, :]
        last = ends[1, p, 8 - HALO : 8, :]
        one[p] = jnp.where(even, last, first)
        two[p] = jnp.where(even, first, last)


def pack_kernel(density, out, own, sems):
    part = BAND // PARTS
    copies = []
    for p in range(PLANES):
        for i in range(PARTS):
            at = pl.ds(part * i, part)
            copies.append(
                pltpu.make_async_copy(density.at[p, at, :], own.at[p, at, :], sems.at[p, i])
            )
    for copy in copies:
        copy.start()
    for p in range(PLANES):
        own[p, BAND:, :] = jnp.zeros((8, COLS), jnp.float32)
    segment, left, right, _ = window_masks()

    def joined(rolled, q, m):
        rest = jnp.where(segment[m][1], rolled[1][q], rolled[2][q])
        return jnp.where(segment[m][0], rolled[0][q], rest)

    for p in range(PLANES):
        for copy in copies[PARTS * p : PARTS * (p + 1)]:
            copy.wait()
        for j in range(TILES):
            count = min(8, RAW_ROWS - 8 * j)
            rolled = []
            for k in range(SEGS):
                start = RAW_ROWS * k + 8 * j
                rows = own[p, start : start + 8, :]
                tiles = [rows[:, LANES * q : LANES * (q + 1)] for q in range(4)]
                rolled.append([pltpu.roll(x, WIDE * k, 1) if k else x for x in tiles])
            for t, m, value in windows(rolled, joined, left, right):
                start = CHUNK * t + RAW_ROWS * p + 8 * j
                out[start : start + count, :] = (value * SCALE)[:count]


def halo_kernel(sent, two, from_one, from_two, out, edge):
    band = lax.axis_index("rows")
    bands = lax.axis_size("rows")
    even = band % 2 == 0

    def above(source):
        for p in range(PLANES):
            edge[p, 0:HALO, :] = source[p]

    def below(source):
        for p in range(PLANES):
            edge[p, HALO : 2 * HALO, :] = source[p]

    @pl.when(even)
    def _():
        below(from_one)

    @pl.when(jnp.logical_not(even))
    def _():
        above(from_one)

    @pl.when(even & (band > 0))
    def _():
        above(from_two)

    @pl.when(jnp.logical_not(even) & (band < bands - 1))
    def _():
        below(from_two)

    @pl.when(band == 0)
    def _():
        for p in range(PLANES):
            for i in range(HALO):
                edge[p, HALO - 1 - i : HALO - i, :] = two[p, i : i + 1, :]

    @pl.when(band == bands - 1)
    def _():
        for p in range(PLANES):
            for i in range(HALO):
                edge[p, HALO + i : HALO + i + 1, :] = two[p, HALO - 1 - i : HALO - i, :]

    _, left, right, spare = window_masks()

    def joined(tiles, q, m):
        return tiles[q]

    for p in range(PLANES):
        tiles = [edge[p, :, LANES * q : LANES * (q + 1)] for q in range(4)]
        for t, m, value in windows(tiles, joined, left, right):
            for g in range(WIDE // 8):
                start = CHUNK * t + RAW_ROWS * p + 8 * g
                moved = pltpu.roll(value, SPARE - 8 * g, 1)
                here = sent[start : start + 8, :]
                out[start : start + 8, :] = jnp.where(spare[m], moved * SCALE, here)


def flux(change):
    return change / (SCALE * SCALE + change * change)


def rows_at(j, by=0):
    if isinstance(j, int):
        return slice(TOP + 8 * j + by, TOP + 8 * j + by + 8)
    return pl.ds(pl.multiple_of(8 * j, 8) + TOP + by, 8)


def put(ref, p, tiles):
    for j in range(TILES):
        ref[p, rows_at(j), :] = tiles[j]
    last = SEG_ROWS - 8 * (TILES - 1) - 1
    ref[p, TOP - 1 : TOP, :] = pltpu.roll(tiles[-1], WIDE, 1)[last : last + 1]
    ref[p, TOP + SEG_ROWS : TOP + SEG_ROWS + 1, :] = pltpu.roll(tiles[0], LANES - WIDE, 1)[0:1]


def take(ref, p, by=0):
    return [ref[p, rows_at(j, by), :] for j in range(TILES)]


class Tile:
    def __init__(self):
        self.block = lax.axis_index("depth") // GROUP
        tile = lax.axis_index("depth") % GROUP
        self.start = TILE * (tile % 4) - HALO
        local = (lane_index() - self.start + LANES) % LANES
        column = local % WIDE
        first, last = tile == 0, tile == GROUP - 1
        self.at_first = jnp.logical_and(column == HALO, first)
        self.at_last = jnp.logical_and(column == HALO + TILE - 1, last)
        self.open_face = jnp.where(
            jnp.logical_or(self.at_last, jnp.logical_and(column == HALO - 1, first)), 0.0, 1.0
        )
        row = lax.broadcasted_iota(jnp.int32, (8, LANES), 0)
        self.local = local
        self.segment = [(local >= WIDE * k) & (local < WIDE * (k + 1)) for k in range(SEGS)]
        self.top = self.segment[0] & (row < HALO)
        self.bottom = self.segment[2] & (row < HALO)
        self.head = self.segment[1] & (row == 0)
        self.foot = self.segment[1] & (row >= 4) & (row < 6)

    def unpack(self, raw, start):
        def load(by):
            return raw[pl.ds(start + by, 8), :]

        zeroth, end = load(0), load(RAW_ROWS - 8)
        tiles = []
        for j in range(TILES):
            if j == 0:
                parts = (pltpu.roll(zeroth, 4, 0), pltpu.roll(zeroth, 1, 0), load(2))
            elif j < TILES - 1:
                parts = (load(8 * j - 4), load(8 * j - 1), load(8 * j + 2))
            else:
                parts = (pltpu.roll(end, 7, 0), pltpu.roll(end, 4, 0), end)
            rest = jnp.where(self.segment[1], parts[1], parts[2])
            tiles.append(jnp.where(self.segment[0], parts[0], rest))
        halo = None
        for g in range(WIDE // 8):
            rows = load(8 * g) if g else zeroth
            moved = pltpu.roll(rows, LANES - SPARE + 8 * g, 1)
            halo = moved if halo is None else jnp.where(self.local >= 8 * g, moved, halo)
        head = pltpu.roll(pltpu.roll(end, WIDE, 1), 1, 0)
        foot = pltpu.roll(pltpu.roll(zeroth, LANES - WIDE, 1), 4, 0)
        below = pltpu.roll(pltpu.roll(halo, 2 * WIDE, 1), 4, 0)
        tiles[0] = jnp.where(self.top, halo, jnp.where(self.head, head, tiles[0]))
        tiles[-1] = jnp.where(self.bottom, below, jnp.where(self.foot, foot, tiles[-1]))
        return tiles


def diffuse(src, p, dst, to, fluxes, slot, flux_nearer, tile):
    f = take(src, p)
    below = take(src, p, 1)
    deeper = take(src, p + 1)
    flux_deeper = [flux(deeper[j] - f[j]) for j in range(TILES)]
    row = [flux(below[j] - f[j]) for j in range(TILES)]
    for j in range(TILES):
        fluxes[slot, rows_at(j), :] = row[j]
    last = SEG_ROWS - 8 * (TILES - 1) - 1
    fluxes[slot, TOP - 1 : TOP, :] = pltpu.roll(row[-1], WIDE, 1)[last : last + 1]
    row_prev = take(fluxes, slot, -1)
    new = []
    for j in range(TILES):
        col = flux((pltpu.roll(f[j], LANES - 1, 1) - f[j]) * tile.open_face)
        total = flux_deeper[j] - flux_nearer[j]
        total = total + (row[j] - row_prev[j])
        total = total + (col - pltpu.roll(col, 1, 1))
        new.append(f[j] + total)
    put(dst, to, new)
    return flux_deeper


def first_flux(src, p):
    here, deeper = take(src, p), take(src, p + 1)
    return [flux(deeper[j] - here[j]) for j in range(TILES)]


ALONG_ROWS = lax.GatherDimensionNumbers(
    offset_dims=(),
    collapsed_slice_dims=(0,),
    start_index_map=(0,),
    operand_batching_dims=(1,),
    start_indices_batching_dims=(1,),
)


def along_rows(x, k):
    return lax.gather(
        x, k[..., None], ALONG_ROWS, (1, 1), mode=lax.GatherScatterMode.PROMISE_IN_BOUNDS
    )


def tables(transfer):
    even, odd = [], []
    for c in range(4):
        for half, first in ((even, 0), (odd, 1)):
            knots = transfer[pl.ds(first, 8, stride=2), :]
            half.append(jnp.broadcast_to(knots[:, c : c + 1], (8, LANES)))
    return even, odd


def shade(src, p, j, carry, lookup, tile):
    red, green, blue, remaining = carry
    even, odd = lookup
    f = src[p, rows_at(j), :]
    depth = src[p + 1, rows_at(j), :] - src[p - 1, rows_at(j), :]
    row = src[p, rows_at(j, 1), :] - src[p, rows_at(j, -1), :]
    right = jnp.where(tile.at_last, f, pltpu.roll(f, LANES - 1, 1))
    left = jnp.where(tile.at_first, f, pltpu.roll(f, 1, 1))
    col = right - left
    square = depth * depth + row * row + col * col + SCALE * SCALE
    gain = 1.0 - AMBIENT
    along = jnp.abs(0.64 * gain * depth + 0.6 * gain * row + 0.48 * gain * col)
    shading = AMBIENT + along * lax.rsqrt(square)
    position = f * ((KNOTS - 1) / UPPER_DENSITY / SCALE)
    k = position.astype(jnp.int32)
    frac = position - k.astype(jnp.float32)
    near_odd = jnp.bitwise_and(lax.shift_right_logical(k, 1), 7)
    near_even = jnp.bitwise_and(lax.shift_right_logical(k + 1, 1), 7)
    weight_odd = jnp.where(jnp.bitwise_and(k, 1) == 0, frac, 1.0 - frac)
    mixed = []
    for c in range(4):
        low = along_rows(even[c], near_even)
        mixed.append(low + weight_odd * (along_rows(odd[c], near_odd) - low))
    kept = jnp.exp(mixed[3] * (-OPTICAL_DEPTH / (DEEP * BLOCKS)))
    weight = remaining * (1.0 - kept) * shading
    return (
        red + weight * mixed[0],
        green + weight * mixed[1],
        blue + weight * mixed[2],
        remaining * kept,
    )


def inner_kernel(mine, knots, out, fa, fb, fluxes, sums):
    tile = Tile()
    zero = jnp.zeros((8, LANES), jnp.float32)
    is_first = tile.block == 0

    def fill(i, carry):
        for u in range(8):
            for p in range(PLANES):
                k = 8 * i + u
                put(fa, FRONT + PLANES * k + p, tile.unpack(mine, CHUNK * k + RAW_ROWS * p))
        return carry

    lax.fori_loop(0, GROUP // 8, fill, 0)
    for i in range(HALO):
        for j in range(TILES):
            plane = fa[FRONT + DEEP - HALO + i, rows_at(j), :]
            out[TAIL + i, 8 * j : 8 * j + 8, :] = plane

    @pl.when(is_first)
    def _():
        for i in range(HALO):
            fa[FRONT - 1 - i] = fa[FRONT + i]

    src, dst = fa, fb
    for sweep in range(PASSES):
        lo, hi = FRONT + sweep + 1, FRONT + DEEP - 1 - sweep

        @pl.when(is_first)
        def _(src=src, dst=dst, lo=lo):
            carry = first_flux(src, lo - 5)
            for u in range(4):
                p = lo - 4 + u
                carry = diffuse(src, p, dst, p, fluxes, u, carry, tile)

        count = hi - lo
        unroll = 6 if count % 6 == 0 else UNROLL

        def step(i, carry, src=src, dst=dst, lo=lo, unroll=unroll):
            for u in range(unroll):
                p = lo + unroll * i + u
                carry = diffuse(src, p, dst, p, fluxes, u, carry, tile)
            return carry

        whole = count // unroll
        carry = lax.fori_loop(0, whole, step, first_flux(src, lo - 1))
        for u in range(count - unroll * whole):
            p = lo + unroll * whole + u
            carry = diffuse(src, p, dst, p, fluxes, u, carry, tile)
        for i in range(2):
            for j in range(TILES):
                out[2 * sweep + i, 8 * j : 8 * j + 8, :] = dst[hi - 2 + i, rows_at(j), :]
        src, dst = dst, src

    lookup = tables(knots)
    start = (zero, zero, zero, zero + 1.0)

    def rows(j):
        return pl.ds(pl.multiple_of(8 * j, 8), 8)

    @pl.when(is_first)
    def _():
        def shaded(j, unused):
            carry = start
            for u in range(HALO):
                carry = shade(src, FRONT + u, j, carry, lookup, tile)
            for c in range(4):
                sums[c, rows(j), :] = carry[c]
            return unused

        lax.fori_loop(0, TILES, shaded, 0)

    @pl.when(jnp.logical_not(is_first))
    def _():
        for c in range(4):
            for j in range(TILES):
                sums[c, 8 * j : 8 * j + 8, :] = start[c]

    def shaded(j, unused):
        def planes(i, carry):
            for u in range(SHADED):
                p = FRONT + HALO + SHADED * i + u
                carry = shade(src, p, j, carry, lookup, tile)
            return carry

        carry = tuple(sums[c, rows(j), :] for c in range(4))
        carry = lax.fori_loop(0, (DEEP - 2 * HALO) // SHADED, planes, carry)
        for c in range(4):
            out[2 * PASSES + c, rows(j), :] = carry[c]
        return unused

    lax.fori_loop(0, TILES, shaded, 0)


def outer_kernel(after, inner, knots, out, fa, fb, fluxes):
    tile = Tile()
    lookup = tables(knots)
    is_last = tile.block == BLOCKS - 1

    def tail(to, i):
        put(fa, to, [inner[TAIL + i, 8 * j : 8 * j + 8, :] for j in range(TILES)])

    for i in range(2):
        tail(i, HALO - 2 + i)

    @pl.when(jnp.logical_not(is_last))
    def _():
        for i in range(2 * HALO):
            k, p = divmod(i, PLANES)
            put(fa, 2 + i, tile.unpack(after, CHUNK * k + RAW_ROWS * p))

    @pl.when(is_last)
    def _():
        for i in range(2 * HALO):
            tail(2 + i, max(HALO - 1 - i, 0))

    src, dst = fa, fb
    for sweep in range(PASSES):
        carry = first_flux(src, 0)
        for i in range(2 * HALO):
            carry = diffuse(src, i + 1, dst, i + 2, fluxes, i, carry, tile)
        for i in range(2):
            rest = [inner[2 * sweep + i, 8 * j : 8 * j + 8, :] for j in range(TILES)]
            put(dst, i, rest)
        src, dst = dst, src

    lane = lane_index()
    for j in range(TILES):
        sums = tuple(inner[2 * PASSES + c, 8 * j : 8 * j + 8, :] for c in range(4))
        for i in range(2 * HALO):
            if i == HALO:
                own = sums
            sums = shade(src, i + 1, j, sums, lookup, tile)
        sums = [jnp.where(is_last, own[c], sums[c]) for c in range(4)]
        for k in range(SEGS):
            value = None
            for c in range(4):
                by = TILE * c - WIDE * k - HALO - tile.start + LANES * 2
                moved = pltpu.roll(sums[c], lax.rem(by, LANES), 1)
                value = moved if value is None else jnp.where(lane >= TILE * c, moved, value)
            first = SEG_ROWS * k + 8 * j - HALO
            lo, hi = max(first, 0), min(first + min(8, SEG_ROWS - 8 * j), BAND)
            if lo < hi:
                out[lo:hi, :] = value[lo - first : hi - first]


def gather_kernel(parts, out):
    lane = lane_index(GROUP)
    total = jnp.zeros((GROUP, LANES), jnp.float32)
    remaining = jnp.ones((GROUP, LANES), jnp.float32)
    for b in range(BLOCKS):
        v = parts[GROUP * b : GROUP * (b + 1)]
        kept = v
        for c in range(3):
            kept = jnp.where(
                jnp.logical_and(lane >= TILE * c, lane < TILE * (c + 1)),
                pltpu.roll(v, TILE * (c + 1), 1),
                kept,
            )
        total = total + remaining * v
        remaining = remaining * kept
    total = jnp.where(lane >= 3 * TILE, 1.0 - remaining, total)
    turned = [total] + [pltpu.roll(total, TILE * s, 1) for s in range(1, 4)]
    for c in range(4):
        for t in range(GROUP):
            m = t % 4
            out[c, :, TILE * t : TILE * (t + 1)] = turned[(m - c) % 4][
                t : t + 1, TILE * m : TILE * (m + 1)
            ]


def call(kernel, shape, scratch, *operands, **options):
    spec = pl.BlockSpec(memory_space=VMEM)
    operands = [pltpu.with_memory_space_constraint(x, VMEM) for x in operands]
    return pl.pallas_call(
        kernel,
        out_shape=VMEM(shape, jnp.float32),
        in_specs=[spec] * len(operands),
        out_specs=spec,
        scratch_shapes=[VMEM(s, jnp.float32) for s in scratch],
        **options,
    )(*operands)


def shifted(value, axis, by):
    size = lax.axis_size(axis)
    pairs = [(i, i + by) for i in range(size) if 0 <= i + by < size]
    return lax.ppermute(value, axis, pairs)


def rendered(density, transfer_table):
    bands = lax.axis_size("rows")
    edge = VMEM((PLANES, HALO, COLS), jnp.float32)
    one, two = pl.pallas_call(
        slice_kernel,
        out_shape=[edge, edge],
        in_specs=[pl.BlockSpec(memory_space=pl.ANY)],
        out_specs=[pl.BlockSpec(memory_space=VMEM)] * 2,
        scratch_shapes=[
            VMEM((2, PLANES, 8, COLS), jnp.float32),
            pltpu.SemaphoreType.DMA((2,)),
        ],
        name="slice_kernel",
    )(density)
    pairs = [(i, i + 1) for i in range(0, bands, 2)]
    from_one = lax.ppermute(one, "rows", pairs + [(b, a) for a, b in pairs])
    pairs = [(i, i + 1) for i in range(1, bands - 1, 2)]
    from_two = lax.ppermute(two, "rows", pairs + [(b, a) for a, b in pairs])
    chunks = (GROUP * CHUNK, LANES)
    cut = pl.pallas_call(
        pack_kernel,
        out_shape=VMEM(chunks, jnp.float32),
        in_specs=[pl.BlockSpec(memory_space=pl.ANY)],
        out_specs=pl.BlockSpec(memory_space=VMEM),
        scratch_shapes=[
            VMEM((PLANES, BAND + 8, COLS), jnp.float32),
            pltpu.SemaphoreType.DMA((PLANES, PARTS)),
        ],
        name="pack_kernel",
    )(density)
    sent = call(
        halo_kernel,
        chunks,
        [(PLANES, 8, COLS)],
        cut,
        two,
        from_one,
        from_two,
        input_output_aliases={0: 0},
    )
    groups = [[GROUP * b + i for i in range(GROUP)] for b in range(BLOCKS)]
    sent = sent.reshape(GROUP, CHUNK, 1, LANES)
    mine = lax.all_to_all(sent, "depth", 0, 0, axis_index_groups=groups, tiled=True)
    mine = mine.reshape(GROUP * CHUNK, LANES)
    after = shifted(mine[: 2 * HALO // PLANES * CHUNK], "depth", -GROUP)
    knots = transfer_table.T
    field = (FRONT + DEEP, TALL, LANES)
    inner = call(
        inner_kernel,
        (TAIL + HALO, LINES, LANES),
        [field, field, (UNROLL, TALL, LANES), (4, LINES, LANES)],
        mine,
        knots,
    )
    few = (2 * HALO + 2, TALL, LANES)
    partial = call(
        outer_kernel,
        (BAND, LANES),
        [few, few, (2 * HALO, TALL, LANES)],
        after,
        inner,
        knots,
    )
    parts = lax.all_to_all(partial, "depth", 0, 0, tiled=True)
    spec = pl.BlockSpec(memory_space=VMEM)
    return pl.pallas_call(
        gather_kernel,
        out_shape=jax.ShapeDtypeStruct((4, 1, COLS), jnp.float32),
        in_specs=[spec],
        out_specs=spec,
        name="gather_kernel",
    )(pltpu.with_memory_space_constraint(parts, VMEM))


def solution(mesh):
    placed = (P("depth", "rows", None), P())
    return jax.shard_map(
        rendered,
        mesh=mesh,
        in_specs=placed,
        out_specs=P(None, ("rows", "depth"), None),
        check_vma=False,
    )
```

```python
import jax
import jax.numpy as jnp
from jax import lax
from jax.experimental import pallas as pl
from jax.experimental.pallas import tpu as pltpu
from jax.sharding import PartitionSpec as P


PASSES = 3
KNOTS = 16
TIME_STEP = 0.15
OPTICAL_DEPTH = 3.0
UPPER_DENSITY = 6.0
AMBIENT = 0.35
SCALE = TIME_STEP**-0.5

GROUP = 16
BLOCKS = 8
HALO = 4
BAND = 128
COLS = 512
TILE = COLS // GROUP
WIDE = TILE + 2 * HALO
SEGS = 3
SEG_ROWS = 46
RAW_ROWS = 43
TILES = 6
LINES = 8 * TILES
PLANES = 2
DEEP = GROUP * PLANES
LANES = 128
TOP = 8
TALL = 64
FRONT = HALO
CHUNK = 2 * RAW_ROWS
SPARE = SEGS * WIDE
TAIL = 2 * PASSES + 4
PARTS = 4
UNROLL = 7
SHADED = 8
VMEM = pltpu.VMEM


def lane_index(rows=8):
    return lax.broadcasted_iota(jnp.int32, (rows, LANES), 1)


def window_masks():
    lane = lane_index()
    segment, left, right, spare = [], [], [], []
    for m in range(4):
        local = (lane - (TILE * m - HALO)) % LANES
        segment.append([(local >= WIDE * k) & (local < WIDE * (k + 1)) for k in range(SEGS)])
        column = local % WIDE
        left.append(column < HALO)
        right.append(column >= WIDE - HALO)
        spare.append(local >= SPARE)
    return segment, left, right, spare


def windows(tiles, joined, left, right):
    for t in range(GROUP):
        q, m = divmod(t, 4)
        value = joined(tiles, q, m)
        if m == 0 and q > 0:
            value = jnp.where(left[m], joined(tiles, q - 1, m), value)
        if m == 3 and q < 3:
            value = jnp.where(right[m], joined(tiles, q + 1, m), value)
        yield t, m, value


def slice_kernel(density, one, two, ends, sems):
    even = lax.axis_index("rows") % 2 == 0
    copies = []
    for i, row in enumerate((0, BAND - 8)):
        source = density.at[:, pl.ds(row, 8), :]
        copies.append(pltpu.make_async_copy(source, ends.at[i], sems.at[i]))
    for copy in copies:
        copy.start()
    for copy in copies:
        copy.wait()
    for p in range(PLANES):
        first = ends[0, p, 0:HALO, :]
        last = ends[1, p, 8 - HALO : 8, :]
        one[p] = jnp.where(even, last, first)
        two[p] = jnp.where(even, first, last)


def pack_kernel(density, out, own, sems):
    part = BAND // PARTS
    copies = []
    for p in range(PLANES):
        for i in range(PARTS):
            at = pl.ds(part * i, part)
            copies.append(
                pltpu.make_async_copy(density.at[p, at, :], own.at[p, at, :], sems.at[p, i])
            )
    for copy in copies:
        copy.start()
    for p in range(PLANES):
        own[p, BAND:, :] = jnp.zeros((8, COLS), jnp.float32)
    segment, left, right, _ = window_masks()

    def joined(rolled, q, m):
        rest = jnp.where(segment[m][1], rolled[1][q], rolled[2][q])
        return jnp.where(segment[m][0], rolled[0][q], rest)

    for p in range(PLANES):
        for copy in copies[PARTS * p : PARTS * (p + 1)]:
            copy.wait()
        for j in range(TILES):
            count = min(8, RAW_ROWS - 8 * j)
            rolled = []
            for k in range(SEGS):
                start = RAW_ROWS * k + 8 * j
                rows = own[p, start : start + 8, :]
                tiles = [rows[:, LANES * q : LANES * (q + 1)] for q in range(4)]
                rolled.append([pltpu.roll(x, WIDE * k, 1) if k else x for x in tiles])
            for t, m, value in windows(rolled, joined, left, right):
                start = CHUNK * t + RAW_ROWS * p + 8 * j
                out[start : start + count, :] = (value * SCALE)[:count]


def halo_kernel(sent, two, from_one, from_two, out, edge):
    band = lax.axis_index("rows")
    bands = lax.axis_size("rows")
    even = band % 2 == 0

    def above(source):
        for p in range(PLANES):
            edge[p, 0:HALO, :] = source[p]

    def below(source):
        for p in range(PLANES):
            edge[p, HALO : 2 * HALO, :] = source[p]

    @pl.when(even)
    def _():
        below(from_one)

    @pl.when(jnp.logical_not(even))
    def _():
        above(from_one)

    @pl.when(even & (band > 0))
    def _():
        above(from_two)

    @pl.when(jnp.logical_not(even) & (band < bands - 1))
    def _():
        below(from_two)

    @pl.when(band == 0)
    def _():
        for p in range(PLANES):
            for i in range(HALO):
                edge[p, HALO - 1 - i : HALO - i, :] = two[p, i : i + 1, :]

    @pl.when(band == bands - 1)
    def _():
        for p in range(PLANES):
            for i in range(HALO):
                edge[p, HALO + i : HALO + i + 1, :] = two[p, HALO - 1 - i : HALO - i, :]

    _, left, right, spare = window_masks()

    def joined(tiles, q, m):
        return tiles[q]

    for p in range(PLANES):
        tiles = [edge[p, :, LANES * q : LANES * (q + 1)] for q in range(4)]
        for t, m, value in windows(tiles, joined, left, right):
            for g in range(WIDE // 8):
                start = CHUNK * t + RAW_ROWS * p + 8 * g
                moved = pltpu.roll(value, SPARE - 8 * g, 1)
                here = sent[start : start + 8, :]
                out[start : start + 8, :] = jnp.where(spare[m], moved * SCALE, here)


def flux(change):
    return change / (SCALE * SCALE + change * change)


def rows_at(j, by=0):
    if isinstance(j, int):
        return slice(TOP + 8 * j + by, TOP + 8 * j + by + 8)
    return pl.ds(pl.multiple_of(8 * j, 8) + TOP + by, 8)


def put(ref, p, tiles):
    for j in range(TILES):
        ref[p, rows_at(j), :] = tiles[j]
    last = SEG_ROWS - 8 * (TILES - 1) - 1
    ref[p, TOP - 1 : TOP, :] = pltpu.roll(tiles[-1], WIDE, 1)[last : last + 1]
    ref[p, TOP + SEG_ROWS : TOP + SEG_ROWS + 1, :] = pltpu.roll(tiles[0], LANES - WIDE, 1)[0:1]


def take(ref, p, by=0):
    return [ref[p, rows_at(j, by), :] for j in range(TILES)]


class Tile:
    def __init__(self):
        self.block = lax.axis_index("depth") // GROUP
        tile = lax.axis_index("depth") % GROUP
        self.start = TILE * (tile % 4) - HALO
        local = (lane_index() - self.start + LANES) % LANES
        column = local % WIDE
        first, last = tile == 0, tile == GROUP - 1
        self.at_first = jnp.logical_and(column == HALO, first)
        self.at_last = jnp.logical_and(column == HALO + TILE - 1, last)
        self.open_face = jnp.where(
            jnp.logical_or(self.at_last, jnp.logical_and(column == HALO - 1, first)), 0.0, 1.0
        )
        row = lax.broadcasted_iota(jnp.int32, (8, LANES), 0)
        self.local = local
        self.segment = [(local >= WIDE * k) & (local < WIDE * (k + 1)) for k in range(SEGS)]
        self.top = self.segment[0] & (row < HALO)
        self.bottom = self.segment[2] & (row < HALO)
        self.head = self.segment[1] & (row == 0)
        self.foot = self.segment[1] & (row >= 4) & (row < 6)

    def unpack(self, raw, start):
        def load(by):
            return raw[pl.ds(start + by, 8), :]

        zeroth, end = load(0), load(RAW_ROWS - 8)
        tiles = []
        for j in range(TILES):
            if j == 0:
                parts = (pltpu.roll(zeroth, 4, 0), pltpu.roll(zeroth, 1, 0), load(2))
            elif j < TILES - 1:
                parts = (load(8 * j - 4), load(8 * j - 1), load(8 * j + 2))
            else:
                parts = (pltpu.roll(end, 7, 0), pltpu.roll(end, 4, 0), end)
            rest = jnp.where(self.segment[1], parts[1], parts[2])
            tiles.append(jnp.where(self.segment[0], parts[0], rest))
        halo = None
        for g in range(WIDE // 8):
            rows = load(8 * g) if g else zeroth
            moved = pltpu.roll(rows, LANES - SPARE + 8 * g, 1)
            halo = moved if halo is None else jnp.where(self.local >= 8 * g, moved, halo)
        head = pltpu.roll(pltpu.roll(end, WIDE, 1), 1, 0)
        foot = pltpu.roll(pltpu.roll(zeroth, LANES - WIDE, 1), 4, 0)
        below = pltpu.roll(pltpu.roll(halo, 2 * WIDE, 1), 4, 0)
        tiles[0] = jnp.where(self.top, halo, jnp.where(self.head, head, tiles[0]))
        tiles[-1] = jnp.where(self.bottom, below, jnp.where(self.foot, foot, tiles[-1]))
        return tiles


def diffuse(src, p, dst, to, fluxes, slot, flux_nearer, tile):
    f = take(src, p)
    below = take(src, p, 1)
    deeper = take(src, p + 1)
    flux_deeper = [flux(deeper[j] - f[j]) for j in range(TILES)]
    row = [flux(below[j] - f[j]) for j in range(TILES)]
    for j in range(TILES):
        fluxes[slot, rows_at(j), :] = row[j]
    last = SEG_ROWS - 8 * (TILES - 1) - 1
    fluxes[slot, TOP - 1 : TOP, :] = pltpu.roll(row[-1], WIDE, 1)[last : last + 1]
    row_prev = take(fluxes, slot, -1)
    new = []
    for j in range(TILES):
        col = flux((pltpu.roll(f[j], LANES - 1, 1) - f[j]) * tile.open_face)
        total = flux_deeper[j] - flux_nearer[j]
        total = total + (row[j] - row_prev[j])
        total = total + (col - pltpu.roll(col, 1, 1))
        new.append(f[j] + total)
    put(dst, to, new)
    return flux_deeper


def first_flux(src, p):
    here, deeper = take(src, p), take(src, p + 1)
    return [flux(deeper[j] - here[j]) for j in range(TILES)]


ALONG_ROWS = lax.GatherDimensionNumbers(
    offset_dims=(),
    collapsed_slice_dims=(0,),
    start_index_map=(0,),
    operand_batching_dims=(1,),
    start_indices_batching_dims=(1,),
)


def along_rows(x, k):
    return lax.gather(
        x, k[..., None], ALONG_ROWS, (1, 1), mode=lax.GatherScatterMode.PROMISE_IN_BOUNDS
    )


def tables(transfer):
    even, odd = [], []
    for c in range(4):
        for half, first in ((even, 0), (odd, 1)):
            knots = transfer[pl.ds(first, 8, stride=2), :]
            half.append(jnp.broadcast_to(knots[:, c : c + 1], (8, LANES)))
    return even, odd


def shade(src, p, j, carry, lookup, tile):
    red, green, blue, remaining = carry
    even, odd = lookup
    f = src[p, rows_at(j), :]
    depth = src[p + 1, rows_at(j), :] - src[p - 1, rows_at(j), :]
    row = src[p, rows_at(j, 1), :] - src[p, rows_at(j, -1), :]
    right = jnp.where(tile.at_last, f, pltpu.roll(f, LANES - 1, 1))
    left = jnp.where(tile.at_first, f, pltpu.roll(f, 1, 1))
    col = right - left
    square = depth * depth + row * row + col * col + SCALE * SCALE
    gain = 1.0 - AMBIENT
    along = jnp.abs(0.64 * gain * depth + 0.6 * gain * row + 0.48 * gain * col)
    shading = AMBIENT + along * lax.rsqrt(square)
    position = f * ((KNOTS - 1) / UPPER_DENSITY / SCALE)
    k = position.astype(jnp.int32)
    frac = position - k.astype(jnp.float32)
    near_odd = jnp.bitwise_and(lax.shift_right_logical(k, 1), 7)
    near_even = jnp.bitwise_and(lax.shift_right_logical(k + 1, 1), 7)
    weight_odd = jnp.where(jnp.bitwise_and(k, 1) == 0, frac, 1.0 - frac)
    mixed = []
    for c in range(4):
        low = along_rows(even[c], near_even)
        mixed.append(low + weight_odd * (along_rows(odd[c], near_odd) - low))
    kept = jnp.exp(mixed[3] * (-OPTICAL_DEPTH / (DEEP * BLOCKS)))
    weight = remaining * (1.0 - kept) * shading
    return (
        red + weight * mixed[0],
        green + weight * mixed[1],
        blue + weight * mixed[2],
        remaining * kept,
    )


def inner_kernel(mine, knots, out, fa, fb, fluxes, sums):
    tile = Tile()
    zero = jnp.zeros((8, LANES), jnp.float32)
    is_first = tile.block == 0

    def fill(i, carry):
        for u in range(8):
            for p in range(PLANES):
                k = 8 * i + u
                put(fa, FRONT + PLANES * k + p, tile.unpack(mine, CHUNK * k + RAW_ROWS * p))
        return carry

    lax.fori_loop(0, GROUP // 8, fill, 0)
    for i in range(HALO):
        out[TAIL + i] = fa[FRONT + DEEP - HALO + i]

    @pl.when(is_first)
    def _():
        for i in range(HALO):
            fa[FRONT - 1 - i] = fa[FRONT + i]

    src, dst = fa, fb
    for sweep in range(PASSES):
        lo, hi = FRONT + sweep + 1, FRONT + DEEP - 1 - sweep

        @pl.when(is_first)
        def _(src=src, dst=dst, lo=lo):
            carry = first_flux(src, lo - 5)
            for u in range(4):
                p = lo - 4 + u
                carry = diffuse(src, p, dst, p, fluxes, u, carry, tile)

        count = hi - lo
        unroll = 6 if count % 6 == 0 else UNROLL

        def step(i, carry, src=src, dst=dst, lo=lo, unroll=unroll):
            for u in range(unroll):
                p = lo + unroll * i + u
                carry = diffuse(src, p, dst, p, fluxes, u, carry, tile)
            return carry

        whole = count // unroll
        carry = lax.fori_loop(0, whole, step, first_flux(src, lo - 1))
        for u in range(count - unroll * whole):
            p = lo + unroll * whole + u
            carry = diffuse(src, p, dst, p, fluxes, u, carry, tile)
        for i in range(2):
            out[2 * sweep + i] = dst[hi - 2 + i]
        src, dst = dst, src

    lookup = tables(knots)
    start = (zero, zero, zero, zero + 1.0)

    def rows(j):
        return pl.ds(pl.multiple_of(8 * j, 8), 8)

    @pl.when(is_first)
    def _():
        def shaded(j, unused):
            carry = start
            for u in range(HALO):
                carry = shade(src, FRONT + u, j, carry, lookup, tile)
            for c in range(4):
                sums[c, rows(j), :] = carry[c]
            return unused

        lax.fori_loop(0, TILES, shaded, 0)

    @pl.when(jnp.logical_not(is_first))
    def _():
        for c in range(4):
            for j in range(TILES):
                sums[c, 8 * j : 8 * j + 8, :] = start[c]

    def shaded(j, unused):
        def planes(i, carry):
            for u in range(SHADED):
                p = FRONT + HALO + SHADED * i + u
                carry = shade(src, p, j, carry, lookup, tile)
            return carry

        carry = tuple(sums[c, rows(j), :] for c in range(4))
        carry = lax.fori_loop(0, (DEEP - 2 * HALO) // SHADED, planes, carry)
        for c in range(4):
            out[2 * PASSES + c, rows(j), :] = carry[c]
        return unused

    lax.fori_loop(0, TILES, shaded, 0)


def outer_kernel(after, inner, knots, out, fa, fb, fluxes):
    tile = Tile()
    lookup = tables(knots)
    is_last = tile.block == BLOCKS - 1

    def tail(to, i):
        fa[to] = inner[TAIL + i]

    for i in range(2):
        tail(i, HALO - 2 + i)

    @pl.when(jnp.logical_not(is_last))
    def _():
        for i in range(2 * HALO):
            k, p = divmod(i, PLANES)
            put(fa, 2 + i, tile.unpack(after, CHUNK * k + RAW_ROWS * p))

    @pl.when(is_last)
    def _():
        for i in range(2 * HALO):
            tail(2 + i, max(HALO - 1 - i, 0))

    src, dst = fa, fb
    for sweep in range(PASSES):
        carry = first_flux(src, 0)
        for i in range(2 * HALO):
            carry = diffuse(src, i + 1, dst, i + 2, fluxes, i, carry, tile)
        for i in range(2):
            dst[i] = inner[2 * sweep + i]
        src, dst = dst, src

    lane = lane_index()
    for j in range(TILES):
        sums = tuple(inner[2 * PASSES + c, 8 * j : 8 * j + 8, :] for c in range(4))
        for i in range(2 * HALO):
            if i == HALO:
                own = sums
            sums = shade(src, i + 1, j, sums, lookup, tile)
        sums = [jnp.where(is_last, own[c], sums[c]) for c in range(4)]
        for k in range(SEGS):
            value = None
            for c in range(4):
                by = TILE * c - WIDE * k - HALO - tile.start + LANES * 2
                moved = pltpu.roll(sums[c], lax.rem(by, LANES), 1)
                value = moved if value is None else jnp.where(lane >= TILE * c, moved, value)
            first = SEG_ROWS * k + 8 * j - HALO
            lo, hi = max(first, 0), min(first + min(8, SEG_ROWS - 8 * j), BAND)
            if lo < hi:
                out[lo:hi, :] = value[lo - first : hi - first]


def gather_kernel(parts, out):
    lane = lane_index(GROUP)
    total = jnp.zeros((GROUP, LANES), jnp.float32)
    remaining = jnp.ones((GROUP, LANES), jnp.float32)
    for b in range(BLOCKS):
        v = parts[GROUP * b : GROUP * (b + 1)]
        kept = v
        for c in range(3):
            kept = jnp.where(
                jnp.logical_and(lane >= TILE * c, lane < TILE * (c + 1)),
                pltpu.roll(v, TILE * (c + 1), 1),
                kept,
            )
        total = total + remaining * v
        remaining = remaining * kept
    total = jnp.where(lane >= 3 * TILE, 1.0 - remaining, total)
    turned = [total] + [pltpu.roll(total, TILE * s, 1) for s in range(1, 4)]
    for c in range(4):
        for t in range(GROUP):
            m = t % 4
            out[c, :, TILE * t : TILE * (t + 1)] = turned[(m - c) % 4][
                t : t + 1, TILE * m : TILE * (m + 1)
            ]


def call(kernel, shape, scratch, *operands, **options):
    spec = pl.BlockSpec(memory_space=VMEM)
    operands = [pltpu.with_memory_space_constraint(x, VMEM) for x in operands]
    return pl.pallas_call(
        kernel,
        out_shape=VMEM(shape, jnp.float32),
        in_specs=[spec] * len(operands),
        out_specs=spec,
        scratch_shapes=[VMEM(s, jnp.float32) for s in scratch],
        **options,
    )(*operands)


def shifted(value, axis, by):
    size = lax.axis_size(axis)
    pairs = [(i, i + by) for i in range(size) if 0 <= i + by < size]
    return lax.ppermute(value, axis, pairs)


def rendered(density, transfer_table):
    bands = lax.axis_size("rows")
    edge = VMEM((PLANES, HALO, COLS), jnp.float32)
    one, two = pl.pallas_call(
        slice_kernel,
        out_shape=[edge, edge],
        in_specs=[pl.BlockSpec(memory_space=pl.ANY)],
        out_specs=[pl.BlockSpec(memory_space=VMEM)] * 2,
        scratch_shapes=[
            VMEM((2, PLANES, 8, COLS), jnp.float32),
            pltpu.SemaphoreType.DMA((2,)),
        ],
        name="slice_kernel",
    )(density)
    pairs = [(i, i + 1) for i in range(0, bands, 2)]
    from_one = lax.ppermute(one, "rows", pairs + [(b, a) for a, b in pairs])
    pairs = [(i, i + 1) for i in range(1, bands - 1, 2)]
    from_two = lax.ppermute(two, "rows", pairs + [(b, a) for a, b in pairs])
    chunks = (GROUP * CHUNK, LANES)
    cut = pl.pallas_call(
        pack_kernel,
        out_shape=VMEM(chunks, jnp.float32),
        in_specs=[pl.BlockSpec(memory_space=pl.ANY)],
        out_specs=pl.BlockSpec(memory_space=VMEM),
        scratch_shapes=[
            VMEM((PLANES, BAND + 8, COLS), jnp.float32),
            pltpu.SemaphoreType.DMA((PLANES, PARTS)),
        ],
        name="pack_kernel",
    )(density)
    sent = call(
        halo_kernel,
        chunks,
        [(PLANES, 8, COLS)],
        cut,
        two,
        from_one,
        from_two,
        input_output_aliases={0: 0},
    )
    groups = [[GROUP * b + i for i in range(GROUP)] for b in range(BLOCKS)]
    sent = sent.reshape(GROUP, CHUNK, 1, LANES)
    mine = lax.all_to_all(sent, "depth", 0, 0, axis_index_groups=groups, tiled=True)
    mine = mine.reshape(GROUP * CHUNK, LANES)
    after = shifted(mine[: 2 * HALO // PLANES * CHUNK], "depth", -GROUP)
    knots = transfer_table.T
    field = (FRONT + DEEP, TALL, LANES)
    inner = call(
        inner_kernel,
        (TAIL + HALO, TALL, LANES),
        [field, field, (UNROLL, TALL, LANES), (4, LINES, LANES)],
        mine,
        knots,
    )
    few = (2 * HALO + 2, TALL, LANES)
    partial = call(
        outer_kernel,
        (BAND, LANES),
        [few, few, (2 * HALO, TALL, LANES)],
        after,
        inner,
        knots,
    )
    parts = lax.all_to_all(partial, "depth", 0, 0, tiled=True)
    spec = pl.BlockSpec(memory_space=VMEM)
    return pl.pallas_call(
        gather_kernel,
        out_shape=jax.ShapeDtypeStruct((4, 1, COLS), jnp.float32),
        in_specs=[spec],
        out_specs=spec,
        name="gather_kernel",
    )(pltpu.with_memory_space_constraint(parts, VMEM))


def solution(mesh):
    placed = (P("depth", "rows", None), P())
    return jax.shard_map(
        rendered,
        mesh=mesh,
        in_specs=placed,
        out_specs=P(None, ("rows", "depth"), None),
        check_vma=False,
    )
```

```python
import jax
import jax.numpy as jnp
from jax import lax
from jax.experimental import pallas as pl
from jax.experimental.pallas import tpu as pltpu
from jax.sharding import PartitionSpec as P


PASSES = 3
KNOTS = 16
TIME_STEP = 0.15
OPTICAL_DEPTH = 3.0
UPPER_DENSITY = 6.0
AMBIENT = 0.35
SCALE = TIME_STEP**-0.5

GROUP = 16
BLOCKS = 8
HALO = 4
BAND = 128
COLS = 512
TILE = COLS // GROUP
WIDE = TILE + 2 * HALO
SEGS = 3
SEG_ROWS = 46
RAW_ROWS = 43
TURN = WIDE - TILE
TILES = 6
LINES = 8 * TILES
PLANES = 2
DEEP = GROUP * PLANES
LANES = 128
TOP = 8
TALL = 64
FRONT = HALO
CHUNK = 2 * RAW_ROWS
SPARE = SEGS * WIDE
TAIL = 2 * PASSES + 4
PARTS = 4
UNROLL = 7
SHADED = 8
VMEM = pltpu.VMEM


def lane_index(rows=8):
    return lax.broadcasted_iota(jnp.int32, (rows, LANES), 1)


def window_masks():
    lane = lane_index()
    segment, left, right, spare = [], [], [], []
    for m in range(4):
        local = (lane - (TILE * m - HALO)) % LANES
        segment.append([(local >= WIDE * k) & (local < WIDE * (k + 1)) for k in range(SEGS)])
        column = local % WIDE
        left.append(column < HALO)
        right.append(column >= WIDE - HALO)
        spare.append(local >= SPARE)
    return segment, left, right, spare


def windows(tiles, joined, left, right):
    for t in range(GROUP):
        q, m = divmod(t, 4)
        value = joined(tiles, q, m)
        if m == 0 and q > 0:
            value = jnp.where(left[m], joined(tiles, q - 1, m), value)
        if m == 3 and q < 3:
            value = jnp.where(right[m], joined(tiles, q + 1, m), value)
        yield t, m, value


def slice_kernel(density, one, two, ends, sems):
    even = lax.axis_index("rows") % 2 == 0
    copies = []
    for i, row in enumerate((0, BAND - 8)):
        source = density.at[:, pl.ds(row, 8), :]
        copies.append(pltpu.make_async_copy(source, ends.at[i], sems.at[i]))
    for copy in copies:
        copy.start()
    for copy in copies:
        copy.wait()
    for p in range(PLANES):
        first = ends[0, p, 0:HALO, :]
        last = ends[1, p, 8 - HALO : 8, :]
        one[p] = jnp.where(even, last, first)
        two[p] = jnp.where(even, first, last)


def pack_kernel(density, out, own, sems):
    part = BAND // PARTS
    copies = []
    for p in range(PLANES):
        for i in range(PARTS):
            at = pl.ds(part * i, part)
            copies.append(
                pltpu.make_async_copy(density.at[p, at, :], own.at[p, at, :], sems.at[p, i])
            )
    for copy in copies:
        copy.start()
    for p in range(PLANES):
        own[p, BAND:, :] = jnp.zeros((8, COLS), jnp.float32)
    segment, left, right, _ = window_masks()

    def joined(rolled, q, m):
        rest = jnp.where(segment[m][1], rolled[1][q], rolled[2][q])
        return jnp.where(segment[m][0], rolled[0][q], rest)

    for p in range(PLANES):
        for copy in copies[PARTS * p : PARTS * (p + 1)]:
            copy.wait()
        for j in range(TILES):
            count = min(8, RAW_ROWS - 8 * j)
            rolled = []
            for k in range(SEGS):
                start = RAW_ROWS * k + 8 * j
                rows = own[p, start : start + 8, :]
                tiles = [rows[:, LANES * q : LANES * (q + 1)] for q in range(4)]
                rolled.append([pltpu.roll(x, WIDE * k, 1) if k else x for x in tiles])
            for t, m, value in windows(rolled, joined, left, right):
                start = CHUNK * t + RAW_ROWS * p + 8 * j
                out[start : start + count, :] = (value * SCALE)[:count]


def halo_kernel(sent, two, from_one, from_two, out, edge):
    band = lax.axis_index("rows")
    bands = lax.axis_size("rows")
    even = band % 2 == 0

    def above(source):
        for p in range(PLANES):
            edge[p, 0:HALO, :] = source[p]

    def below(source):
        for p in range(PLANES):
            edge[p, HALO : 2 * HALO, :] = source[p]

    @pl.when(even)
    def _():
        below(from_one)

    @pl.when(jnp.logical_not(even))
    def _():
        above(from_one)

    @pl.when(even & (band > 0))
    def _():
        above(from_two)

    @pl.when(jnp.logical_not(even) & (band < bands - 1))
    def _():
        below(from_two)

    @pl.when(band == 0)
    def _():
        for p in range(PLANES):
            for i in range(HALO):
                edge[p, HALO - 1 - i : HALO - i, :] = two[p, i : i + 1, :]

    @pl.when(band == bands - 1)
    def _():
        for p in range(PLANES):
            for i in range(HALO):
                edge[p, HALO + i : HALO + i + 1, :] = two[p, HALO - 1 - i : HALO - i, :]

    _, left, right, spare = window_masks()

    def joined(tiles, q, m):
        return tiles[q]

    for p in range(PLANES):
        tiles = [edge[p, :, LANES * q : LANES * (q + 1)] for q in range(4)]
        for t, m, value in windows(tiles, joined, left, right):
            for g in range(WIDE // 8):
                start = CHUNK * t + RAW_ROWS * p + 8 * g
                moved = pltpu.roll(value, SPARE - 8 * g, 1)
                here = sent[start : start + 8, :]
                out[start : start + 8, :] = jnp.where(spare[m], moved * SCALE, here)


def flux(change):
    return change / (SCALE * SCALE + change * change)


def rows_at(j, by=0):
    if isinstance(j, int):
        return slice(TOP + 8 * j + by, TOP + 8 * j + by + 8)
    return pl.ds(pl.multiple_of(8 * j, 8) + TOP + by, 8)


def put(ref, p, tiles):
    for j in range(TILES):
        ref[p, rows_at(j), :] = tiles[j]
    last = SEG_ROWS - 8 * (TILES - 1) - 1
    ref[p, TOP - 1 : TOP, :] = pltpu.roll(tiles[-1], WIDE, 1)[last : last + 1]
    ref[p, TOP + SEG_ROWS : TOP + SEG_ROWS + 1, :] = pltpu.roll(tiles[0], LANES - WIDE, 1)[0:1]


def take(ref, p, by=0):
    return [ref[p, rows_at(j, by), :] for j in range(TILES)]


class Tile:
    def __init__(self):
        self.block = lax.axis_index("depth") // GROUP
        tile = lax.axis_index("depth") % GROUP
        self.start = TILE * (tile % 4) - HALO
        local = (lane_index() - self.start + LANES) % LANES
        column = local % WIDE
        first, last = tile == 0, tile == GROUP - 1
        self.at_first = jnp.logical_and(column == HALO, first)
        self.at_last = jnp.logical_and(column == HALO + TILE - 1, last)
        self.open_face = jnp.where(
            jnp.logical_or(self.at_last, jnp.logical_and(column == HALO - 1, first)), 0.0, 1.0
        )
        row = lax.broadcasted_iota(jnp.int32, (8, LANES), 0)
        self.local = local
        self.segment = [(local >= WIDE * k) & (local < WIDE * (k + 1)) for k in range(SEGS)]
        self.top = self.segment[0] & (row < HALO)
        self.bottom = self.segment[2] & (row < HALO)
        self.head = self.segment[1] & (row == 0)
        self.foot = self.segment[1] & (row >= 4) & (row < 6)

    def unpack(self, raw, start):
        def load(by):
            return raw[pl.ds(start + by, 8), :]

        zeroth, end = load(0), load(RAW_ROWS - 8)
        tiles = []
        for j in range(TILES):
            if j == 0:
                parts = (pltpu.roll(zeroth, 4, 0), pltpu.roll(zeroth, 1, 0), load(2))
            elif j < TILES - 1:
                parts = (load(8 * j - 4), load(8 * j - 1), load(8 * j + 2))
            else:
                parts = (pltpu.roll(end, 7, 0), pltpu.roll(end, 4, 0), end)
            rest = jnp.where(self.segment[1], parts[1], parts[2])
            tiles.append(jnp.where(self.segment[0], parts[0], rest))
        halo = None
        for g in range(WIDE // 8):
            rows = load(8 * g) if g else zeroth
            moved = pltpu.roll(rows, LANES - SPARE + 8 * g, 1)
            halo = moved if halo is None else jnp.where(self.local >= 8 * g, moved, halo)
        head = pltpu.roll(pltpu.roll(end, WIDE, 1), 1, 0)
        foot = pltpu.roll(pltpu.roll(zeroth, LANES - WIDE, 1), 4, 0)
        below = pltpu.roll(pltpu.roll(halo, 2 * WIDE, 1), 4, 0)
        tiles[0] = jnp.where(self.top, halo, jnp.where(self.head, head, tiles[0]))
        tiles[-1] = jnp.where(self.bottom, below, jnp.where(self.foot, foot, tiles[-1]))
        return tiles


def diffuse(src, p, dst, to, fluxes, slot, flux_nearer, tile):
    f = take(src, p)
    below = take(src, p, 1)
    deeper = take(src, p + 1)
    flux_deeper = [flux(deeper[j] - f[j]) for j in range(TILES)]
    row = [flux(below[j] - f[j]) for j in range(TILES)]
    for j in range(TILES):
        fluxes[slot, rows_at(j), :] = row[j]
    last = SEG_ROWS - 8 * (TILES - 1) - 1
    fluxes[slot, TOP - 1 : TOP, :] = pltpu.roll(row[-1], WIDE, 1)[last : last + 1]
    row_prev = take(fluxes, slot, -1)
    new = []
    for j in range(TILES):
        col = flux((pltpu.roll(f[j], LANES - 1, 1) - f[j]) * tile.open_face)
        total = flux_deeper[j] - flux_nearer[j]
        total = total + (row[j] - row_prev[j])
        total = total + (col - pltpu.roll(col, 1, 1))
        new.append(f[j] + total)
    put(dst, to, new)
    return flux_deeper


def first_flux(src, p):
    here, deeper = take(src, p), take(src, p + 1)
    return [flux(deeper[j] - here[j]) for j in range(TILES)]


ALONG_ROWS = lax.GatherDimensionNumbers(
    offset_dims=(),
    collapsed_slice_dims=(0,),
    start_index_map=(0,),
    operand_batching_dims=(1,),
    start_indices_batching_dims=(1,),
)


def along_rows(x, k):
    return lax.gather(
        x, k[..., None], ALONG_ROWS, (1, 1), mode=lax.GatherScatterMode.PROMISE_IN_BOUNDS
    )


def tables(transfer):
    even, odd = [], []
    for c in range(4):
        for half, first in ((even, 0), (odd, 1)):
            knots = transfer[pl.ds(first, 8, stride=2), :]
            half.append(jnp.broadcast_to(knots[:, c : c + 1], (8, LANES)))
    return even, odd


def shade(src, p, j, carry, lookup, tile):
    red, green, blue, remaining = carry
    even, odd = lookup
    f = src[p, rows_at(j), :]
    depth = src[p + 1, rows_at(j), :] - src[p - 1, rows_at(j), :]
    row = src[p, rows_at(j, 1), :] - src[p, rows_at(j, -1), :]
    right = jnp.where(tile.at_last, f, pltpu.roll(f, LANES - 1, 1))
    left = jnp.where(tile.at_first, f, pltpu.roll(f, 1, 1))
    col = right - left
    square = depth * depth + row * row + col * col + SCALE * SCALE
    gain = 1.0 - AMBIENT
    along = jnp.abs(0.64 * gain * depth + 0.6 * gain * row + 0.48 * gain * col)
    shading = AMBIENT + along * lax.rsqrt(square)
    position = f * ((KNOTS - 1) / UPPER_DENSITY / SCALE)
    k = position.astype(jnp.int32)
    frac = position - k.astype(jnp.float32)
    near_odd = jnp.bitwise_and(lax.shift_right_logical(k, 1), 7)
    near_even = jnp.bitwise_and(lax.shift_right_logical(k + 1, 1), 7)
    weight_odd = jnp.where(jnp.bitwise_and(k, 1) == 0, frac, 1.0 - frac)
    mixed = []
    for c in range(4):
        low = along_rows(even[c], near_even)
        mixed.append(low + weight_odd * (along_rows(odd[c], near_odd) - low))
    kept = jnp.exp(mixed[3] * (-OPTICAL_DEPTH / (DEEP * BLOCKS)))
    weight = remaining * (1.0 - kept) * shading
    return (
        red + weight * mixed[0],
        green + weight * mixed[1],
        blue + weight * mixed[2],
        remaining * kept,
    )


def inner_kernel(mine, knots, out, fa, fb, fluxes, sums):
    tile = Tile()
    zero = jnp.zeros((8, LANES), jnp.float32)
    is_first = tile.block == 0

    def fill(i, carry):
        for u in range(8):
            for p in range(PLANES):
                k = 8 * i + u
                put(fa, FRONT + PLANES * k + p, tile.unpack(mine, CHUNK * k + RAW_ROWS * p))
        return carry

    lax.fori_loop(0, GROUP // 8, fill, 0)
    for i in range(HALO):
        out[TAIL + i] = fa[FRONT + DEEP - HALO + i]

    @pl.when(is_first)
    def _():
        for i in range(HALO):
            fa[FRONT - 1 - i] = fa[FRONT + i]

    src, dst = fa, fb
    for sweep in range(PASSES):
        lo, hi = FRONT + sweep + 1, FRONT + DEEP - 1 - sweep

        @pl.when(is_first)
        def _(src=src, dst=dst, lo=lo):
            carry = first_flux(src, lo - 5)
            for u in range(4):
                p = lo - 4 + u
                carry = diffuse(src, p, dst, p, fluxes, u, carry, tile)

        count = hi - lo
        unroll = 6 if count % 6 == 0 else UNROLL

        def step(i, carry, src=src, dst=dst, lo=lo, unroll=unroll):
            for u in range(unroll):
                p = lo + unroll * i + u
                carry = diffuse(src, p, dst, p, fluxes, u, carry, tile)
            return carry

        whole = count // unroll
        carry = lax.fori_loop(0, whole, step, first_flux(src, lo - 1))
        for u in range(count - unroll * whole):
            p = lo + unroll * whole + u
            carry = diffuse(src, p, dst, p, fluxes, u, carry, tile)
        for i in range(2):
            out[2 * sweep + i] = dst[hi - 2 + i]
        src, dst = dst, src

    lookup = tables(knots)
    start = (zero, zero, zero, zero + 1.0)

    def rows(j):
        return pl.ds(pl.multiple_of(8 * j, 8), 8)

    @pl.when(is_first)
    def _():
        def shaded(j, unused):
            carry = start
            for u in range(HALO):
                carry = shade(src, FRONT + u, j, carry, lookup, tile)
            for c in range(4):
                sums[c, rows(j), :] = carry[c]
            return unused

        lax.fori_loop(0, TILES, shaded, 0)

    @pl.when(jnp.logical_not(is_first))
    def _():
        for c in range(4):
            for j in range(TILES):
                sums[c, 8 * j : 8 * j + 8, :] = start[c]

    def shaded(j, unused):
        def planes(i, carry):
            for u in range(SHADED):
                p = FRONT + HALO + SHADED * i + u
                carry = shade(src, p, j, carry, lookup, tile)
            return carry

        carry = tuple(sums[c, rows(j), :] for c in range(4))
        carry = lax.fori_loop(0, (DEEP - 2 * HALO) // SHADED, planes, carry)
        for c in range(4):
            out[2 * PASSES + c, rows(j), :] = carry[c]
        return unused

    lax.fori_loop(0, TILES, shaded, 0)


def outer_kernel(after, inner, knots, out, fa, fb, fluxes):
    tile = Tile()
    lookup = tables(knots)
    is_last = tile.block == BLOCKS - 1

    def tail(to, i):
        fa[to] = inner[TAIL + i]

    for i in range(2):
        tail(i, HALO - 2 + i)

    @pl.when(jnp.logical_not(is_last))
    def _():
        for i in range(2 * HALO):
            k, p = divmod(i, PLANES)
            put(fa, 2 + i, tile.unpack(after, CHUNK * k + RAW_ROWS * p))

    @pl.when(is_last)
    def _():
        for i in range(2 * HALO):
            tail(2 + i, max(HALO - 1 - i, 0))

    src, dst = fa, fb
    for sweep in range(PASSES):
        carry = first_flux(src, 0)
        for i in range(2 * HALO):
            carry = diffuse(src, i + 1, dst, i + 2, fluxes, i, carry, tile)
        for i in range(2):
            dst[i] = inner[2 * sweep + i]
        src, dst = dst, src

    lane = lane_index()
    for j in range(TILES):
        sums = tuple(inner[2 * PASSES + c, 8 * j : 8 * j + 8, :] for c in range(4))
        for i in range(2 * HALO):
            if i == HALO:
                own = sums
            sums = shade(src, i + 1, j, sums, lookup, tile)
        sums = [jnp.where(is_last, own[c], sums[c]) for c in range(4)]
        turned = []
        for m in range(4):
            rest = jnp.where(tile.segment[1], sums[(m + 1) % 4], sums[(m + 2) % 4])
            picked = jnp.where(tile.segment[0], sums[m], rest)
            by = TILE * m - HALO - tile.start + LANES * 2
            turned.append(pltpu.roll(picked, lax.rem(by, LANES), 1))
        for k in range(SEGS):
            place = (lane - TURN * k + LANES) % LANES
            value = turned[-k % 4]
            for c in range(1, 4):
                value = jnp.where(place >= TILE * c, turned[(c - k) % 4], value)
            first = SEG_ROWS * k + 8 * j - HALO
            lo, hi = max(first, 0), min(first + min(8, SEG_ROWS - 8 * j), BAND)
            if lo < hi:
                out[lo:hi, :] = value[lo - first : hi - first]


def gather_kernel(parts, out):
    lane = lane_index(GROUP)
    segment = (lax.axis_index("depth") + HALO) // SEG_ROWS
    back = lax.rem(LANES - TURN * segment, LANES)
    total = jnp.zeros((GROUP, LANES), jnp.float32)
    remaining = jnp.ones((GROUP, LANES), jnp.float32)
    for b in range(BLOCKS):
        v = pltpu.roll(parts[GROUP * b : GROUP * (b + 1)], back, 1)
        kept = v
        for c in range(3):
            kept = jnp.where(
                jnp.logical_and(lane >= TILE * c, lane < TILE * (c + 1)),
                pltpu.roll(v, TILE * (c + 1), 1),
                kept,
            )
        total = total + remaining * v
        remaining = remaining * kept
    total = jnp.where(lane >= 3 * TILE, 1.0 - remaining, total)
    turned = [total] + [pltpu.roll(total, TILE * s, 1) for s in range(1, 4)]
    for c in range(4):
        for t in range(GROUP):
            m = t % 4
            out[c, :, TILE * t : TILE * (t + 1)] = turned[(m - c) % 4][
                t : t + 1, TILE * m : TILE * (m + 1)
            ]


def call(kernel, shape, scratch, *operands, **options):
    spec = pl.BlockSpec(memory_space=VMEM)
    operands = [pltpu.with_memory_space_constraint(x, VMEM) for x in operands]
    return pl.pallas_call(
        kernel,
        out_shape=VMEM(shape, jnp.float32),
        in_specs=[spec] * len(operands),
        out_specs=spec,
        scratch_shapes=[VMEM(s, jnp.float32) for s in scratch],
        **options,
    )(*operands)


def shifted(value, axis, by):
    size = lax.axis_size(axis)
    pairs = [(i, i + by) for i in range(size) if 0 <= i + by < size]
    return lax.ppermute(value, axis, pairs)


def rendered(density, transfer_table):
    bands = lax.axis_size("rows")
    edge = VMEM((PLANES, HALO, COLS), jnp.float32)
    one, two = pl.pallas_call(
        slice_kernel,
        out_shape=[edge, edge],
        in_specs=[pl.BlockSpec(memory_space=pl.ANY)],
        out_specs=[pl.BlockSpec(memory_space=VMEM)] * 2,
        scratch_shapes=[
            VMEM((2, PLANES, 8, COLS), jnp.float32),
            pltpu.SemaphoreType.DMA((2,)),
        ],
        name="slice_kernel",
    )(density)
    pairs = [(i, i + 1) for i in range(0, bands, 2)]
    from_one = lax.ppermute(one, "rows", pairs + [(b, a) for a, b in pairs])
    pairs = [(i, i + 1) for i in range(1, bands - 1, 2)]
    from_two = lax.ppermute(two, "rows", pairs + [(b, a) for a, b in pairs])
    chunks = (GROUP * CHUNK, LANES)
    cut = pl.pallas_call(
        pack_kernel,
        out_shape=VMEM(chunks, jnp.float32),
        in_specs=[pl.BlockSpec(memory_space=pl.ANY)],
        out_specs=pl.BlockSpec(memory_space=VMEM),
        scratch_shapes=[
            VMEM((PLANES, BAND + 8, COLS), jnp.float32),
            pltpu.SemaphoreType.DMA((PLANES, PARTS)),
        ],
        name="pack_kernel",
    )(density)
    sent = call(
        halo_kernel,
        chunks,
        [(PLANES, 8, COLS)],
        cut,
        two,
        from_one,
        from_two,
        input_output_aliases={0: 0},
    )
    groups = [[GROUP * b + i for i in range(GROUP)] for b in range(BLOCKS)]
    sent = sent.reshape(GROUP, CHUNK, 1, LANES)
    mine = lax.all_to_all(sent, "depth", 0, 0, axis_index_groups=groups, tiled=True)
    mine = mine.reshape(GROUP * CHUNK, LANES)
    after = shifted(mine[: 2 * HALO // PLANES * CHUNK], "depth", -GROUP)
    knots = transfer_table.T
    field = (FRONT + DEEP, TALL, LANES)
    inner = call(
        inner_kernel,
        (TAIL + HALO, TALL, LANES),
        [field, field, (UNROLL, TALL, LANES), (4, LINES, LANES)],
        mine,
        knots,
    )
    few = (2 * HALO + 2, TALL, LANES)
    partial = call(
        outer_kernel,
        (BAND, LANES),
        [few, few, (2 * HALO, TALL, LANES)],
        after,
        inner,
        knots,
    )
    parts = lax.all_to_all(partial, "depth", 0, 0, tiled=True)
    spec = pl.BlockSpec(memory_space=VMEM)
    return pl.pallas_call(
        gather_kernel,
        out_shape=jax.ShapeDtypeStruct((4, 1, COLS), jnp.float32),
        in_specs=[spec],
        out_specs=spec,
        name="gather_kernel",
    )(pltpu.with_memory_space_constraint(parts, VMEM))


def solution(mesh):
    placed = (P("depth", "rows", None), P())
    return jax.shard_map(
        rendered,
        mesh=mesh,
        in_specs=placed,
        out_specs=P(None, ("rows", "depth"), None),
        check_vma=False,
    )
```

```python
import jax
import jax.numpy as jnp
from jax import lax
from jax.experimental import pallas as pl
from jax.experimental.pallas import tpu as pltpu
from jax.sharding import PartitionSpec as P


PASSES = 3
KNOTS = 16
TIME_STEP = 0.15
OPTICAL_DEPTH = 3.0
UPPER_DENSITY = 6.0
AMBIENT = 0.35
SCALE = TIME_STEP**-0.5

GROUP = 16
BLOCKS = 8
HALO = 4
BAND = 128
COLS = 512
TILE = COLS // GROUP
WIDE = TILE + 2 * HALO
SEGS = 3
SEG_ROWS = 46
RAW_ROWS = 43
TURN = WIDE - TILE
TILES = 6
LINES = 8 * TILES
PLANES = 2
DEEP = GROUP * PLANES
LANES = 128
TOP = 8
TALL = 64
FRONT = HALO
CHUNK = 2 * RAW_ROWS
SPARE = SEGS * WIDE
TAIL = 2 * PASSES + 4
PARTS = 4
UNROLL = 7
SHADED = 8
VMEM = pltpu.VMEM


def lane_index(rows=8):
    return lax.broadcasted_iota(jnp.int32, (rows, LANES), 1)


def window_masks():
    lane = lane_index()
    segment, left, right, spare = [], [], [], []
    for m in range(4):
        local = (lane - (TILE * m - HALO)) % LANES
        segment.append([(local >= WIDE * k) & (local < WIDE * (k + 1)) for k in range(SEGS)])
        column = local % WIDE
        left.append(column < HALO)
        right.append(column >= WIDE - HALO)
        spare.append(local >= SPARE)
    return segment, left, right, spare


def windows(tiles, joined, left, right):
    for t in range(GROUP):
        q, m = divmod(t, 4)
        value = joined(tiles, q, m)
        if m == 0 and q > 0:
            value = jnp.where(left[m], joined(tiles, q - 1, m), value)
        if m == 3 and q < 3:
            value = jnp.where(right[m], joined(tiles, q + 1, m), value)
        yield t, m, value


def slice_kernel(density, one, two, ends, sems):
    even = lax.axis_index("rows") % 2 == 0
    copies = []
    for i, row in enumerate((0, BAND - 8)):
        source = density.at[:, pl.ds(row, 8), :]
        copies.append(pltpu.make_async_copy(source, ends.at[i], sems.at[i]))
    for copy in copies:
        copy.start()
    for copy in copies:
        copy.wait()
    for p in range(PLANES):
        first = ends[0, p, 0:HALO, :]
        last = ends[1, p, 8 - HALO : 8, :]
        one[p] = jnp.where(even, last, first)
        two[p] = jnp.where(even, first, last)


def pack_kernel(density, out, own, sems):
    part = BAND // PARTS
    copies = []
    for p in range(PLANES):
        for i in range(PARTS):
            at = pl.ds(part * i, part)
            copies.append(
                pltpu.make_async_copy(density.at[p, at, :], own.at[p, at, :], sems.at[p, i])
            )
    for copy in copies:
        copy.start()
    for p in range(PLANES):
        own[p, BAND:, :] = jnp.zeros((8, COLS), jnp.float32)
    segment, left, right, _ = window_masks()

    def joined(rolled, q, m):
        rest = jnp.where(segment[m][1], rolled[1][q], rolled[2][q])
        return jnp.where(segment[m][0], rolled[0][q], rest)

    for p in range(PLANES):
        for copy in copies[PARTS * p : PARTS * (p + 1)]:
            copy.wait()
        for j in range(TILES):
            count = min(8, RAW_ROWS - 8 * j)
            rolled = []
            for k in range(SEGS):
                start = RAW_ROWS * k + 8 * j
                rows = own[p, start : start + 8, :]
                tiles = [rows[:, LANES * q : LANES * (q + 1)] for q in range(4)]
                rolled.append([pltpu.roll(x, WIDE * k, 1) if k else x for x in tiles])
            for t, m, value in windows(rolled, joined, left, right):
                start = CHUNK * t + RAW_ROWS * p + 8 * j
                out[start : start + count, :] = (value * SCALE)[:count]


def halo_kernel(sent, two, from_one, from_two, out, edge):
    band = lax.axis_index("rows")
    bands = lax.axis_size("rows")
    even = band % 2 == 0

    def above(source):
        for p in range(PLANES):
            edge[p, 0:HALO, :] = source[p]

    def below(source):
        for p in range(PLANES):
            edge[p, HALO : 2 * HALO, :] = source[p]

    @pl.when(even)
    def _():
        below(from_one)

    @pl.when(jnp.logical_not(even))
    def _():
        above(from_one)

    @pl.when(even & (band > 0))
    def _():
        above(from_two)

    @pl.when(jnp.logical_not(even) & (band < bands - 1))
    def _():
        below(from_two)

    @pl.when(band == 0)
    def _():
        for p in range(PLANES):
            for i in range(HALO):
                edge[p, HALO - 1 - i : HALO - i, :] = two[p, i : i + 1, :]

    @pl.when(band == bands - 1)
    def _():
        for p in range(PLANES):
            for i in range(HALO):
                edge[p, HALO + i : HALO + i + 1, :] = two[p, HALO - 1 - i : HALO - i, :]

    _, left, right, spare = window_masks()

    def joined(tiles, q, m):
        return tiles[q]

    for p in range(PLANES):
        tiles = [edge[p, :, LANES * q : LANES * (q + 1)] for q in range(4)]
        for t, m, value in windows(tiles, joined, left, right):
            for g in range(WIDE // 8):
                start = CHUNK * t + RAW_ROWS * p + 8 * g
                moved = pltpu.roll(value, SPARE - 8 * g, 1)
                here = sent[start : start + 8, :]
                out[start : start + 8, :] = jnp.where(spare[m], moved * SCALE, here)


def flux(change):
    return change / (SCALE * SCALE + change * change)


def rows_at(j, by=0):
    if isinstance(j, int):
        return slice(TOP + 8 * j + by, TOP + 8 * j + by + 8)
    return pl.ds(pl.multiple_of(8 * j, 8) + TOP + by, 8)


def put(ref, p, tiles):
    for j in range(TILES):
        ref[p, rows_at(j), :] = tiles[j]
    last = SEG_ROWS - 8 * (TILES - 1) - 1
    ref[p, TOP - 1 : TOP, :] = pltpu.roll(tiles[-1], WIDE, 1)[last : last + 1]
    ref[p, TOP + SEG_ROWS : TOP + SEG_ROWS + 1, :] = pltpu.roll(tiles[0], LANES - WIDE, 1)[0:1]


def take(ref, p, by=0):
    return [ref[p, rows_at(j, by), :] for j in range(TILES)]


class Tile:
    def __init__(self):
        self.block = lax.axis_index("depth") // GROUP
        tile = lax.axis_index("depth") % GROUP
        self.start = TILE * (tile % 4) - HALO
        local = (lane_index() - self.start + LANES) % LANES
        column = local % WIDE
        first, last = tile == 0, tile == GROUP - 1
        self.at_first = jnp.logical_and(column == HALO, first)
        self.at_last = jnp.logical_and(column == HALO + TILE - 1, last)
        self.open_face = jnp.where(
            jnp.logical_or(self.at_last, jnp.logical_and(column == HALO - 1, first)), 0.0, 1.0
        )
        row = lax.broadcasted_iota(jnp.int32, (8, LANES), 0)
        self.local = local
        self.segment = [(local >= WIDE * k) & (local < WIDE * (k + 1)) for k in range(SEGS)]
        self.top = self.segment[0] & (row < HALO)
        self.bottom = self.segment[2] & (row < HALO)
        self.head = self.segment[1] & (row == 0)
        self.foot = self.segment[1] & (row >= 4) & (row < 6)

    def unpack(self, raw, start):
        def load(by):
            return raw[pl.ds(start + by, 8), :]

        zeroth, end = load(0), load(RAW_ROWS - 8)
        tiles = []
        for j in range(TILES):
            if j == 0:
                parts = (pltpu.roll(zeroth, 4, 0), pltpu.roll(zeroth, 1, 0), load(2))
            elif j < TILES - 1:
                parts = (load(8 * j - 4), load(8 * j - 1), load(8 * j + 2))
            else:
                parts = (pltpu.roll(end, 7, 0), pltpu.roll(end, 4, 0), end)
            rest = jnp.where(self.segment[1], parts[1], parts[2])
            tiles.append(jnp.where(self.segment[0], parts[0], rest))
        halo = None
        for g in range(WIDE // 8):
            rows = load(8 * g) if g else zeroth
            moved = pltpu.roll(rows, LANES - SPARE + 8 * g, 1)
            halo = moved if halo is None else jnp.where(self.local >= 8 * g, moved, halo)
        head = pltpu.roll(pltpu.roll(end, WIDE, 1), 1, 0)
        foot = pltpu.roll(pltpu.roll(zeroth, LANES - WIDE, 1), 4, 0)
        below = pltpu.roll(pltpu.roll(halo, 2 * WIDE, 1), 4, 0)
        tiles[0] = jnp.where(self.top, halo, jnp.where(self.head, head, tiles[0]))
        tiles[-1] = jnp.where(self.bottom, below, jnp.where(self.foot, foot, tiles[-1]))
        return tiles


def diffuse(src, p, dst, to, fluxes, slot, flux_nearer, tile):
    f = take(src, p)
    below = take(src, p, 1)
    deeper = take(src, p + 1)
    flux_deeper = [flux(deeper[j] - f[j]) for j in range(TILES)]
    row = [flux(below[j] - f[j]) for j in range(TILES)]
    for j in range(TILES):
        fluxes[slot, rows_at(j), :] = row[j]
    last = SEG_ROWS - 8 * (TILES - 1) - 1
    fluxes[slot, TOP - 1 : TOP, :] = pltpu.roll(row[-1], WIDE, 1)[last : last + 1]
    row_prev = take(fluxes, slot, -1)
    new = []
    for j in range(TILES):
        col = flux((pltpu.roll(f[j], LANES - 1, 1) - f[j]) * tile.open_face)
        total = flux_deeper[j] - flux_nearer[j]
        total = total + (row[j] - row_prev[j])
        total = total + (col - pltpu.roll(col, 1, 1))
        new.append(f[j] + total)
    put(dst, to, new)
    return flux_deeper


def first_flux(src, p):
    here, deeper = take(src, p), take(src, p + 1)
    return [flux(deeper[j] - here[j]) for j in range(TILES)]


ALONG_ROWS = lax.GatherDimensionNumbers(
    offset_dims=(),
    collapsed_slice_dims=(0,),
    start_index_map=(0,),
    operand_batching_dims=(1,),
    start_indices_batching_dims=(1,),
)


def along_rows(x, k):
    return lax.gather(
        x, k[..., None], ALONG_ROWS, (1, 1), mode=lax.GatherScatterMode.PROMISE_IN_BOUNDS
    )


def tables(transfer):
    even, odd = [], []
    for c in range(4):
        for half, first in ((even, 0), (odd, 1)):
            knots = transfer[pl.ds(first, 8, stride=2), :]
            half.append(jnp.broadcast_to(knots[:, c : c + 1], (8, LANES)))
    return even, odd


def shade(src, p, j, carry, lookup, tile):
    red, green, blue, remaining = carry
    even, odd = lookup
    f = src[p, rows_at(j), :]
    depth = src[p + 1, rows_at(j), :] - src[p - 1, rows_at(j), :]
    row = src[p, rows_at(j, 1), :] - src[p, rows_at(j, -1), :]
    right = jnp.where(tile.at_last, f, pltpu.roll(f, LANES - 1, 1))
    left = jnp.where(tile.at_first, f, pltpu.roll(f, 1, 1))
    col = right - left
    square = depth * depth + row * row + col * col + SCALE * SCALE
    gain = 1.0 - AMBIENT
    along = jnp.abs(0.64 * gain * depth + 0.6 * gain * row + 0.48 * gain * col)
    shading = AMBIENT + along * lax.rsqrt(square)
    position = f * ((KNOTS - 1) / UPPER_DENSITY / SCALE)
    k = position.astype(jnp.int32)
    frac = position - k.astype(jnp.float32)
    near_odd = jnp.bitwise_and(lax.shift_right_logical(k, 1), 7)
    near_even = jnp.bitwise_and(lax.shift_right_logical(k + 1, 1), 7)
    weight_odd = jnp.where(jnp.bitwise_and(k, 1) == 0, frac, 1.0 - frac)
    mixed = []
    for c in range(4):
        low = along_rows(even[c], near_even)
        mixed.append(low + weight_odd * (along_rows(odd[c], near_odd) - low))
    kept = jnp.exp(mixed[3] * (-OPTICAL_DEPTH / (DEEP * BLOCKS)))
    weight = remaining * (1.0 - kept) * shading
    return (
        red + weight * mixed[0],
        green + weight * mixed[1],
        blue + weight * mixed[2],
        remaining * kept,
    )


def inner_kernel(mine, knots, out, fa, fb, fluxes, sums):
    tile = Tile()
    zero = jnp.zeros((8, LANES), jnp.float32)
    is_first = tile.block == 0

    def fill(i, carry):
        for u in range(GROUP):
            for p in range(PLANES):
                k = GROUP * i + u
                put(fa, FRONT + PLANES * k + p, tile.unpack(mine, CHUNK * k + RAW_ROWS * p))
        return carry

    lax.fori_loop(0, 1, fill, 0)
    for i in range(HALO):
        out[TAIL + i] = fa[FRONT + DEEP - HALO + i]

    @pl.when(is_first)
    def _():
        for i in range(HALO):
            fa[FRONT - 1 - i] = fa[FRONT + i]

    src, dst = fa, fb
    for sweep in range(PASSES):
        lo, hi = FRONT + sweep + 1, FRONT + DEEP - 1 - sweep

        @pl.when(is_first)
        def _(src=src, dst=dst, lo=lo):
            carry = first_flux(src, lo - 5)
            for u in range(4):
                p = lo - 4 + u
                carry = diffuse(src, p, dst, p, fluxes, u, carry, tile)

        count = hi - lo
        unroll = 6 if count % 6 == 0 else UNROLL

        def step(i, carry, src=src, dst=dst, lo=lo, unroll=unroll):
            for u in range(unroll):
                p = lo + unroll * i + u
                carry = diffuse(src, p, dst, p, fluxes, u, carry, tile)
            return carry

        whole = count // unroll
        carry = lax.fori_loop(0, whole, step, first_flux(src, lo - 1))
        for u in range(count - unroll * whole):
            p = lo + unroll * whole + u
            carry = diffuse(src, p, dst, p, fluxes, u, carry, tile)
        for i in range(2):
            out[2 * sweep + i] = dst[hi - 2 + i]
        src, dst = dst, src

    lookup = tables(knots)
    start = (zero, zero, zero, zero + 1.0)

    def rows(j):
        return pl.ds(pl.multiple_of(8 * j, 8), 8)

    @pl.when(is_first)
    def _():
        def shaded(j, unused):
            carry = start
            for u in range(HALO):
                carry = shade(src, FRONT + u, j, carry, lookup, tile)
            for c in range(4):
                sums[c, rows(j), :] = carry[c]
            return unused

        lax.fori_loop(0, TILES, shaded, 0)

    @pl.when(jnp.logical_not(is_first))
    def _():
        for c in range(4):
            for j in range(TILES):
                sums[c, 8 * j : 8 * j + 8, :] = start[c]

    def shaded(j, unused):
        def planes(i, carry):
            for u in range(SHADED):
                p = FRONT + HALO + SHADED * i + u
                carry = shade(src, p, j, carry, lookup, tile)
            return carry

        carry = tuple(sums[c, rows(j), :] for c in range(4))
        carry = lax.fori_loop(0, (DEEP - 2 * HALO) // SHADED, planes, carry)
        for c in range(4):
            out[2 * PASSES + c, rows(j), :] = carry[c]
        return unused

    lax.fori_loop(0, TILES, shaded, 0)


def outer_kernel(after, inner, knots, out, fa, fb, fluxes):
    tile = Tile()
    lookup = tables(knots)
    is_last = tile.block == BLOCKS - 1

    def tail(to, i):
        fa[to] = inner[TAIL + i]

    for i in range(2):
        tail(i, HALO - 2 + i)

    @pl.when(jnp.logical_not(is_last))
    def _():
        for i in range(2 * HALO):
            k, p = divmod(i, PLANES)
            put(fa, 2 + i, tile.unpack(after, CHUNK * k + RAW_ROWS * p))

    @pl.when(is_last)
    def _():
        for i in range(2 * HALO):
            tail(2 + i, max(HALO - 1 - i, 0))

    src, dst = fa, fb
    for sweep in range(PASSES):
        carry = first_flux(src, 0)
        for i in range(2 * HALO):
            carry = diffuse(src, i + 1, dst, i + 2, fluxes, i, carry, tile)
        for i in range(2):
            dst[i] = inner[2 * sweep + i]
        src, dst = dst, src

    lane = lane_index()
    for j in range(TILES):
        sums = tuple(inner[2 * PASSES + c, 8 * j : 8 * j + 8, :] for c in range(4))
        for i in range(2 * HALO):
            if i == HALO:
                own = sums
            sums = shade(src, i + 1, j, sums, lookup, tile)
        sums = [jnp.where(is_last, own[c], sums[c]) for c in range(4)]
        turned = []
        for m in range(4):
            rest = jnp.where(tile.segment[1], sums[(m + 1) % 4], sums[(m + 2) % 4])
            picked = jnp.where(tile.segment[0], sums[m], rest)
            by = TILE * m - HALO - tile.start + LANES * 2
            turned.append(pltpu.roll(picked, lax.rem(by, LANES), 1))
        for k in range(SEGS):
            place = (lane - TURN * k + LANES) % LANES
            value = turned[-k % 4]
            for c in range(1, 4):
                value = jnp.where(place >= TILE * c, turned[(c - k) % 4], value)
            first = SEG_ROWS * k + 8 * j - HALO
            lo, hi = max(first, 0), min(first + min(8, SEG_ROWS - 8 * j), BAND)
            if lo < hi:
                out[lo:hi, :] = value[lo - first : hi - first]


def gather_kernel(parts, out):
    lane = lane_index(GROUP)
    segment = (lax.axis_index("depth") + HALO) // SEG_ROWS
    back = lax.rem(LANES - TURN * segment, LANES)
    total = jnp.zeros((GROUP, LANES), jnp.float32)
    remaining = jnp.ones((GROUP, LANES), jnp.float32)
    for b in range(BLOCKS):
        v = pltpu.roll(parts[GROUP * b : GROUP * (b + 1)], back, 1)
        kept = v
        for c in range(3):
            kept = jnp.where(
                jnp.logical_and(lane >= TILE * c, lane < TILE * (c + 1)),
                pltpu.roll(v, TILE * (c + 1), 1),
                kept,
            )
        total = total + remaining * v
        remaining = remaining * kept
    total = jnp.where(lane >= 3 * TILE, 1.0 - remaining, total)
    turned = [total] + [pltpu.roll(total, TILE * s, 1) for s in range(1, 4)]
    for c in range(4):
        for t in range(GROUP):
            m = t % 4
            out[c, :, TILE * t : TILE * (t + 1)] = turned[(m - c) % 4][
                t : t + 1, TILE * m : TILE * (m + 1)
            ]


def call(kernel, shape, scratch, *operands, **options):
    spec = pl.BlockSpec(memory_space=VMEM)
    operands = [pltpu.with_memory_space_constraint(x, VMEM) for x in operands]
    return pl.pallas_call(
        kernel,
        out_shape=VMEM(shape, jnp.float32),
        in_specs=[spec] * len(operands),
        out_specs=spec,
        scratch_shapes=[VMEM(s, jnp.float32) for s in scratch],
        **options,
    )(*operands)


def shifted(value, axis, by):
    size = lax.axis_size(axis)
    pairs = [(i, i + by) for i in range(size) if 0 <= i + by < size]
    return lax.ppermute(value, axis, pairs)


def rendered(density, transfer_table):
    bands = lax.axis_size("rows")
    edge = VMEM((PLANES, HALO, COLS), jnp.float32)
    one, two = pl.pallas_call(
        slice_kernel,
        out_shape=[edge, edge],
        in_specs=[pl.BlockSpec(memory_space=pl.ANY)],
        out_specs=[pl.BlockSpec(memory_space=VMEM)] * 2,
        scratch_shapes=[
            VMEM((2, PLANES, 8, COLS), jnp.float32),
            pltpu.SemaphoreType.DMA((2,)),
        ],
        name="slice_kernel",
    )(density)
    pairs = [(i, i + 1) for i in range(0, bands, 2)]
    from_one = lax.ppermute(one, "rows", pairs + [(b, a) for a, b in pairs])
    pairs = [(i, i + 1) for i in range(1, bands - 1, 2)]
    from_two = lax.ppermute(two, "rows", pairs + [(b, a) for a, b in pairs])
    chunks = (GROUP * CHUNK, LANES)
    cut = pl.pallas_call(
        pack_kernel,
        out_shape=VMEM(chunks, jnp.float32),
        in_specs=[pl.BlockSpec(memory_space=pl.ANY)],
        out_specs=pl.BlockSpec(memory_space=VMEM),
        scratch_shapes=[
            VMEM((PLANES, BAND + 8, COLS), jnp.float32),
            pltpu.SemaphoreType.DMA((PLANES, PARTS)),
        ],
        name="pack_kernel",
    )(density)
    sent = call(
        halo_kernel,
        chunks,
        [(PLANES, 8, COLS)],
        cut,
        two,
        from_one,
        from_two,
        input_output_aliases={0: 0},
    )
    groups = [[GROUP * b + i for i in range(GROUP)] for b in range(BLOCKS)]
    sent = sent.reshape(GROUP, CHUNK, 1, LANES)
    mine = lax.all_to_all(sent, "depth", 0, 0, axis_index_groups=groups, tiled=True)
    mine = mine.reshape(GROUP * CHUNK, LANES)
    after = shifted(mine[: 2 * HALO // PLANES * CHUNK], "depth", -GROUP)
    knots = transfer_table.T
    field = (FRONT + DEEP, TALL, LANES)
    inner = call(
        inner_kernel,
        (TAIL + HALO, TALL, LANES),
        [field, field, (UNROLL, TALL, LANES), (4, LINES, LANES)],
        mine,
        knots,
    )
    few = (2 * HALO + 2, TALL, LANES)
    partial = call(
        outer_kernel,
        (BAND, LANES),
        [few, few, (2 * HALO, TALL, LANES)],
        after,
        inner,
        knots,
    )
    parts = lax.all_to_all(partial, "depth", 0, 0, tiled=True)
    spec = pl.BlockSpec(memory_space=VMEM)
    return pl.pallas_call(
        gather_kernel,
        out_shape=jax.ShapeDtypeStruct((4, 1, COLS), jnp.float32),
        in_specs=[spec],
        out_specs=spec,
        name="gather_kernel",
    )(pltpu.with_memory_space_constraint(parts, VMEM))


def solution(mesh):
    placed = (P("depth", "rows", None), P())
    return jax.shard_map(
        rendered,
        mesh=mesh,
        in_specs=placed,
        out_specs=P(None, ("rows", "depth"), None),
        check_vma=False,
    )
```
